32 devices in a mesh: dp: 8 (over y, x, core), group: 4 (over z).
Axes of the slice: x: 2, y: 2, z: 4, core: 2. Of those that a mesh axis runs over, the one named last changes fastest.
Arguments:
- tokens: bfloat16 [32768, 1024], P(('dp', 'group')), may hold values from -6 to 6
- cotangent: bfloat16 [32768, 1024], P(('dp', 'group')), may hold values from -6 to 6
- order: int32 [4, 8], P('group'), may hold values from 0 to 7, each once within a row
- lengths: int32 [8, 4, 4], P(None, 'group'), may hold values from 1 to 960, 1024 in all within a row
- adapter_ids: int32 [8, 4, 4], P(None, 'group'), may hold values from 0 to 7
- norm_gain: float32 [1024], replicated, may hold values from 0.5 to 1.5
- ffn_gain: float32 [1024], replicated, may hold values from 0.5 to 1.5
- conv_weight: float32 [3, 1024], replicated, may hold values from -3.5 to 3.5
- in_weight: bfloat16 [1024, 3072], P(None, 'group'), may hold values from -0.1875 to 0.1875
- out_weight: bfloat16 [1024, 1024], P(None, 'group'), may hold values from -0.1875 to 0.1875
- gate_weight: bfloat16 [1024, 4608], P(None, 'group'), may hold values from -0.1875 to 0.1875
- up_weight: bfloat16 [1024, 4608], P(None, 'group'), may hold values from -0.1875 to 0.1875
- down_weight: bfloat16 [4608, 1024], P(None, 'group'), may hold values from -0.09375 to 0.09375
- input_first_factor: bfloat16 [1024, 128], replicated, may hold values from -0.1875 to 0.1875
- input_second_factor: bfloat16 [128, 3072], replicated, may hold values from -0.75 to 0.75
- output_first_factor: bfloat16 [1024, 128], replicated, may hold values from -0.1875 to 0.1875
- output_second_factor: bfloat16 [128, 1024], replicated, may hold values from -0.75 to 0.75
- gate_first_factor: bfloat16 [1024, 128], replicated, may hold values from -0.1875 to 0.1875
- gate_second_factor: bfloat16 [128, 4608], replicated, may hold values from -0.75 to 0.75
- up_first_factor: bfloat16 [1024, 128], replicated, may hold values from -0.1875 to 0.1875
- up_second_factor: bfloat16 [128, 4608], replicated, may hold values from -0.75 to 0.75
- down_first_factor: bfloat16 [4608, 128], replicated, may hold values from -0.09375 to 0.09375
- down_second_factor: bfloat16 [128, 1024], replicated, may hold values from -0.75 to 0.75
Outputs:
- block_output: bfloat16 [32768, 1024], P(('dp', 'group'))
- input_grad: bfloat16 [32768, 1024], P(('dp', 'group'))
- grad_in_a: float32 [1024, 128], P('group')
- grad_in_b: float32 [128, 3072], P(None, 'group')
- grad_out_a: float32 [1024, 128], P('group')
- grad_out_b: float32 [128, 1024], P(None, 'group')
- grad_gate_a: float32 [1024, 128], P('group')
- grad_gate_b: float32 [128, 4608], P(None, 'group')
- grad_up_a: float32 [1024, 128], P('group')
- grad_up_b: float32 [128, 4608], P(None, 'group')
- grad_down_a: float32 [4608, 128], P('group')
- grad_down_b: float32 [128, 1024], P(None, 'group')
The draws below stay inside these ranges and needn't reach their ends.
Inputs may be any that keep to these rules, and one draw needn't show every extreme that they name: Each row of order is a permutation. The 4 lengths of a pack sum to 1024; every draw has a sequence of exactly 960.
All inputs are finite; a program needn't handle non-finite values.
Results may differ from the reference program's by a relative error of at most 0.017.
Values may be sent and summed in bfloat16 or wider, within the bound.
No kernel may reach another device: no remote copies, remote signals or barrier semaphores. Data moves between devices by JAX's collectives and lax.ppermute only.
A program may use at most 320 MiB of HBM per device.

```python
import math
import jax
import jax.numpy as jnp
import numpy as np
from jax import lax

MODEL_DIM = 1024
FEEDFORWARD_DIM = 4608
ADAPTER_RANK = 16
ADAPTERS = 8
SEQS_DEV = 4
PACK_TOKENS = 1024
MAX_LEN = 960
ADAPTER_COLUMNS = 128
TOKENS = 32768
N_DP = 8
N_GROUP = 4


def place_ends(values, key, low, top_value):
    longest = values.shape.index(max(values.shape))
    spots = []
    for shift in (0, 1):
        where = [jax.random.randint(jax.random.fold_in(key, axis), (), 0, length) for axis, length in enumerate(values.shape)]
        where[longest] = (where[longest] + shift) % values.shape[longest]
        spots.append(tuple(where))
    return values.at[spots[0]].set(low).at[spots[1]].set(top_value)


def with_spikes(entries, rng, source, target, parts, factor):
    owner, partner = [(jnp.arange(entries.shape[dim]) // (entries.shape[dim] // parts)).reshape([-1 if axis == dim else 1 for axis in range(entries.ndim)]) for dim in (source, target)]
    chosen = jax.random.permutation(rng, parts)[partner]
    strong = (owner == chosen) | (owner == (partner + parts // 2) % parts)
    return jnp.where(strong, factor * entries, entries)


def level_of(stream_key, dims, shards, smallest, high):
    factor_of, own = 1.0, jax.random.fold_in(stream_key, 6)
    for dim, parts in shards:
        draws = jnp.exp(jax.random.uniform(jax.random.fold_in(own, dim), (parts,), jnp.float32, smallest / len(shards), high / len(shards)))
        factor_of = factor_of * jnp.repeat(draws, dims[dim] // parts).reshape([-1 if axis == dim else 1 for axis in range(len(dims))])
    return factor_of


def split_up(count, total, reach, skew):
    portions = [(1 << 20) // math.isqrt(rank ** skew) + 1 for rank in range(2, count + 1)]
    spare, given = total - reach - (count - 1), [1] * (count - 1)
    while spare > 0:
        movable = [i for i in range(count - 1) if given[i] < reach]
        whole, remaining = sum([portions[i] for i in movable]), spare
        for i in movable:
            addition = min(reach - given[i], max(1, remaining * portions[i] // whole), spare)
            given[i] = given[i] + addition
            spare = spare - addition
    return np.array([reach] + given)


def uneven_parts(rng, count, total, bound, slope):
    if count == 2:
        one = jax.random.randint(rng, (), max(1, total - bound), min(bound, total - 1) + 1)
        return jnp.stack([one, total - one])
    sizes = jnp.asarray(split_up(count, total, bound, slope), jnp.int32)
    couples = (count - 1) // 2
    source_of, taker = sizes[1:1 + 2 * couples:2], sizes[2:2 + 2 * couples:2]
    slack = jnp.minimum(source_of - 1, bound - taker)
    passed = jax.random.randint(jax.random.fold_in(rng, 1), (couples,), 0, 1 << 20) % (slack + 1)
    sizes = sizes.at[1:1 + 2 * couples:2].set(source_of - passed).at[2:2 + 2 * couples:2].set(taker + passed)
    return sizes[jax.random.permutation(jax.random.fold_in(rng, 2), count)]


def centred(key, dims, width, limit, cuts=(), kind=jnp.bfloat16):
    factor_of = level_of(key, dims, cuts, -0.22, 0.18) if cuts else 1.0
    values = jax.random.normal(key, dims, jnp.float32) * width * factor_of
    return jnp.minimum(jnp.maximum(values, -limit), limit).astype(kind)


def bell_draw_with(rng, shape, scale, bound, split, heavy, kind=jnp.bfloat16):
    values = scale * jax.random.normal(rng, shape, jnp.float32)
    if split:
        values = values * level_of(rng, shape, split, -0.22, 0.18)
    return jnp.clip(with_spikes(values, jax.random.fold_in(rng, 3), *heavy), -bound, bound).astype(kind)


def setup_inputs(seed: int = 0) -> dict:
    keys = jax.random.split(jax.random.key(seed), 24)
    tokens = centred(keys[0], (TOKENS, MODEL_DIM), 1.0, 6.0, ((0, 32),))
    cotangent = bell_draw_with(keys[1], (TOKENS, MODEL_DIM), 1.0, 6.0, ((0, 32),), (0, 1, 32, 2.75))
    order = jax.vmap(lambda own: jax.random.permutation(own, N_DP))(jax.random.split(keys[2], N_GROUP)).reshape((N_GROUP, N_DP)).astype(jnp.int32)
    lengths = jax.vmap(lambda own: uneven_parts(own, SEQS_DEV, PACK_TOKENS, MAX_LEN, 2))(jax.random.split(keys[3], N_DP * N_GROUP)).reshape((N_DP, N_GROUP, SEQS_DEV)).astype(jnp.int32)
    adapter_ids = place_ends(jax.random.randint(keys[4], (N_DP, N_GROUP, SEQS_DEV), 0, ADAPTERS), jax.random.fold_in(keys[4], 1), 0, ADAPTERS - 1).astype(jnp.int32)
    norm_gain = jnp.clip(1.0 + 0.1 * jax.random.normal(keys[5], (MODEL_DIM,), jnp.float32), 0.5, 1.5)
    ffn_gain = jnp.clip(1.0 + 0.1 * jax.random.normal(keys[6], (MODEL_DIM,), jnp.float32), 0.5, 1.5)
    conv_weight = centred(keys[7], (3, MODEL_DIM), 3 ** -0.5, 3.5, (), jnp.float32)
    in_weight = centred(keys[8], (MODEL_DIM, 3 * MODEL_DIM), MODEL_DIM ** -0.5, 0.1875, ((1, 4),))
    out_weight = centred(keys[9], (MODEL_DIM, MODEL_DIM), MODEL_DIM ** -0.5, 0.1875, ((1, 4),))
    gate_weight = centred(keys[10], (MODEL_DIM, FEEDFORWARD_DIM), MODEL_DIM ** -0.5, 0.1875, ((1, 4),))
    up_weight = centred(keys[11], (MODEL_DIM, FEEDFORWARD_DIM), MODEL_DIM ** -0.5, 0.1875, ((1, 4),))
    down_weight = centred(keys[12], (FEEDFORWARD_DIM, MODEL_DIM), FEEDFORWARD_DIM ** -0.5, 0.09375, ((1, 4),))
    input_first_factor = centred(keys[13], (MODEL_DIM, ADAPTER_COLUMNS), MODEL_DIM ** -0.5, 0.1875)
    input_second_factor = centred(keys[14], (ADAPTER_COLUMNS, 3 * MODEL_DIM), 0.125, 0.75)
    output_first_factor = centred(keys[15], (MODEL_DIM, ADAPTER_COLUMNS), MODEL_DIM ** -0.5, 0.1875)
    output_second_factor = centred(keys[16], (ADAPTER_COLUMNS, MODEL_DIM), 0.125, 0.75)
    gate_first_factor = centred(keys[17], (MODEL_DIM, ADAPTER_COLUMNS), MODEL_DIM ** -0.5, 0.1875)
    gate_second_factor = centred(keys[18], (ADAPTER_COLUMNS, FEEDFORWARD_DIM), 0.125, 0.75)
    up_first_factor = centred(keys[19], (MODEL_DIM, ADAPTER_COLUMNS), MODEL_DIM ** -0.5, 0.1875)
    up_second_factor = centred(keys[20], (ADAPTER_COLUMNS, FEEDFORWARD_DIM), 0.125, 0.75)
    down_first_factor = centred(keys[21], (FEEDFORWARD_DIM, ADAPTER_COLUMNS), FEEDFORWARD_DIM ** -0.5, 0.09375)
    down_second_factor = centred(keys[22], (ADAPTER_COLUMNS, MODEL_DIM), 0.125, 0.75)
    return dict(tokens=tokens, cotangent=cotangent, order=order, lengths=lengths, adapter_ids=adapter_ids, norm_gain=norm_gain, ffn_gain=ffn_gain, conv_weight=conv_weight, in_weight=in_weight, out_weight=out_weight, gate_weight=gate_weight, up_weight=up_weight, down_weight=down_weight, input_first_factor=input_first_factor, input_second_factor=input_second_factor, output_first_factor=output_first_factor, output_second_factor=output_second_factor, gate_first_factor=gate_first_factor, gate_second_factor=gate_second_factor, up_first_factor=up_first_factor, up_second_factor=up_second_factor, down_first_factor=down_first_factor, down_second_factor=down_second_factor)


@jax.custom_vjp
def rank_space_output(v):
    return lax.optimization_barrier(v.astype(jnp.bfloat16)).astype(jnp.float32)

@jax.custom_vjp
def rank_space_backward(v):
    return v

def low_keep(v):
    return (rank_space_output(v), None)

def low_pass(kept, grad):
    return (grad,)

def back_keep(v):
    return (v, None)

def back_low(kept, grad):
    return (rank_space_output(grad),)
rank_space_output.defvjp(low_keep, low_pass)
rank_space_backward.defvjp(back_keep, back_low)
eps_norm = 1e-05
adapter_scale = 2.0

def matrix_multiply(left, right):
    return jnp.dot(left, right, precision=lax.Precision.HIGHEST, preferred_element_type=jnp.float32)

def rms_norm(values, gain):
    return values * lax.rsqrt(lax.optimization_barrier(jnp.mean(values * values, axis=-1, keepdims=True)) + eps_norm) * gain

def per_token_tables(sequence_length_row, adapter_index_row, count_of_rows, adapter_column_span):
    finish = jnp.cumsum(sequence_length_row).astype(jnp.int32)
    starts = (finish - sequence_length_row).astype(jnp.int32)
    counter = jnp.arange(count_of_rows, dtype=jnp.int32)
    member = ((counter[:, None] >= starts[None, :]) & (counter[:, None] < finish[None, :])).astype(jnp.int32)
    beginning = lax.optimization_barrier(jnp.sum(member * starts[None, :], axis=1)).astype(jnp.int32)
    position = counter - beginning
    chosen = lax.optimization_barrier(jnp.sum(member * adapter_index_row[None, :], axis=1)).astype(jnp.int32)
    column_span = jnp.arange(adapter_column_span, dtype=jnp.int32) // ADAPTER_RANK
    select_adapter = (column_span[None, :] == chosen[:, None]).astype(jnp.float32)
    after_one = (position >= 1).astype(jnp.float32)[:, None]
    after_two = (position >= 2).astype(jnp.float32)[:, None]
    return (select_adapter, after_one, after_two)

def delayed(values, amount):
    return jnp.concatenate([jnp.zeros((amount, values.shape[1]), values.dtype), values[:-amount]], axis=0)

def adapter_project(input_rows, frozen_weight, adapter_down_factor, adapter_up_factor, select_adapter):
    reduced_sum = rank_space_backward(rank_space_output(matrix_multiply(input_rows, adapter_down_factor)))
    return rank_space_backward(matrix_multiply(input_rows, frozen_weight) + adapter_scale * matrix_multiply(reduced_sum * select_adapter, adapter_up_factor))

def block_forward(hidden_in, adapters, frozen_weight, adapter_tables):
    input_first_factor, input_second_factor, output_first_factor, output_second_factor, gate_first_factor, gate_second_factor, up_first_factor, up_second_factor, down_first_factor, down_second_factor = adapters
    norm_gain, ffn_gain, conv_weight, in_weight, out_weight, gate_weight, up_weight, down_weight = frozen_weight
    select_adapter, after_one, after_two = adapter_tables
    normed = rank_space_output(rms_norm(hidden_in, norm_gain))
    mixed_in = adapter_project(normed, in_weight, input_first_factor, input_second_factor, select_adapter)
    input_gate = mixed_in[:, :MODEL_DIM]
    output_gate = mixed_in[:, MODEL_DIM:2 * MODEL_DIM]
    conv_input = mixed_in[:, 2 * MODEL_DIM:]
    gated = input_gate * conv_input
    convolved = conv_weight[2] * gated + conv_weight[1] * delayed(gated, 1) * after_one + conv_weight[0] * delayed(gated, 2) * after_two
    mixer = rank_space_output(output_gate * convolved)
    middle = hidden_in + adapter_project(mixer, out_weight, output_first_factor, output_second_factor, select_adapter)
    normed_two = rank_space_output(rms_norm(middle, ffn_gain))
    gate_pre = adapter_project(normed_two, gate_weight, gate_first_factor, gate_second_factor, select_adapter)
    up_pre = adapter_project(normed_two, up_weight, up_first_factor, up_second_factor, select_adapter)
    activated = rank_space_output(jax.nn.silu(gate_pre) * up_pre)
    return middle + adapter_project(activated, down_weight, down_first_factor, down_second_factor, select_adapter)

def reference(tokens, cotangent, order, lengths, adapter_ids, norm_gain, ffn_gain, conv_weight, in_weight, out_weight, gate_weight, up_weight, down_weight, input_first_factor, input_second_factor, output_first_factor, output_second_factor, gate_first_factor, gate_second_factor, up_first_factor, up_second_factor, down_first_factor, down_second_factor):
    frozen_weight = (norm_gain.astype(jnp.float32), ffn_gain.astype(jnp.float32), conv_weight.astype(jnp.float32), in_weight.astype(jnp.float32), out_weight.astype(jnp.float32), gate_weight.astype(jnp.float32), up_weight.astype(jnp.float32), down_weight.astype(jnp.float32))
    adapters = (input_first_factor.astype(jnp.float32), input_second_factor.astype(jnp.float32), output_first_factor.astype(jnp.float32), output_second_factor.astype(jnp.float32), gate_first_factor.astype(jnp.float32), gate_second_factor.astype(jnp.float32), up_first_factor.astype(jnp.float32), up_second_factor.astype(jnp.float32), down_first_factor.astype(jnp.float32), down_second_factor.astype(jnp.float32))
    counting = jnp.arange(N_DP, dtype=jnp.int32)
    match = order[:, :, None] == counting[None, None, :]
    inverse = lax.optimization_barrier(jnp.sum(jnp.where(match, counting[None, :, None], 0), axis=1)).astype(jnp.int32)
    grads_dealt = cotangent.astype(jnp.float32).reshape(N_DP, N_GROUP, PACK_TOKENS, MODEL_DIM)
    grads_home = jax.vmap(lambda column, picks: column[picks], in_axes=(1, 0), out_axes=1)(grads_dealt, inverse)
    packs = N_DP * N_GROUP
    token_packs = tokens.astype(jnp.float32).reshape(packs, PACK_TOKENS, MODEL_DIM)
    grads_home = grads_home.reshape(packs, PACK_TOKENS, MODEL_DIM)
    length_rows = lengths.reshape(packs, SEQS_DEV)
    adapter_rows = adapter_ids.reshape(packs, SEQS_DEV)

    def one_pack(carry, items):
        hidden_in, upstream, sequence_length_row, adapter_index_row = items
        adapter_tables = per_token_tables(sequence_length_row, adapter_index_row, PACK_TOKENS, ADAPTER_COLUMNS)

        def forward(values, params):
            return block_forward(values, params, frozen_weight, adapter_tables)
        result, pull = jax.vjp(forward, hidden_in, adapters)
        grad_in, grad_adapters = pull(upstream)
        carry = jax.tree.map(lambda total, term: total + term, carry, grad_adapters)
        return (carry, (result.astype(jnp.bfloat16), grad_in.astype(jnp.bfloat16)))
    start_carry = jax.tree.map(lambda arr: jnp.zeros(arr.shape, jnp.float32), adapters)
    totals, (results, grads_in) = lax.scan(one_pack, start_carry, (token_packs, grads_home, length_rows, adapter_rows))
    block_output = results.reshape(TOKENS, MODEL_DIM)
    input_grad = grads_in.reshape(TOKENS, MODEL_DIM)
    return (block_output, input_grad, totals[0], totals[1], totals[2], totals[3], totals[4], totals[5], totals[6], totals[7], totals[8], totals[9])
```

```python
import jax
import jax.numpy as jnp
from jax import lax
from jax.sharding import PartitionSpec as P

ADAPTER_RANK = 16


eps_norm = 1e-05
adapter_scale = 2.0


def matrix_product(left, right):
    return jnp.dot(left, right, preferred_element_type=jnp.float32)


def transposed_left_matmul(left, right):
    return lax.dot_general(
        left, right, (((0,), (0,)), ((), ())), preferred_element_type=jnp.float32
    )


def transposed_right_matmul(left, right):
    return lax.dot_general(
        left, right, (((1,), (1,)), ((), ())), preferred_element_type=jnp.float32
    )


def per_token_tables(
    sequence_length_row, adapter_index_row, count_of_rows, adapter_column_span, adapter_rank_size
):
    count = sequence_length_row.shape[0]
    earlier = jnp.arange(count)[:, None] <= jnp.arange(count)[None, :]
    finish = jnp.sum(jnp.where(earlier, sequence_length_row[:, None], 0), axis=0)
    starts = finish - sequence_length_row
    counter = jnp.arange(count_of_rows, dtype=jnp.int32)
    member = ((counter[:, None] >= starts[None, :]) & (counter[:, None] < finish[None, :])).astype(
        jnp.int32
    )
    beginning = jnp.sum(member * starts[None, :], axis=1)
    position = counter - beginning
    chosen = jnp.sum(member * adapter_index_row[None, :], axis=1)
    column_span = jnp.arange(adapter_column_span, dtype=jnp.int32) // adapter_rank_size
    select_adapter = (column_span[None, :] == chosen[:, None]).astype(jnp.bfloat16)
    after_one = (position >= 1).astype(jnp.float32)[:, None]
    after_two = (position >= 2).astype(jnp.float32)[:, None]
    return (select_adapter, after_one, after_two)


def delayed(values, amount):
    return jnp.concatenate(
        [jnp.zeros((amount, values.shape[1]), values.dtype), values[:-amount]], axis=0
    )


def advanced(values, amount):
    return jnp.concatenate(
        [values[amount:], jnp.zeros((amount, values.shape[1]), values.dtype)], axis=0
    )


def regroup(values, picks, pieces):
    size = values.shape[0] // pieces
    return jnp.concatenate(
        [lax.dynamic_slice_in_dim(values, picks[i] * size, size, 0) for i in range(pieces)], axis=0
    )


def gather_weight(shard):
    size = shard.shape[0] // lax.axis_size("dp")
    piece = lax.dynamic_slice_in_dim(shard, lax.axis_index("dp") * size, size, 0)
    stacked = lax.all_gather(piece, ("group", "dp"))
    return stacked.reshape(lax.axis_size("group"), shard.shape[0], shard.shape[1])


def wide_product(rows, stacked):
    out = jnp.einsum("rk,gkn->rgn", rows, stacked, preferred_element_type=jnp.float32)
    return out.reshape(rows.shape[0], -1)


def wide_product_back(grads, stacked):
    shaped = grads.reshape(grads.shape[0], stacked.shape[0], stacked.shape[2])
    return jnp.einsum("rgn,gkn->rk", shaped, stacked, preferred_element_type=jnp.float32)


def reduce_grads(terms):
    groups = lax.axis_size("group")
    parts = [t.astype(jnp.bfloat16).reshape(groups, -1, t.shape[1]) for t in terms]
    joined = jnp.concatenate(parts, axis=1)
    flat = joined.reshape(-1, joined.shape[2])
    mine = lax.psum_scatter(flat, ("group", "dp"), scatter_dimension=0, tiled=True)
    share = lax.all_gather(mine, "dp", tiled=True)
    out, at = [], 0
    for p in parts:
        out.append(share[at : at + p.shape[1]].astype(jnp.float32))
        at += p.shape[1]
    return out


def inverse_root(values):
    return lax.rsqrt(jnp.mean(values * values, axis=-1, keepdims=True) + eps_norm)


def norm_back(values, inverse, gain, incoming_gradient):
    scaled = gain * incoming_gradient
    return inverse * scaled - values * (inverse * inverse * inverse) * jnp.mean(
        values * scaled, axis=-1, keepdims=True
    )


def adapter_project(
    input_rows, frozen_weight, adapter_down_factor, adapter_up_factor, select_adapter
):
    reduced_sum = (
        matrix_product(input_rows, adapter_down_factor).astype(jnp.bfloat16) * select_adapter
    )
    return (
        wide_product(input_rows, frozen_weight)
        + adapter_scale * matrix_product(reduced_sum, adapter_up_factor),
        reduced_sum,
    )


def adapter_project_backward(
    incoming_gradient,
    input_rows,
    frozen_weight,
    adapter_down_factor,
    adapter_up_factor,
    reduced_sum,
    select_adapter,
):
    gradient_rank_space = incoming_gradient.astype(jnp.bfloat16)
    gradient_up_factor = adapter_scale * transposed_left_matmul(gradient_rank_space, reduced_sum)
    gradient_reduced_sum = (
        adapter_scale
        * transposed_right_matmul(gradient_rank_space, adapter_up_factor)
        * select_adapter
    ).astype(jnp.bfloat16)
    grad_down = transposed_left_matmul(input_rows, gradient_reduced_sum)
    input_gradients = wide_product_back(
        gradient_rank_space, frozen_weight
    ) + transposed_right_matmul(gradient_reduced_sum, adapter_down_factor)
    return (input_gradients, grad_down, gradient_up_factor)


def local(
    tokens,
    cotangent,
    order,
    lengths,
    adapter_ids,
    norm_gain,
    ffn_gain,
    conv_weight,
    in_weight,
    out_weight,
    gate_weight,
    up_weight,
    down_weight,
    input_first_factor,
    input_second_factor,
    output_first_factor,
    output_second_factor,
    gate_first_factor,
    gate_second_factor,
    up_first_factor,
    up_second_factor,
    down_first_factor,
    down_second_factor,
):
    dp_count = lax.axis_size("dp")
    dp_index = lax.axis_index("dp")
    count_of_rows = tokens.shape[0]
    model_width = tokens.shape[1]
    order_row = order[0]
    counting = jnp.arange(dp_count, dtype=jnp.int32)
    inverse_row = jnp.sum(
        jnp.where(order_row[None, :] == counting[:, None], counting[None, :], 0), axis=1
    )
    arrived = lax.all_to_all(cotangent, "dp", split_axis=0, concat_axis=0, tiled=True)
    cotangent = lax.all_to_all(
        regroup(arrived, inverse_row, dp_count), "dp", split_axis=0, concat_axis=0, tiled=True
    )
    pack_source = dp_index
    hidden_in = tokens
    sequence_length_row = lengths[:, 0, :][pack_source]
    adapter_index_row = adapter_ids[:, 0, :][pack_source]
    select_adapter, after_one, after_two = per_token_tables(
        sequence_length_row,
        adapter_index_row,
        count_of_rows,
        input_first_factor.shape[1],
        ADAPTER_RANK,
    )
    shards = (in_weight, out_weight, gate_weight, up_weight, down_weight)
    full_in, full_out, full_gate, full_up, full_down = [gather_weight(w) for w in shards]
    hidden32 = hidden_in.astype(jnp.float32)
    inverse_one = inverse_root(hidden32)
    normed = (hidden32 * inverse_one * norm_gain).astype(jnp.bfloat16)
    mixed_in, reduced_in = adapter_project(
        normed, full_in, input_first_factor, input_second_factor, select_adapter
    )
    input_gate = mixed_in[:, :model_width]
    output_gate = mixed_in[:, model_width : 2 * model_width]
    conv_input = mixed_in[:, 2 * model_width :]
    gated = input_gate * conv_input
    convolved = (
        conv_weight[2] * gated
        + conv_weight[1] * delayed(gated, 1) * after_one
        + conv_weight[0] * delayed(gated, 2) * after_two
    )
    mixer = (output_gate * convolved).astype(jnp.bfloat16)
    branch, reduced_out = adapter_project(
        mixer, full_out, output_first_factor, output_second_factor, select_adapter
    )
    middle = hidden32 + branch
    inverse_two = inverse_root(middle)
    normed_two = (middle * inverse_two * ffn_gain).astype(jnp.bfloat16)
    gate_pre, reduced_gate = adapter_project(
        normed_two, full_gate, gate_first_factor, gate_second_factor, select_adapter
    )
    up_pre, reduced_up = adapter_project(
        normed_two, full_up, up_first_factor, up_second_factor, select_adapter
    )
    sigmoid_gate = jax.nn.sigmoid(gate_pre)
    activated = (gate_pre * sigmoid_gate * up_pre).astype(jnp.bfloat16)
    ffn_out, reduced_down = adapter_project(
        activated, full_down, down_first_factor, down_second_factor, select_adapter
    )
    result = (middle + ffn_out).astype(jnp.bfloat16)
    back_in, back_out, back_gate, back_up, back_down = full_in, full_out, full_gate, full_up, full_down
    upstream32 = cotangent.astype(jnp.float32)
    grad_act, down_a_grad, down_b_grad = adapter_project_backward(
        upstream32,
        activated,
        back_down,
        down_first_factor,
        down_second_factor,
        reduced_down,
        select_adapter,
    )
    grad_gate_pre = grad_act * up_pre * (sigmoid_gate * (1.0 + gate_pre * (1.0 - sigmoid_gate)))
    grad_up_pre = grad_act * gate_pre * sigmoid_gate
    grad_from_gate, gate_a_grad, gate_b_grad = adapter_project_backward(
        grad_gate_pre,
        normed_two,
        back_gate,
        gate_first_factor,
        gate_second_factor,
        reduced_gate,
        select_adapter,
    )
    grad_from_up, up_a_grad, up_b_grad = adapter_project_backward(
        grad_up_pre,
        normed_two,
        back_up,
        up_first_factor,
        up_second_factor,
        reduced_up,
        select_adapter,
    )
    grad_middle = upstream32 + norm_back(
        middle, inverse_two, ffn_gain, grad_from_gate + grad_from_up
    )
    grad_mixer, out_a_grad, out_b_grad = adapter_project_backward(
        grad_middle,
        mixer,
        back_out,
        output_first_factor,
        output_second_factor,
        reduced_out,
        select_adapter,
    )
    grad_output_gate = grad_mixer * convolved
    grad_conv = grad_mixer * output_gate
    grad_gated = (
        conv_weight[2] * grad_conv
        + conv_weight[1] * advanced(grad_conv * after_one, 1)
        + conv_weight[0] * advanced(grad_conv * after_two, 2)
    )
    grad_mixed = jnp.concatenate(
        [grad_gated * conv_input, grad_output_gate, grad_gated * input_gate], axis=1
    )
    grad_normed, in_a_grad, in_b_grad = adapter_project_backward(
        grad_mixed,
        normed,
        back_in,
        input_first_factor,
        input_second_factor,
        reduced_in,
        select_adapter,
    )
    grad_input = (grad_middle + norm_back(hidden32, inverse_one, norm_gain, grad_normed)).astype(
        jnp.bfloat16
    )
    early = reduce_grads(
        [down_a_grad, down_b_grad, gate_a_grad, gate_b_grad, up_a_grad, up_b_grad, out_a_grad, out_b_grad]
    )
    late = reduce_grads([in_a_grad, in_b_grad])
    totals = (
        late[0], late[1].T, early[6], early[7].T, early[2], early[3].T, early[4], early[5].T,
        early[0], early[1].T,
    )
    return (
        result,
        grad_input,
        totals[0],
        totals[1],
        totals[2],
        totals[3],
        totals[4],
        totals[5],
        totals[6],
        totals[7],
        totals[8],
        totals[9],
    )


def solution(mesh):
    in_specs = (
        P(("dp", "group"), None),
        P(("dp", "group"), None),
        P("group", None),
        P(None, "group", None),
        P(None, "group", None),
        P(),
        P(),
        P(),
        P(None, "group"),
        P(None, "group"),
        P(None, "group"),
        P(None, "group"),
        P(None, "group"),
        P(),
        P(),
        P(),
        P(),
        P(),
        P(),
        P(),
        P(),
        P(),
        P(),
    )
    out_specs = (
        P(("dp", "group"), None),
        P(("dp", "group"), None),
        P("group", None),
        P(None, "group"),
        P("group", None),
        P(None, "group"),
        P("group", None),
        P(None, "group"),
        P("group", None),
        P(None, "group"),
        P("group", None),
        P(None, "group"),
    )
    return jax.shard_map(local, mesh=mesh, in_specs=in_specs, out_specs=out_specs, check_vma=False)
```

```python
import jax
import jax.numpy as jnp
from jax import lax
from jax.experimental import pallas as pl
from jax.experimental.pallas import tpu as pltpu
from jax.sharding import PartitionSpec as P

ADAPTER_RANK = 16


eps_norm = 1e-05
adapter_scale = 2.0


def matrix_product(left, right):
    return jnp.dot(left, right, preferred_element_type=jnp.float32)


def transposed_left_matmul(left, right):
    return lax.dot_general(
        left, right, (((0,), (0,)), ((), ())), preferred_element_type=jnp.float32
    )


def transposed_right_matmul(left, right):
    return lax.dot_general(
        left, right, (((1,), (1,)), ((), ())), preferred_element_type=jnp.float32
    )


def per_token_tables(
    sequence_length_row, adapter_index_row, count_of_rows, adapter_column_span, adapter_rank_size
):
    count = sequence_length_row.shape[0]
    earlier = jnp.arange(count)[:, None] <= jnp.arange(count)[None, :]
    finish = jnp.sum(jnp.where(earlier, sequence_length_row[:, None], 0), axis=0)
    starts = finish - sequence_length_row
    counter = jnp.arange(count_of_rows, dtype=jnp.int32)
    member = ((counter[:, None] >= starts[None, :]) & (counter[:, None] < finish[None, :])).astype(
        jnp.int32
    )
    beginning = jnp.sum(member * starts[None, :], axis=1)
    position = counter - beginning
    chosen = jnp.sum(member * adapter_index_row[None, :], axis=1)
    column_span = jnp.arange(adapter_column_span, dtype=jnp.int32) // adapter_rank_size
    select_adapter = (column_span[None, :] == chosen[:, None]).astype(jnp.bfloat16)
    after_one = (position >= 1).astype(jnp.float32)[:, None]
    after_two = (position >= 2).astype(jnp.float32)[:, None]
    return (select_adapter, after_one, after_two)


def delayed(values, amount):
    return jnp.concatenate(
        [jnp.zeros((amount, values.shape[1]), values.dtype), values[:-amount]], axis=0
    )


def advanced(values, amount):
    return jnp.concatenate(
        [values[amount:], jnp.zeros((amount, values.shape[1]), values.dtype)], axis=0
    )


def regroup(values, picks, pieces):
    size = values.shape[0] // pieces
    return jnp.concatenate(
        [lax.dynamic_slice_in_dim(values, picks[i] * size, size, 0) for i in range(pieces)], axis=0
    )


def gather_weight(shard):
    size = shard.shape[0] // lax.axis_size("dp")
    piece = lax.dynamic_slice_in_dim(shard, lax.axis_index("dp") * size, size, 0)
    stacked = lax.all_gather(piece, ("group", "dp"))
    return stacked.reshape(lax.axis_size("group"), shard.shape[0], shard.shape[1])


def wide_product(rows, stacked):
    out = jnp.einsum("rk,gkn->rgn", rows, stacked, preferred_element_type=jnp.float32)
    return out.reshape(rows.shape[0], -1)


def wide_product_back(grads, stacked):
    shaped = grads.reshape(grads.shape[0], stacked.shape[0], stacked.shape[2])
    return jnp.einsum("rgn,gkn->rk", shaped, stacked, preferred_element_type=jnp.float32)


def reduce_grads(terms):
    groups = lax.axis_size("group")
    parts = [t.astype(jnp.bfloat16).reshape(groups, -1, t.shape[1]) for t in terms]
    joined = jnp.concatenate(parts, axis=1)
    flat = joined.reshape(-1, joined.shape[2])
    mine = lax.psum_scatter(flat, ("group", "dp"), scatter_dimension=0, tiled=True)
    share = lax.all_gather(mine, "dp", tiled=True)
    out, at = [], 0
    for p in parts:
        out.append(share[at : at + p.shape[1]].astype(jnp.float32))
        at += p.shape[1]
    return out


def inverse_root(values):
    return lax.rsqrt(jnp.mean(values * values, axis=-1, keepdims=True) + eps_norm)


def norm_back(values, inverse, gain, incoming_gradient):
    scaled = gain * incoming_gradient
    return inverse * scaled - values * (inverse * inverse * inverse) * jnp.mean(
        values * scaled, axis=-1, keepdims=True
    )


def adapter_project(
    input_rows, frozen_weight, adapter_down_factor, adapter_up_factor, select_adapter
):
    reduced_sum = (
        matrix_product(input_rows, adapter_down_factor).astype(jnp.bfloat16) * select_adapter
    )
    return (
        wide_product(input_rows, frozen_weight)
        + adapter_scale * matrix_product(reduced_sum, adapter_up_factor),
        reduced_sum,
    )


def adapter_project_backward(
    incoming_gradient,
    input_rows,
    frozen_weight,
    adapter_down_factor,
    adapter_up_factor,
    reduced_sum,
    select_adapter,
):
    gradient_rank_space = incoming_gradient.astype(jnp.bfloat16)
    gradient_up_factor = adapter_scale * transposed_left_matmul(gradient_rank_space, reduced_sum)
    gradient_reduced_sum = (
        adapter_scale
        * transposed_right_matmul(gradient_rank_space, adapter_up_factor)
        * select_adapter
    ).astype(jnp.bfloat16)
    grad_down = transposed_left_matmul(input_rows, gradient_reduced_sum)
    input_gradients = wide_product_back(
        gradient_rank_space, frozen_weight
    ) + transposed_right_matmul(gradient_reduced_sum, adapter_down_factor)
    return (input_gradients, grad_down, gradient_up_factor)


def local(
    tokens,
    cotangent,
    order,
    lengths,
    adapter_ids,
    norm_gain,
    ffn_gain,
    conv_weight,
    in_weight,
    out_weight,
    gate_weight,
    up_weight,
    down_weight,
    input_first_factor,
    input_second_factor,
    output_first_factor,
    output_second_factor,
    gate_first_factor,
    gate_second_factor,
    up_first_factor,
    up_second_factor,
    down_first_factor,
    down_second_factor,
):
    dp_count = lax.axis_size("dp")
    dp_index = lax.axis_index("dp")
    count_of_rows = tokens.shape[0]
    model_width = tokens.shape[1]
    order_row = order[0]
    counting = jnp.arange(dp_count, dtype=jnp.int32)
    inverse_row = jnp.sum(
        jnp.where(order_row[None, :] == counting[:, None], counting[None, :], 0), axis=1
    )
    arrived = lax.all_to_all(cotangent, "dp", split_axis=0, concat_axis=0, tiled=True)
    cotangent = lax.all_to_all(
        regroup(arrived, inverse_row, dp_count), "dp", split_axis=0, concat_axis=0, tiled=True
    )
    pack_source = dp_index
    hidden_in = tokens
    sequence_length_row = lengths[:, 0, :][pack_source]
    adapter_index_row = adapter_ids[:, 0, :][pack_source]
    select_adapter, after_one, after_two = per_token_tables(
        sequence_length_row,
        adapter_index_row,
        count_of_rows,
        input_first_factor.shape[1],
        ADAPTER_RANK,
    )
    shards = (in_weight, out_weight, gate_weight, up_weight, down_weight)
    full_in, full_out, full_gate, full_up, full_down = [gather_weight(w) for w in shards]
    hidden32 = hidden_in.astype(jnp.float32)
    inverse_one = inverse_root(hidden32)
    normed = (hidden32 * inverse_one * norm_gain).astype(jnp.bfloat16)
    mixed_in, reduced_in = adapter_project(
        normed, full_in, input_first_factor, input_second_factor, select_adapter
    )
    input_gate = mixed_in[:, :model_width]
    output_gate = mixed_in[:, model_width : 2 * model_width]
    conv_input = mixed_in[:, 2 * model_width :]
    gated = input_gate * conv_input
    convolved = (
        conv_weight[2] * gated
        + conv_weight[1] * delayed(gated, 1) * after_one
        + conv_weight[0] * delayed(gated, 2) * after_two
    )
    mixer = (output_gate * convolved).astype(jnp.bfloat16)
    branch, reduced_out = adapter_project(
        mixer, full_out, output_first_factor, output_second_factor, select_adapter
    )
    middle = hidden32 + branch
    inverse_two = inverse_root(middle)
    normed_two = (middle * inverse_two * ffn_gain).astype(jnp.bfloat16)
    gate_pre, reduced_gate = adapter_project(
        normed_two, full_gate, gate_first_factor, gate_second_factor, select_adapter
    )
    up_pre, reduced_up = adapter_project(
        normed_two, full_up, up_first_factor, up_second_factor, select_adapter
    )
    sigmoid_gate = jax.nn.sigmoid(gate_pre)
    activated = (gate_pre * sigmoid_gate * up_pre).astype(jnp.bfloat16)
    ffn_out, reduced_down = adapter_project(
        activated, full_down, down_first_factor, down_second_factor, select_adapter
    )
    result = (middle + ffn_out).astype(jnp.bfloat16)
    back_in, back_out, back_gate, back_up, back_down = full_in, full_out, full_gate, full_up, full_down
    upstream32 = cotangent.astype(jnp.float32)
    grad_act, down_a_grad, down_b_grad = adapter_project_backward(
        upstream32,
        activated,
        back_down,
        down_first_factor,
        down_second_factor,
        reduced_down,
        select_adapter,
    )
    grad_gate_pre = grad_act * up_pre * (sigmoid_gate * (1.0 + gate_pre * (1.0 - sigmoid_gate)))
    grad_up_pre = grad_act * gate_pre * sigmoid_gate
    grad_from_gate, gate_a_grad, gate_b_grad = adapter_project_backward(
        grad_gate_pre,
        normed_two,
        back_gate,
        gate_first_factor,
        gate_second_factor,
        reduced_gate,
        select_adapter,
    )
    grad_from_up, up_a_grad, up_b_grad = adapter_project_backward(
        grad_up_pre,
        normed_two,
        back_up,
        up_first_factor,
        up_second_factor,
        reduced_up,
        select_adapter,
    )
    grad_middle = upstream32 + norm_back(
        middle, inverse_two, ffn_gain, grad_from_gate + grad_from_up
    )
    grad_mixer, out_a_grad, out_b_grad = adapter_project_backward(
        grad_middle,
        mixer,
        back_out,
        output_first_factor,
        output_second_factor,
        reduced_out,
        select_adapter,
    )
    grad_output_gate = grad_mixer * convolved
    grad_conv = grad_mixer * output_gate
    grad_gated = (
        conv_weight[2] * grad_conv
        + conv_weight[1] * advanced(grad_conv * after_one, 1)
        + conv_weight[0] * advanced(grad_conv * after_two, 2)
    )
    grad_mixed = jnp.concatenate(
        [grad_gated * conv_input, grad_output_gate, grad_gated * input_gate], axis=1
    )
    grad_normed, in_a_grad, in_b_grad = adapter_project_backward(
        grad_mixed,
        normed,
        back_in,
        input_first_factor,
        input_second_factor,
        reduced_in,
        select_adapter,
    )
    grad_input = (grad_middle + norm_back(hidden32, inverse_one, norm_gain, grad_normed)).astype(
        jnp.bfloat16
    )
    early = reduce_grads(
        [down_a_grad, down_b_grad, gate_a_grad, gate_b_grad, up_a_grad, up_b_grad, out_a_grad, out_b_grad]
    )
    late = reduce_grads([in_a_grad, in_b_grad])
    totals = (
        late[0], late[1].T, early[6], early[7].T, early[2], early[3].T, early[4], early[5].T,
        early[0], early[1].T,
    )
    return (
        result,
        grad_input,
        totals[0],
        totals[1],
        totals[2],
        totals[3],
        totals[4],
        totals[5],
        totals[6],
        totals[7],
        totals[8],
        totals[9],
    )


f32 = jnp.float32
bf16 = jnp.bfloat16
VMEM_BYTES = 60 * 2**20
PARTS = 3
X_BIT, Y_BIT, CORE_BIT = 2, 4, 1


def nn(a, b):
    return lax.dot_general(a, b, (((1,), (0,)), ((), ())), preferred_element_type=f32)


def nt(a, b):
    return lax.dot_general(a, b, (((1,), (1,)), ((), ())), preferred_element_type=f32)


def swap_dp(values, bit):
    return lax.ppermute(values, "dp", [(i, i ^ bit) for i in range(lax.axis_size("dp"))])


def stacked(parts):
    size = parts[0].shape[0]

    def kernel(*refs):
        out_ref, sems = refs[-2], refs[-1]
        copies = [
            pltpu.make_async_copy(refs[k], out_ref.at[k * size : (k + 1) * size], sems.at[k])
            for k in range(len(parts))
        ]
        for copy in copies:
            copy.start()
        for copy in copies:
            copy.wait()

    return pl.pallas_call(
        kernel,
        name="stacked",
        out_shape=jax.ShapeDtypeStruct((len(parts) * size, parts[0].shape[1]), parts[0].dtype),
        in_specs=[any_spec()] * len(parts),
        out_specs=vmem_spec(),
        scratch_shapes=[pltpu.SemaphoreType.DMA((len(parts),))],
    )(*parts)


def from_planes(piece):
    groups = lax.axis_size("group")
    return stacked(
        [
            lax.ppermute(piece, "group", [(i, (i + t) % groups) for i in range(groups)])
            for t in range(1, groups)
        ]
    )


def after(values, *others):
    return lax.optimization_barrier((values, *others))[0]


def piece_table():
    masks = [0, X_BIT, Y_BIT, X_BIT | Y_BIT]
    masks = masks + [m | CORE_BIT for m in masks]
    return [(m, (1, 2, 3)) for m in masks]


def any_spec():
    return pl.BlockSpec(memory_space=pl.ANY)


def vmem_spec():
    return pl.BlockSpec(memory_space=pltpu.VMEM)


def smem_spec():
    return pl.BlockSpec(memory_space=pltpu.SMEM)


def params():
    return pltpu.CompilerParams(vmem_limit_bytes=VMEM_BYTES)


def cost(flops):
    return pl.CostEstimate(flops=int(flops) // 16, transcendentals=0, bytes_accessed=int(flops) // 16000)


def sds(shape, dtype):
    return jax.ShapeDtypeStruct(shape, dtype)


BN = 256


def col(i):
    return pl.ds(pl.multiple_of(i * BN, BN), BN)


ROWS = 128


def row(i):
    return pl.ds(pl.multiple_of(i * ROWS, ROWS), ROWS)


def loop(n, body):
    def step(i, carry):
        body(i)
        return carry

    lax.fori_loop(0, n, step, 0)


def front_call(ids, pieces, in_shard, out_shard, x, gain1, gain2, taps, sel2, m1, m2,
               a_in, b_in, a_out, b_out, a_gu):
    rows, d = x.shape
    table = piece_table()
    n_pieces = len(pieces)
    h_in = in_shard.shape[1]
    h_out = out_shard.shape[1]
    pr = d // lax.axis_size("dp")
    c = a_in.shape[1]

    def kernel(*refs):
        ids_ref = refs[0]
        p_refs = refs[1 : 1 + n_pieces]
        (in_ref, out_ref, x_ref, g1_ref, g2_ref, taps_ref, sel_ref, m1_ref, m2_ref, a_in_ref, b_in_ref,
         a_out_ref, b_out_ref, a_gu_ref) = refs[1 + n_pieces : 15 + n_pieces]
        (n1_ref, zin_ref, mix_ref, cv_ref, y_ref, zout_ref, h_ref, n2_ref, zgu_ref, w_in_hbm, w_out_hbm,
         w_in, w_out, sem_in, sem_out, sem_store) = refs[15 + n_pieces :]
        s = ids_ref[0]
        z = ids_ref[1]

        def put(buf, sem, src, r0, c0, width):
            pltpu.make_async_copy(
                src, buf.at[pl.ds(pl.multiple_of(r0, 128), src.shape[0]), pl.ds(pl.multiple_of(c0, 128), width)], sem
            ).start()

        put(w_in, sem_in, in_ref, 0, z * h_in, h_in)
        for p_ref, (mask, steps) in zip(p_refs, table):
            for k, t in enumerate(steps):
                put(w_in, sem_in, p_ref.at[k * pr : (k + 1) * pr, :h_in], (s ^ mask) * pr, ((z - t) & 3) * h_in, h_in)
        put(w_out, sem_out, out_ref, 0, z * h_out, h_out)
        for p_ref, (mask, steps) in zip(p_refs, table):
            for k, t in enumerate(steps):
                put(w_out, sem_out, p_ref.at[k * pr : (k + 1) * pr, h_in:], (s ^ mask) * pr, ((z - t) & 3) * h_out, h_out)

        g1 = g1_ref[...]

        def norm1(i):
            v = x_ref[row(i), :].astype(f32)
            r = lax.rsqrt(jnp.mean(v * v, axis=-1, keepdims=True) + eps_norm)
            n1_ref[row(i), :] = (v * r * g1).astype(bf16)

        loop(rows // ROWS, norm1)
        zin_ref[...] = nn(n1_ref[...], a_in_ref[...]).astype(bf16) * sel_ref[...]
        pltpu.make_async_copy(w_in, w_in, sem_in).wait()
        store_in = pltpu.make_async_copy(w_in, w_in_hbm, sem_store.at[0])
        store_in.start()
        m1 = m1_ref[...]
        m2 = m2_ref[...]
        blocks = d // BN

        def mix(j):
            def part(k):
                cc = col(k * blocks + j)
                return nn(n1_ref[...], w_in[:, cc]) + nn(zin_ref[...], b_in_ref[:, cc])

            bg = part(0)
            mix_ref[:, col(j)] = bg.astype(bf16)
            xv = part(2)
            mix_ref[:, col(2 * blocks + j)] = xv.astype(bf16)
            bx = bg * xv
            cv = (
                taps_ref[2:3, col(j)] * bx
                + taps_ref[1:2, col(j)] * pltpu.roll(bx, 1, 0) * m1
                + taps_ref[0:1, col(j)] * pltpu.roll(bx, 2, 0) * m2
            )
            cv_ref[:, col(j)] = cv.astype(bf16)
            cg = part(1)
            mix_ref[:, col(blocks + j)] = cg.astype(bf16)
            y_ref[:, col(j)] = (cg * cv).astype(bf16)

        loop(blocks, mix)
        zout_ref[...] = nn(y_ref[...], a_out_ref[...]).astype(bf16) * sel_ref[...]
        pltpu.make_async_copy(w_out, w_out, sem_out).wait()
        store_out = pltpu.make_async_copy(w_out, w_out_hbm, sem_store.at[1])
        store_out.start()

        def mid(j):
            o = nn(y_ref[...], w_out[:, col(j)]) + nn(zout_ref[...], b_out_ref[:, col(j)])
            h_ref[:, col(j)] = x_ref[:, col(j)].astype(f32) + o

        loop(blocks, mid)
        g2 = g2_ref[...]

        def norm2(i):
            v = h_ref[row(i), :]
            r = lax.rsqrt(jnp.mean(v * v, axis=-1, keepdims=True) + eps_norm)
            n2_ref[row(i), :] = (v * r * g2).astype(bf16)

        loop(rows // ROWS, norm2)
        sel = sel_ref[...]
        zgu_ref[...] = nn(n2_ref[...], a_gu_ref[...]).astype(bf16) * jnp.concatenate([sel, sel], axis=1)
        store_in.wait()
        store_out.wait()

    outs = [
        sds((rows, d), bf16), sds((rows, c), bf16), sds((rows, 3 * d), bf16), sds((rows, d), bf16),
        sds((rows, d), bf16), sds((rows, c), bf16), sds((rows, d), f32), sds((rows, d), bf16),
        sds((rows, 2 * c), bf16), sds((d, 3 * d), bf16), sds((d, d), bf16),
    ]
    return pl.pallas_call(
        kernel,
        name="front",
        out_shape=outs,
        in_specs=[smem_spec()] + [any_spec()] * (n_pieces + 2) + [vmem_spec()] * 12,
        out_specs=[vmem_spec()] * 9 + [any_spec()] * 2,
        scratch_shapes=[
            pltpu.VMEM((d, 3 * d), bf16), pltpu.VMEM((d, d), bf16),
            pltpu.SemaphoreType.DMA, pltpu.SemaphoreType.DMA, pltpu.SemaphoreType.DMA((2,)),
        ],
        compiler_params=params(),
        cost_estimate=cost(2.6 * rows * d * 4 * d),
    )(ids, *pieces, in_shard, out_shard, x, gain1, gain2, taps, sel2, m1, m2, a_in, b_in, a_out, b_out, a_gu)


def ffn_call(part, ids, pieces, gate_shard, up_shard, down_shard, n2, dy, zgu, dzd,
             b_gate, b_up, a_down, acc, dn, dz_acc, zd_acc):
    rows, d = n2.shape
    table = piece_table()
    n_pieces = len(pieces)
    quarter = gate_shard.shape[1]
    width = quarter // PARTS
    fp = 4 * width
    pr = d // lax.axis_size("dp")
    dr = fp // lax.axis_size("dp")
    c = zgu.shape[1] // 2
    h_d = down_shard.shape[1]
    first = acc is None
    dps = lax.axis_size("dp")

    def kernel(*refs):
        ids_ref = refs[0]
        p_refs = refs[1 : 1 + n_pieces]
        rest = refs[1 + n_pieces :]
        (gs_ref, us_ref, ds_ref, bg_hbm, bu_hbm, ad_hbm, acc_hbm, dn_hbm, n2_ref, dy_ref, zgu_ref, dzd_ref,
         dz_in, zd_in) = rest[:14]
        (acc_out, dn_out, dz_ref, zd_ref, grads_ref, wg, wu, wd, bg, bu, ad, acc_ref, dn_ref, act, dgb, dub,
         g_tmp, u_tmp, da_tmp, g_all, sems) = rest[14:]
        s = ids_ref[0]
        z = ids_ref[1]
        sem_g, sem_u, sem_d, sem_f, sem_a, sem_n, sem_o = [sems.at[i] for i in range(7)]

        def put(buf, sem, src, r0, c0, ra=64):
            dst = buf.at[pl.ds(pl.multiple_of(r0, ra), src.shape[0]), pl.ds(pl.multiple_of(c0, 128), src.shape[1])]
            pltpu.make_async_copy(src, dst, sem).start()

        def pieces_to(fn):
            for p_ref, (mask, steps) in zip(p_refs, table):
                for k, t in enumerate(steps):
                    fn(p_ref, k * 3 * pr, s ^ mask, (z - t) & 3)

        mine = pl.ds(part * width, width)
        put(wg, sem_g, gs_ref.at[:, mine], 0, z * width)
        pieces_to(lambda p, r, s_, z_: put(wg, sem_g, p.at[r : r + pr, :], s_ * pr, z_ * width))
        for q in range(4):
            at = pl.ds(q * quarter + part * width, width)
            here = pl.ds(q * width, width)
            pltpu.make_async_copy(bg_hbm.at[:, at], bg.at[:, here], sem_f).start()
            pltpu.make_async_copy(bu_hbm.at[:, at], bu.at[:, here], sem_f).start()
            pltpu.make_async_copy(ad_hbm.at[at, :], ad.at[here, :], sem_f).start()
        put(wu, sem_u, us_ref.at[:, mine], 0, z * width)
        pieces_to(lambda p, r, s_, z_: put(wu, sem_u, p.at[r + pr : r + 2 * pr, :], s_ * pr, z_ * width))
        for q in range(4):
            put(wd, sem_d, ds_ref.at[pl.ds(q * quarter + part * width, width), :], q * width, z * h_d)
        half = dr - pr

        def put_down(p, r, s_, z_):
            put(wd, sem_d, p.at[r + 2 * pr : r + 3 * pr, :h_d], s_ * dr, z_ * h_d)
            put(wd, sem_d, p.at[r + 2 * pr : r + 2 * pr + half, h_d:], s_ * dr + pr, z_ * h_d)
            put(wd, sem_d, p.at[r + 2 * pr + half : r + 3 * pr, h_d:], s_ * dr + pr, z_ * h_d + width - h_d)

        pieces_to(put_down)
        load_acc = pltpu.make_async_copy(acc_hbm, acc_ref, sem_a)
        load_acc.start()
        if not first:
            load_dn = pltpu.make_async_copy(dn_hbm, dn_ref, sem_n)
            load_dn.start()

        zg_t = zgu_ref[:, :c].T
        zu_t = zgu_ref[:, c:].T
        dzd_t = dzd_ref[...].T
        for q in range(4):
            at = pl.ds(q * quarter + part * width, width)
            here = pl.ds(q * width, width)
            pltpu.make_async_copy(bg_hbm.at[:, at], bg.at[:, here], sem_f).wait()
            pltpu.make_async_copy(bu_hbm.at[:, at], bu.at[:, here], sem_f).wait()
            pltpu.make_async_copy(ad_hbm.at[at, :], ad.at[here, :], sem_f).wait()
        pltpu.make_async_copy(wg, wg, sem_g).wait()
        pltpu.make_async_copy(wu, wu, sem_u).wait()
        pltpu.make_async_copy(wd, wd, sem_d).wait()

        def block(j):
            cc = col(j)
            g_tmp[...] = nn(n2_ref[...], wg[:, cc]) + nn(zgu_ref[:, :c], bg[:, cc])
            u_tmp[...] = nn(n2_ref[...], wu[:, cc]) + nn(zgu_ref[:, c:], bu[:, cc])
            da_tmp[...] = nt(dy_ref[...], wd[cc, :]) + nt(dzd_ref[...], ad[cc, :])

            def point(i):
                g = g_tmp[row(i), :]
                u = u_tmp[row(i), :]
                da = da_tmp[row(i), :]
                sg = jax.nn.sigmoid(g)
                gs = g * sg
                act[row(i), cc] = (gs * u).astype(bf16)
                dub[row(i), cc] = (da * gs).astype(bf16)
                dgb[row(i), cc] = (da * u * (sg + gs * (1.0 - sg))).astype(bf16)

            loop(rows // ROWS, point)
            g_all[0, :, cc] = nn(zg_t, dgb[:, cc])
            g_all[1, :, cc] = nn(zu_t, dub[:, cc])
            g_all[2, :, cc] = nn(dzd_t, act[:, cc])

        loop(fp // BN, block)
        for k in range(3):
            for q in range(4):
                v = g_all[k, :, q * width : (q + 1) * width]
                grads_ref[:, q, k] = v.reshape(dps, c // dps, width).astype(bf16)
        dzg = nt(dgb[...], bg[...])
        dzu = nt(dub[...], bu[...])
        zd = nn(act[...], ad[...])
        if first:
            dz_ref[:, :c] = dzg
            dz_ref[:, c:] = dzu
            zd_ref[...] = zd
        else:
            dz_ref[:, :c] = dz_in[:, :c] + dzg
            dz_ref[:, c:] = dz_in[:, c:] + dzu
            zd_ref[...] = zd_in[...] + zd
        load_acc.wait()

        def out_block(j):
            acc_ref[:, col(j)] += nn(act[...], wd[:, col(j)])

        loop(d // BN, out_block)
        store_acc = pltpu.make_async_copy(acc_ref, acc_out, sem_a)
        store_acc.start()
        if not first:
            load_dn.wait()

        def dn_block(j):
            v = nt(dgb[...], wg[col(j), :]) + nt(dub[...], wu[col(j), :])
            dn_ref[:, col(j)] = v if first else dn_ref[:, col(j)] + v

        loop(d // BN, dn_block)
        store_dn = pltpu.make_async_copy(dn_ref, dn_out, sem_n)
        store_dn.start()
        store_acc.wait()
        store_dn.wait()

    outs = [
        sds((rows, d), f32), sds((rows, d), f32), sds((rows, 2 * c), f32), sds((rows, c), f32),
        sds((dps, 4, 3, c // dps, width), bf16),
    ]
    if first:
        acc, dn = dn, dn
        dz_acc = jnp.zeros((8, 2 * c), f32)
        zd_acc = jnp.zeros((8, c), f32)
    return pl.pallas_call(
        kernel,
        name=f"ffn{part}",
        out_shape=outs,
        in_specs=[smem_spec()] + [any_spec()] * (n_pieces + 8) + [vmem_spec()] * 6,
        out_specs=[any_spec()] * 2 + [vmem_spec()] * 3,
        scratch_shapes=[
            pltpu.VMEM((d, fp), bf16), pltpu.VMEM((d, fp), bf16), pltpu.VMEM((fp, d), bf16),
            pltpu.VMEM((c, fp), bf16), pltpu.VMEM((c, fp), bf16), pltpu.VMEM((fp, c), bf16),
            pltpu.VMEM((rows, d), f32), pltpu.VMEM((rows, d), f32),
            pltpu.VMEM((rows, fp), bf16), pltpu.VMEM((rows, fp), bf16), pltpu.VMEM((rows, fp), bf16),
            pltpu.VMEM((rows, BN), f32), pltpu.VMEM((rows, BN), f32), pltpu.VMEM((rows, BN), f32),
            pltpu.VMEM((3, c, fp), f32),
            pltpu.SemaphoreType.DMA((7,)),
        ],
        compiler_params=params(),
        cost_estimate=cost(2.6 * rows * d * 6 * fp),
    )(ids, *pieces, gate_shard, up_shard, down_shard, b_gate, b_up, a_down, acc, dn, n2, dy, zgu, dzd,
      dz_acc, zd_acc)


def norm_back_rows(v, gain, dn):
    r = lax.rsqrt(jnp.mean(v * v, axis=-1, keepdims=True) + eps_norm)
    scaled = gain * dn
    return r * scaled - v * (r * r * r * jnp.mean(v * scaled, axis=-1, keepdims=True))


def spread(ref, at, v):
    dps, c = ref.shape[0], v.shape[0]
    n = v.shape[1] // 4
    for q in range(4):
        ref[:, q, :, at : at + n] = v[:, q * n : (q + 1) * n].reshape(dps, c // dps, n).astype(bf16)


def middle_call(acc, dn, dz_acc, zd_acc, h, n2, dy, y, zout, sel2, gain2, b_down, a_gu, b_out):
    rows, d = h.shape
    c = zout.shape[1]
    blocks = d // BN
    dps = lax.axis_size("dp")

    def kernel(acc_ref, dn_ref, dz_in, zd_in, h_ref, n2_ref, dy_ref, y_ref, zout_ref, sel_ref, g2_ref,
               b_down_ref, a_gu_ref, b_out_ref, res_ref, dh_ref, dhb, dzo, ga_ref, dzgu, zd):
        sel = sel_ref[...]
        sel_f = sel.astype(f32)
        zd[...] = zd_in[...].astype(bf16) * sel
        dzgu[:, :c] = (dz_in[:, :c] * sel_f).astype(bf16)
        dzgu[:, c:] = (dz_in[:, c:] * sel_f).astype(bf16)

        def results(j):
            res_ref[:, col(j)] = (acc_ref[:, col(j)] + nn(zd[...], b_down_ref[:, col(j)])).astype(bf16)

        loop(blocks, results)
        spread(ga_ref, d // 4, nn(zd[...].T, dy_ref[...]))

        def dns(j):
            dh_ref[:, col(j)] = dn_ref[:, col(j)] + nt(dzgu[...], a_gu_ref[col(j), :])

        loop(blocks, dns)
        g = nn(dzgu[...].T, n2_ref[...])
        spread(ga_ref, 2 * (d // 4), g[:c])
        spread(ga_ref, 3 * (d // 4), g[c:])
        g2 = g2_ref[...]

        def norm2(i):
            v = dy_ref[row(i), :].astype(f32) + norm_back_rows(h_ref[row(i), :], g2, dh_ref[row(i), :])
            dh_ref[row(i), :] = v
            dhb[row(i), :] = v.astype(bf16)

        loop(rows // ROWS, norm2)
        dzo[...] = (nt(dhb[...], b_out_ref[...]) * sel_f).astype(bf16)
        spread(ga_ref, 0, nn(zout_ref[...].T, dhb[...]))
        spread(ga_ref, 4 * (d // 4), nn(dzo[...].T, y_ref[...]))

    return pl.pallas_call(
        kernel,
        name="middle",
        out_shape=[
            sds((rows, d), bf16), sds((rows, d), f32), sds((rows, d), bf16), sds((rows, c), bf16),
            sds((dps, 4, c // dps, 5 * (d // 4)), bf16),
        ],
        in_specs=[vmem_spec()] * 14,
        out_specs=[vmem_spec()] * 5,
        scratch_shapes=[pltpu.VMEM((rows, 2 * c), bf16), pltpu.VMEM((rows, c), bf16)],
        compiler_params=params(),
        cost_estimate=cost(2 * rows * d * 4 * d),
    )(acc, dn, dz_acc, zd_acc, h, n2, dy, y, zout, sel2, gain2, b_down, a_gu, b_out)


def back_call(dhb, dzo, mix, cv, zin, n1, sel2, m1, m2, taps, a_out, b_in, w_out):
    rows, d = dhb.shape
    c = zin.shape[1]
    blocks = d // BN
    dps = lax.axis_size("dp")

    def kernel(dhb, dzo, mix_ref, cv_ref, zin_ref, n1_ref, sel_ref, m1_ref, m2_ref, taps_ref, a_out_ref,
               b_in_ref, w_out_ref, dp_ref, dzi_ref, gi_ref):
        sel_f = sel_ref[...].astype(f32)
        m1 = m1_ref[...]
        m2 = m2_ref[...]

        def conv(j):
            dyc = nt(dhb[...], w_out_ref[col(j), :]) + nt(dzo[...], a_out_ref[col(j), :])
            dp_ref[:, col(blocks + j)] = (dyc * cv_ref[:, col(j)].astype(f32)).astype(bf16)
            dcv = dyc * mix_ref[:, col(blocks + j)].astype(f32)
            dbx = (
                taps_ref[2:3, col(j)] * dcv
                + taps_ref[1:2, col(j)] * pltpu.roll(dcv * m1, rows - 1, 0)
                + taps_ref[0:1, col(j)] * pltpu.roll(dcv * m2, rows - 2, 0)
            )
            dp_ref[:, col(j)] = (dbx * mix_ref[:, col(2 * blocks + j)].astype(f32)).astype(bf16)
            dp_ref[:, col(2 * blocks + j)] = (dbx * mix_ref[:, col(j)].astype(f32)).astype(bf16)

        loop(blocks, conv)
        dzi_ref[...] = (nt(dp_ref[...], b_in_ref[...]) * sel_f).astype(bf16)
        spread(gi_ref, 0, nn(zin_ref[...].T, dp_ref[...]))
        spread(gi_ref, 3 * (d // 4), nn(dzi_ref[...].T, n1_ref[...]))

    return pl.pallas_call(
        kernel,
        name="back",
        out_shape=[
            sds((rows, 3 * d), bf16), sds((rows, c), bf16), sds((dps, 4, c // dps, d), bf16),
        ],
        in_specs=[vmem_spec()] * 13,
        out_specs=[vmem_spec()] * 3,
        compiler_params=params(),
        cost_estimate=cost(2 * rows * d * 4 * d),
    )(dhb, dzo, mix, cv, zin, n1, sel2, m1, m2, taps, a_out, b_in, w_out)


def last_call(dp, dzi, dh, x, gain1, a_in, w_in):
    rows, d = x.shape

    def kernel(dp_ref, dzi_ref, dh_ref, x_ref, g1_ref, a_in_ref, w_in_ref, out_ref, dn_ref):
        def dns(j):
            dn_ref[:, col(j)] = nt(dp_ref[...], w_in_ref[col(j), :]) + nt(dzi_ref[...], a_in_ref[col(j), :])

        loop(d // BN, dns)
        g1 = g1_ref[...]

        def norm1(i):
            v = dh_ref[row(i), :] + norm_back_rows(x_ref[row(i), :].astype(f32), g1, dn_ref[row(i), :])
            out_ref[row(i), :] = v.astype(bf16)

        loop(rows // ROWS, norm1)

    return pl.pallas_call(
        kernel,
        name="last",
        out_shape=sds((rows, d), bf16),
        in_specs=[vmem_spec()] * 7,
        out_specs=vmem_spec(),
        scratch_shapes=[pltpu.VMEM((rows, d), f32)],
        compiler_params=params(),
        cost_estimate=cost(2 * rows * d * 4 * d),
    )(dp, dzi, dh, x, gain1, a_in, w_in)


def core_copies(arrays):
    return [swap_dp(a, CORE_BIT) for a in arrays]


def near(zs):
    return [swap_dp(zs, X_BIT), swap_dp(zs, Y_BIT), swap_dp(zs, X_BIT | Y_BIT)]


def spread_over_dp(values):
    s = lax.axis_index("dp")
    values = values[None]
    bit = 1
    while bit < lax.axis_size("dp"):
        other = swap_dp(values, bit)
        mine_first = jnp.concatenate([values, other], axis=0)
        other_first = jnp.concatenate([other, values], axis=0)
        values = jnp.where((s & bit) == 0, mine_first, other_first)
        bit *= 2
    return values


def total(values):
    return jnp.sum(values.astype(f32), axis=0).astype(bf16)


def exchange(values, axis):
    flat = values.reshape(values.shape[0], -1, values.shape[-1])
    return lax.all_to_all(flat, axis, split_axis=0, concat_axis=0, tiled=True).reshape(values.shape)


def send_to_groups(values):
    groups, z = lax.axis_size("group"), lax.axis_index("group")
    out = []
    for t in range(1, groups):
        piece = lax.dynamic_index_in_dim(values, (z + t) % groups, 0, keepdims=False)
        out.append(lax.ppermute(piece, "group", [(i, (i + t) % groups) for i in range(groups)]))
    return [*out, lax.dynamic_index_in_dim(values, z, 0, keepdims=False)]


def add_up(parts):
    whole = parts[0].astype(f32)
    for p in parts[1:]:
        whole = whole + p.astype(f32)
    return whole.astype(bf16)


def local_pieces(
    tokens, cotangent, order, lengths, adapter_ids, norm_gain, ffn_gain, conv_weight,
    in_weight, out_weight, gate_weight, up_weight, down_weight,
    a_in, b_in, a_out, b_out, a_gate, b_gate, a_up, b_up, a_down, b_down,
):
    dp_count = lax.axis_size("dp")
    s = lax.axis_index("dp")
    z = lax.axis_index("group")
    ids = jnp.stack([s, z]).astype(jnp.int32)
    rows, d = tokens.shape
    order_row = order[0]
    counting = jnp.arange(dp_count, dtype=jnp.int32)
    inverse_row = jnp.sum(
        jnp.where(order_row[None, :] == counting[:, None], counting[None, :], 0), axis=1
    )
    pr = d // dp_count
    quarter = gate_weight.shape[1]
    width = quarter // PARTS
    dr = 4 * width // dp_count
    h_d = down_weight.shape[1]

    def rows_of(w):
        return lax.dynamic_slice_in_dim(w, s * pr, pr, 0)

    io_piece = jnp.concatenate([rows_of(in_weight), rows_of(out_weight)], axis=1)
    gate_rows = rows_of(gate_weight)
    up_rows = rows_of(up_weight)
    per = width // dr

    def ffn_piece(j):
        down = lax.dynamic_slice_in_dim(
            down_weight, (s // per) * quarter + j * width + (s % per) * dr, dr, 0
        )
        cols = slice(j * width, (j + 1) * width)
        tail = jnp.concatenate([down[pr:, :128], down[pr:, 128:]], axis=0)
        packed = jnp.concatenate([down[:pr], tail], axis=1)
        return jnp.concatenate([gate_rows[:, cols], up_rows[:, cols], packed], axis=0)

    packed = [ffn_piece(j) for j in range(PARTS)]
    arrived = lax.all_to_all(cotangent, "dp", split_axis=0, concat_axis=0, tiled=True)
    zs_io = from_planes(io_piece)
    near_io = near(zs_io)
    zs = [from_planes(after(packed[0], zs_io))]
    for j in range(1, PARTS):
        zs.append(from_planes(after(packed[j], zs[j - 1])))
    io = [zs_io, *near_io]
    io = io + core_copies(io)
    dy = lax.all_to_all(
        after(regroup(arrived, inverse_row, dp_count), zs_io), "dp", split_axis=0, concat_axis=0, tiled=True
    )

    sel, after_one, after_two = per_token_tables(
        lengths[:, 0, :][s], adapter_ids[:, 0, :][s], rows, a_in.shape[1], ADAPTER_RANK
    )
    sel2 = sel * adapter_scale
    gain1 = norm_gain[None, :]
    gain2 = ffn_gain[None, :]
    a_gu = jnp.concatenate([a_gate, a_up], axis=1)
    nears = near(after(zs[0], dy, *near_io))
    n1, zin, mix, cv, y, zout, h, n2, zgu, w_in, w_out = front_call(
        after(ids, dy, zs[1]), io, in_weight, out_weight, tokens, gain1, gain2, conv_weight,
        sel2, after_one, after_two, a_in, b_in, a_out, b_out, a_gu,
    )
    dzd = (nt(dy, b_down) * sel2.astype(f32)).astype(bf16)
    state = (None, h, None, None)
    previous = n2
    grads = []
    for j in range(PARTS):
        arrays = [zs[j], *[after(v, previous) for v in nears]]
        arrays = arrays + core_copies(arrays)
        if j + 1 < PARTS:
            nears = near(after(zs[j + 1], previous, *arrays[1:4]))
        if j == PARTS - 1:
            early = exchange(after(jnp.concatenate(grads, axis=2), *arrays), "dp")
        *state, g = ffn_call(
            j, after(ids, *zs[j + 1 : j + 3]), arrays, gate_weight, up_weight,
            down_weight, n2, dy, zgu, dzd, b_gate, b_up, a_down, *state,
        )
        previous = state[2]
        grads.append(g)
    late = exchange(grads[-1], "dp")
    early_dp = total(after(early, g))
    early = send_to_groups(early_dp)
    result, dh, dhb, dzo, g_a = middle_call(
        *state, h, n2, dy, y, zout, sel2, after(gain2, early_dp), b_down, a_gu, b_out
    )
    g_a = exchange(g_a, "dp")
    early = add_up([after(early[0], dzo), *early[1:]])
    late_dp = total(after(late, dzo))
    late = send_to_groups(late_dp)
    dp, dzi, g_i = back_call(
        dhb, dzo, mix, cv, zin, n1, sel2, after_one, after_two, after(conv_weight, late_dp, early), a_out, b_in,
        w_out,
    )
    g_i = exchange(g_i, "dp")
    late = add_up([after(late[0], dzi), *late[1:]])
    ffn = jnp.concatenate([early, late], axis=0).astype(f32)
    ga_dp = total(after(g_a, dzi))
    g_a = send_to_groups(ga_dp)
    ffn = lax.all_gather(ffn, "dp")
    input_grad = last_call(dp, dzi, dh, tokens, after(gain1, ga_dp), a_in, w_in)
    g_i = add_up(send_to_groups(total(after(g_i, input_grad))))
    g_a = add_up([after(g_a[0], input_grad), *g_a[1:]])
    small = spread_over_dp(jnp.concatenate([g_a, g_i], axis=1)).astype(f32)
    c = a_in.shape[1]
    ffn = ffn.transpose(1, 0, 2, 3).reshape(PARTS * 3, c, width)

    def joined(k):
        return jnp.concatenate([ffn[3 * j + k] for j in range(PARTS)], axis=1)

    q = d // lax.axis_size("group")
    small = small.reshape(c, -1)
    side, front_grads = small[:, : 5 * q], small[:, 5 * q :]
    cuts = [front_grads[:, : 3 * q], front_grads[:, 3 * q :]] + [side[:, k * q : (k + 1) * q] for k in range(5)]
    g_in_b, g_in_a, g_out_b, g_down_b, g_gate_a, g_up_a, g_out_a = cuts
    return (
        result, input_grad, g_in_a.T, g_in_b, g_out_a.T, g_out_b, g_gate_a.T, joined(0), g_up_a.T, joined(1),
        joined(2).T, g_down_b,
    )


def solution(mesh):
    in_specs = (
        P(("dp", "group"), None),
        P(("dp", "group"), None),
        P("group", None),
        P(None, "group", None),
        P(None, "group", None),
        P(),
        P(),
        P(),
        P(None, "group"),
        P(None, "group"),
        P(None, "group"),
        P(None, "group"),
        P(None, "group"),
        P(),
        P(),
        P(),
        P(),
        P(),
        P(),
        P(),
        P(),
        P(),
        P(),
    )
    out_specs = (
        P(("dp", "group"), None),
        P(("dp", "group"), None),
        P("group", None),
        P(None, "group"),
        P("group", None),
        P(None, "group"),
        P("group", None),
        P(None, "group"),
        P("group", None),
        P(None, "group"),
        P("group", None),
        P(None, "group"),
    )
    small = dict(mesh.shape) == {"dp": 8, "group": 4}
    return jax.shard_map(local_pieces if small else local, mesh=mesh, in_specs=in_specs, out_specs=out_specs, check_vma=False)
```

```python
import jax
import jax.numpy as jnp
from jax import lax
from jax.experimental import pallas as pl
from jax.experimental.pallas import tpu as pltpu
from jax.sharding import PartitionSpec as P

ADAPTER_RANK = 16


eps_norm = 1e-05
adapter_scale = 2.0


def matrix_product(left, right):
    return jnp.dot(left, right, preferred_element_type=jnp.float32)


def transposed_left_matmul(left, right):
    return lax.dot_general(
        left, right, (((0,), (0,)), ((), ())), preferred_element_type=jnp.float32
    )


def transposed_right_matmul(left, right):
    return lax.dot_general(
        left, right, (((1,), (1,)), ((), ())), preferred_element_type=jnp.float32
    )


def per_token_tables(
    sequence_length_row, adapter_index_row, count_of_rows, adapter_column_span, adapter_rank_size
):
    count = sequence_length_row.shape[0]
    earlier = jnp.arange(count)[:, None] <= jnp.arange(count)[None, :]
    finish = jnp.sum(jnp.where(earlier, sequence_length_row[:, None], 0), axis=0)
    starts = finish - sequence_length_row
    counter = jnp.arange(count_of_rows, dtype=jnp.int32)
    member = ((counter[:, None] >= starts[None, :]) & (counter[:, None] < finish[None, :])).astype(
        jnp.int32
    )
    beginning = jnp.sum(member * starts[None, :], axis=1)
    position = counter - beginning
    chosen = jnp.sum(member * adapter_index_row[None, :], axis=1)
    column_span = jnp.arange(adapter_column_span, dtype=jnp.int32) // adapter_rank_size
    select_adapter = (column_span[None, :] == chosen[:, None]).astype(jnp.bfloat16)
    after_one = (position >= 1).astype(jnp.float32)[:, None]
    after_two = (position >= 2).astype(jnp.float32)[:, None]
    return (select_adapter, after_one, after_two)


def delayed(values, amount):
    return jnp.concatenate(
        [jnp.zeros((amount, values.shape[1]), values.dtype), values[:-amount]], axis=0
    )


def advanced(values, amount):
    return jnp.concatenate(
        [values[amount:], jnp.zeros((amount, values.shape[1]), values.dtype)], axis=0
    )


def regroup(values, picks, pieces):
    size = values.shape[0] // pieces
    return jnp.concatenate(
        [lax.dynamic_slice_in_dim(values, picks[i] * size, size, 0) for i in range(pieces)], axis=0
    )


def gather_weight(shard):
    size = shard.shape[0] // lax.axis_size("dp")
    piece = lax.dynamic_slice_in_dim(shard, lax.axis_index("dp") * size, size, 0)
    stacked = lax.all_gather(piece, ("group", "dp"))
    return stacked.reshape(lax.axis_size("group"), shard.shape[0], shard.shape[1])


def wide_product(rows, stacked):
    out = jnp.einsum("rk,gkn->rgn", rows, stacked, preferred_element_type=jnp.float32)
    return out.reshape(rows.shape[0], -1)


def wide_product_back(grads, stacked):
    shaped = grads.reshape(grads.shape[0], stacked.shape[0], stacked.shape[2])
    return jnp.einsum("rgn,gkn->rk", shaped, stacked, preferred_element_type=jnp.float32)


def reduce_grads(terms):
    groups = lax.axis_size("group")
    parts = [t.astype(jnp.bfloat16).reshape(groups, -1, t.shape[1]) for t in terms]
    joined = jnp.concatenate(parts, axis=1)
    flat = joined.reshape(-1, joined.shape[2])
    mine = lax.psum_scatter(flat, ("group", "dp"), scatter_dimension=0, tiled=True)
    share = lax.all_gather(mine, "dp", tiled=True)
    out, at = [], 0
    for p in parts:
        out.append(share[at : at + p.shape[1]].astype(jnp.float32))
        at += p.shape[1]
    return out


def inverse_root(values):
    return lax.rsqrt(jnp.mean(values * values, axis=-1, keepdims=True) + eps_norm)


def norm_back(values, inverse, gain, incoming_gradient):
    scaled = gain * incoming_gradient
    return inverse * scaled - values * (inverse * inverse * inverse) * jnp.mean(
        values * scaled, axis=-1, keepdims=True
    )


def adapter_project(
    input_rows, frozen_weight, adapter_down_factor, adapter_up_factor, select_adapter
):
    reduced_sum = (
        matrix_product(input_rows, adapter_down_factor).astype(jnp.bfloat16) * select_adapter
    )
    return (
        wide_product(input_rows, frozen_weight)
        + adapter_scale * matrix_product(reduced_sum, adapter_up_factor),
        reduced_sum,
    )


def adapter_project_backward(
    incoming_gradient,
    input_rows,
    frozen_weight,
    adapter_down_factor,
    adapter_up_factor,
    reduced_sum,
    select_adapter,
):
    gradient_rank_space = incoming_gradient.astype(jnp.bfloat16)
    gradient_up_factor = adapter_scale * transposed_left_matmul(gradient_rank_space, reduced_sum)
    gradient_reduced_sum = (
        adapter_scale
        * transposed_right_matmul(gradient_rank_space, adapter_up_factor)
        * select_adapter
    ).astype(jnp.bfloat16)
    grad_down = transposed_left_matmul(input_rows, gradient_reduced_sum)
    input_gradients = wide_product_back(
        gradient_rank_space, frozen_weight
    ) + transposed_right_matmul(gradient_reduced_sum, adapter_down_factor)
    return (input_gradients, grad_down, gradient_up_factor)


def local(
    tokens,
    cotangent,
    order,
    lengths,
    adapter_ids,
    norm_gain,
    ffn_gain,
    conv_weight,
    in_weight,
    out_weight,
    gate_weight,
    up_weight,
    down_weight,
    input_first_factor,
    input_second_factor,
    output_first_factor,
    output_second_factor,
    gate_first_factor,
    gate_second_factor,
    up_first_factor,
    up_second_factor,
    down_first_factor,
    down_second_factor,
):
    dp_count = lax.axis_size("dp")
    dp_index = lax.axis_index("dp")
    count_of_rows = tokens.shape[0]
    model_width = tokens.shape[1]
    order_row = order[0]
    counting = jnp.arange(dp_count, dtype=jnp.int32)
    inverse_row = jnp.sum(
        jnp.where(order_row[None, :] == counting[:, None], counting[None, :], 0), axis=1
    )
    arrived = lax.all_to_all(cotangent, "dp", split_axis=0, concat_axis=0, tiled=True)
    cotangent = lax.all_to_all(
        regroup(arrived, inverse_row, dp_count), "dp", split_axis=0, concat_axis=0, tiled=True
    )
    pack_source = dp_index
    hidden_in = tokens
    sequence_length_row = lengths[:, 0, :][pack_source]
    adapter_index_row = adapter_ids[:, 0, :][pack_source]
    select_adapter, after_one, after_two = per_token_tables(
        sequence_length_row,
        adapter_index_row,
        count_of_rows,
        input_first_factor.shape[1],
        ADAPTER_RANK,
    )
    shards = (in_weight, out_weight, gate_weight, up_weight, down_weight)
    full_in, full_out, full_gate, full_up, full_down = [gather_weight(w) for w in shards]
    hidden32 = hidden_in.astype(jnp.float32)
    inverse_one = inverse_root(hidden32)
    normed = (hidden32 * inverse_one * norm_gain).astype(jnp.bfloat16)
    mixed_in, reduced_in = adapter_project(
        normed, full_in, input_first_factor, input_second_factor, select_adapter
    )
    input_gate = mixed_in[:, :model_width]
    output_gate = mixed_in[:, model_width : 2 * model_width]
    conv_input = mixed_in[:, 2 * model_width :]
    gated = input_gate * conv_input
    convolved = (
        conv_weight[2] * gated
        + conv_weight[1] * delayed(gated, 1) * after_one
        + conv_weight[0] * delayed(gated, 2) * after_two
    )
    mixer = (output_gate * convolved).astype(jnp.bfloat16)
    branch, reduced_out = adapter_project(
        mixer, full_out, output_first_factor, output_second_factor, select_adapter
    )
    middle = hidden32 + branch
    inverse_two = inverse_root(middle)
    normed_two = (middle * inverse_two * ffn_gain).astype(jnp.bfloat16)
    gate_pre, reduced_gate = adapter_project(
        normed_two, full_gate, gate_first_factor, gate_second_factor, select_adapter
    )
    up_pre, reduced_up = adapter_project(
        normed_two, full_up, up_first_factor, up_second_factor, select_adapter
    )
    sigmoid_gate = jax.nn.sigmoid(gate_pre)
    activated = (gate_pre * sigmoid_gate * up_pre).astype(jnp.bfloat16)
    ffn_out, reduced_down = adapter_project(
        activated, full_down, down_first_factor, down_second_factor, select_adapter
    )
    result = (middle + ffn_out).astype(jnp.bfloat16)
    back_in, back_out, back_gate, back_up, back_down = full_in, full_out, full_gate, full_up, full_down
    upstream32 = cotangent.astype(jnp.float32)
    grad_act, down_a_grad, down_b_grad = adapter_project_backward(
        upstream32,
        activated,
        back_down,
        down_first_factor,
        down_second_factor,
        reduced_down,
        select_adapter,
    )
    grad_gate_pre = grad_act * up_pre * (sigmoid_gate * (1.0 + gate_pre * (1.0 - sigmoid_gate)))
    grad_up_pre = grad_act * gate_pre * sigmoid_gate
    grad_from_gate, gate_a_grad, gate_b_grad = adapter_project_backward(
        grad_gate_pre,
        normed_two,
        back_gate,
        gate_first_factor,
        gate_second_factor,
        reduced_gate,
        select_adapter,
    )
    grad_from_up, up_a_grad, up_b_grad = adapter_project_backward(
        grad_up_pre,
        normed_two,
        back_up,
        up_first_factor,
        up_second_factor,
        reduced_up,
        select_adapter,
    )
    grad_middle = upstream32 + norm_back(
        middle, inverse_two, ffn_gain, grad_from_gate + grad_from_up
    )
    grad_mixer, out_a_grad, out_b_grad = adapter_project_backward(
        grad_middle,
        mixer,
        back_out,
        output_first_factor,
        output_second_factor,
        reduced_out,
        select_adapter,
    )
    grad_output_gate = grad_mixer * convolved
    grad_conv = grad_mixer * output_gate
    grad_gated = (
        conv_weight[2] * grad_conv
        + conv_weight[1] * advanced(grad_conv * after_one, 1)
        + conv_weight[0] * advanced(grad_conv * after_two, 2)
    )
    grad_mixed = jnp.concatenate(
        [grad_gated * conv_input, grad_output_gate, grad_gated * input_gate], axis=1
    )
    grad_normed, in_a_grad, in_b_grad = adapter_project_backward(
        grad_mixed,
        normed,
        back_in,
        input_first_factor,
        input_second_factor,
        reduced_in,
        select_adapter,
    )
    grad_input = (grad_middle + norm_back(hidden32, inverse_one, norm_gain, grad_normed)).astype(
        jnp.bfloat16
    )
    early = reduce_grads(
        [down_a_grad, down_b_grad, gate_a_grad, gate_b_grad, up_a_grad, up_b_grad, out_a_grad, out_b_grad]
    )
    late = reduce_grads([in_a_grad, in_b_grad])
    totals = (
        late[0], late[1].T, early[6], early[7].T, early[2], early[3].T, early[4], early[5].T,
        early[0], early[1].T,
    )
    return (
        result,
        grad_input,
        totals[0],
        totals[1],
        totals[2],
        totals[3],
        totals[4],
        totals[5],
        totals[6],
        totals[7],
        totals[8],
        totals[9],
    )


f32 = jnp.float32
bf16 = jnp.bfloat16
VMEM_BYTES = 60 * 2**20
PARTS = 3
X_BIT, Y_BIT, CORE_BIT = 2, 4, 1


def nn(a, b):
    return lax.dot_general(a, b, (((1,), (0,)), ((), ())), preferred_element_type=f32)


def nt(a, b):
    return lax.dot_general(a, b, (((1,), (1,)), ((), ())), preferred_element_type=f32)


def swap_dp(values, bit):
    return lax.ppermute(values, "dp", [(i, i ^ bit) for i in range(lax.axis_size("dp"))])


def stacked(parts, start, width):
    size = parts[0].shape[0]

    def kernel(*refs):
        out_ref, sems = refs[-2], refs[-1]
        copies = [
            pltpu.make_async_copy(
                refs[k].at[:, start : start + width], out_ref.at[k * size : (k + 1) * size], sems.at[k]
            )
            for k in range(len(parts))
        ]
        for copy in copies:
            copy.start()
        for copy in copies:
            copy.wait()

    return pl.pallas_call(
        kernel,
        name="stacked",
        out_shape=jax.ShapeDtypeStruct((len(parts) * size, width), parts[0].dtype),
        in_specs=[any_spec()] * len(parts),
        out_specs=vmem_spec(),
        scratch_shapes=[pltpu.SemaphoreType.DMA((len(parts),))],
        compiler_params=pltpu.CompilerParams(vmem_limit_bytes=4 * 2**20),
    )(*parts)


def others(ids, values):
    groups, size, width = values.shape

    def kernel(ids_ref, in_ref, out_ref, sem):
        for t in range(1, groups):
            q = lax.rem(ids_ref[1] + groups - t, groups)
            pltpu.make_async_copy(in_ref.at[q], out_ref.at[(t - 1) * size : t * size], sem).start()
        pltpu.make_async_copy(out_ref, out_ref, sem).wait()

    return pl.pallas_call(
        kernel,
        name="others",
        out_shape=sds(((groups - 1) * size, width), bf16),
        in_specs=[smem_spec(), any_spec()],
        out_specs=vmem_spec(),
        scratch_shapes=[pltpu.SemaphoreType.DMA],
        compiler_params=pltpu.CompilerParams(vmem_limit_bytes=4 * 2**20),
    )(ids, values)


def picked(values, picks, pieces):
    size = values.shape[0] // pieces

    def kernel(picks_ref, in_ref, out_ref, sem):
        for k in range(pieces):
            at = pl.multiple_of(picks_ref[k] * size, size)
            pltpu.make_async_copy(in_ref.at[pl.ds(at, size)], out_ref.at[k * size : (k + 1) * size], sem).start()
        pltpu.make_async_copy(out_ref, out_ref, sem).wait()

    return pl.pallas_call(
        kernel,
        name="picked",
        out_shape=jax.ShapeDtypeStruct(values.shape, values.dtype),
        in_specs=[smem_spec(), any_spec()],
        out_specs=vmem_spec(),
        scratch_shapes=[pltpu.SemaphoreType.DMA],
        compiler_params=pltpu.CompilerParams(vmem_limit_bytes=6 * 2**20),
    )(picks, values)


def totals_by_shift(ids, values):
    terms, groups = values.shape[0], values.shape[1]
    shape = values.shape[2:]

    def kernel(ids_ref, in_ref, *out_refs):
        z = ids_ref[1]
        for t in range(groups):
            q = lax.rem(z + t, groups)
            whole = in_ref[0, q].astype(f32)
            for k in range(1, terms):
                whole = whole + in_ref[k, q].astype(f32)
            out_refs[(t - 1) % groups][...] = whole.astype(bf16)

    return pl.pallas_call(
        kernel,
        name="totals",
        out_shape=[jax.ShapeDtypeStruct(shape, bf16)] * groups,
        in_specs=[smem_spec(), vmem_spec()],
        out_specs=[vmem_spec()] * groups,
        compiler_params=pltpu.CompilerParams(vmem_limit_bytes=8 * 2**20),
    )(ids, values)


def from_planes(joined, widths):
    groups = lax.axis_size("group")
    got = [
        lax.ppermute(joined, "group", [(i, (i + t) % groups) for i in range(groups)])
        for t in range(1, groups)
    ]
    out, at = [], 0
    for width in widths:
        out.append(stacked(got, at, width))
        at += width
    return out


def after(values, *others):
    return lax.optimization_barrier((values, *others))[0]


def piece_table(relay=None):
    both = X_BIT | Y_BIT
    table = [(m, (1, 2, 3)) for m in (0, X_BIT, Y_BIT)]
    if relay is None:
        table.append((both, (1, 2, 3)))
    else:
        table += [(both, tuple(range(1, relay + 1))), (both, tuple(range(relay + 1, 4)))]
    return table + [(m | CORE_BIT, steps) for m, steps in table]


def any_spec():
    return pl.BlockSpec(memory_space=pl.ANY)


def vmem_spec():
    return pl.BlockSpec(memory_space=pltpu.VMEM)


def smem_spec():
    return pl.BlockSpec(memory_space=pltpu.SMEM)


def params(size=VMEM_BYTES):
    return pltpu.CompilerParams(vmem_limit_bytes=size)


def cost(flops):
    return pl.CostEstimate(flops=int(flops) // 4096, transcendentals=0, bytes_accessed=0)


def sds(shape, dtype):
    return jax.ShapeDtypeStruct(shape, dtype)


BN = 256


def col(i):
    return pl.ds(pl.multiple_of(i * BN, BN), BN)


ROWS = 128


def row(i):
    return pl.ds(pl.multiple_of(i * ROWS, ROWS), ROWS)


def loop(n, body):
    def step(i, carry):
        body(i)
        return carry

    lax.fori_loop(0, n, step, 0)


def fetched(pairs, sems):
    copies = [pltpu.make_async_copy(a, b, sems.at[k]) for k, (a, b) in enumerate(pairs)]
    for copy in copies:
        copy.start()
    return [copy.wait for copy in copies]


def put_at(buf, sem, src, r0, c0):
    dst = buf.at[pl.ds(pl.multiple_of(r0, 64), src.shape[0]), pl.ds(pl.multiple_of(c0, 128), src.shape[1])]
    pltpu.make_async_copy(src, dst, sem).start()


def own_pieces(ids, in_shard, out_shard, gate_shard, up_shard, down_shard, dps):
    d = in_shard.shape[0]
    pr = d // dps
    quarter = gate_shard.shape[1]
    width = quarter // PARTS
    dr = 4 * width // dps
    per = width // dr
    h_i, h_o, h_d = in_shard.shape[1], out_shard.shape[1], down_shard.shape[1]
    copies = [1] * (PARTS - 1) + [lax.axis_size("group")]
    shapes = [(pr, h_i + h_o + 3 * width), (pr, 3 * width), (copies[-1] * pr, 3 * width)]

    def kernel(ids_ref, in_ref, out_ref, gate_ref, up_ref, down_ref, *rest):
        outs, sems = rest[:-1], rest[-1]
        s = ids_ref[0]
        mine = pl.ds(pl.multiple_of(s * pr, pr), pr)
        for j in range(PARTS):
            dst = outs[j]
            at = 0

            def put(src, r0=0, n=pr, width_=None):
                for k in range(copies[j]):
                    to = dst.at[k * pr + r0 : k * pr + r0 + n, at : at + width_]
                    pltpu.make_async_copy(src, to, sems.at[j]).start()

            if j == 0:
                put(in_ref.at[mine], width_=h_i)
                at = h_i
                put(out_ref.at[mine], width_=h_o)
                at = h_i + h_o
            cols = pl.ds(j * width, width)
            put(gate_ref.at[mine, cols], width_=width)
            at += width
            put(up_ref.at[mine, cols], width_=width)
            at += width
            top = pl.multiple_of((s // per) * quarter + j * width + (s % per) * dr, 64)
            put(down_ref.at[pl.ds(top, pr)], width_=h_d)
            at += h_d
            half = dr - pr
            put(down_ref.at[pl.ds(top + pr, half), : width - h_d], n=half, width_=width - h_d)
            put(down_ref.at[pl.ds(top + pr, half), width - h_d :], r0=half, n=half, width_=width - h_d)
        for j, dst in enumerate(outs):
            pltpu.make_async_copy(dst, dst, sems.at[j]).wait()

    return pl.pallas_call(
        kernel,
        name="own",
        out_shape=[sds(v, bf16) for v in shapes],
        in_specs=[smem_spec()] + [any_spec()] * 5,
        out_specs=[vmem_spec()] * PARTS,
        scratch_shapes=[pltpu.SemaphoreType.DMA((PARTS,))],
        compiler_params=pltpu.CompilerParams(vmem_limit_bytes=6 * 2**20),
    )(ids, in_shard, out_shard, gate_shard, up_shard, down_shard)


def gather_copies(ids_ref, p_refs, table, pr, buf, sem, shard_ref, lo):
    s, z = ids_ref[0], ids_ref[1]
    n = shard_ref.shape[1]
    put_at(buf, sem, shard_ref, 0, z * n)
    for p_ref, (mask, steps) in zip(p_refs, table):
        for k, t in enumerate(steps):
            put_at(buf, sem, p_ref.at[k * pr : (k + 1) * pr, lo : lo + n], (s ^ mask) * pr, ((z - t) & 3) * n)


def front_call(ids, pieces, relay, in_shard, x, gain1, taps, sel2, m1, m2, a_in, b_in):
    rows, d = x.shape
    table = piece_table(relay)
    n_pieces = len(pieces)
    pr = d // lax.axis_size("dp")
    c = a_in.shape[1]
    blocks = d // BN

    def kernel(*refs):
        ids_ref = refs[0]
        p_refs = refs[1 : 1 + n_pieces]
        (in_ref, x_ref, g1_ref, taps_ref, sel_ref, m1_ref, m2_ref, a_in_ref, b_in_ref) = refs[1 + n_pieces : 10 + n_pieces]
        (n1_out, zin_ref, mix_out, cv_out, y_out, w_out, n1_ref, mix_ref, cv_ref, y_ref, w_in,
         sem_in, sems) = refs[10 + n_pieces :]
        gather_copies(ids_ref, p_refs, table, pr, w_in, sem_in, in_ref, 0)
        g1 = g1_ref[...]

        def norm1(i):
            v = x_ref[row(i), :].astype(f32)
            r = lax.rsqrt(jnp.mean(v * v, axis=-1, keepdims=True) + eps_norm)
            n1_ref[row(i), :] = (v * r * g1).astype(bf16)

        loop(rows // ROWS, norm1)
        zin_ref[...] = nn(n1_ref[...], a_in_ref[...]).astype(bf16) * sel_ref[...]
        pltpu.make_async_copy(w_in, w_in, sem_in).wait()
        stores = fetched([(n1_ref, n1_out), (w_in, w_out)], sems)
        m1 = m1_ref[...]
        m2 = m2_ref[...]

        def mix(j):
            def part(k):
                cc = col(k * blocks + j)
                v = nn(n1_ref[...], w_in[:, cc]) + nn(zin_ref[...], b_in_ref[:, cc])
                mix_ref[:, cc] = v.astype(bf16)
                pltpu.make_async_copy(mix_ref.at[:, cc], mix_out.at[:, cc], sems.at[2]).start()
                return v

            bg = part(0)
            bx = bg * part(2)
            cv = (
                taps_ref[2:3, col(j)] * bx
                + taps_ref[1:2, col(j)] * pltpu.roll(bx, 1, 0) * m1
                + taps_ref[0:1, col(j)] * pltpu.roll(bx, 2, 0) * m2
            )
            cv_ref[:, col(j)] = cv.astype(bf16)
            pltpu.make_async_copy(cv_ref.at[:, col(j)], cv_out.at[:, col(j)], sems.at[3]).start()
            y_ref[:, col(j)] = (part(1) * cv).astype(bf16)
            pltpu.make_async_copy(y_ref.at[:, col(j)], y_out.at[:, col(j)], sems.at[4]).start()

        loop(blocks, mix)
        for wait in stores:
            wait()
        pltpu.make_async_copy(mix_ref, mix_out, sems.at[2]).wait()
        pltpu.make_async_copy(cv_ref, cv_out, sems.at[3]).wait()
        pltpu.make_async_copy(y_ref, y_out, sems.at[4]).wait()

    wide = [(rows, d), (rows, 3 * d), (rows, d), (rows, d), (d, 3 * d)]
    return pl.pallas_call(
        kernel,
        name="front",
        out_shape=[sds(wide[0], bf16), sds((rows, c), bf16)] + [sds(v, bf16) for v in wide[1:]],
        in_specs=[smem_spec()] + [any_spec()] * (n_pieces + 1) + [vmem_spec()] * 8,
        out_specs=[any_spec(), vmem_spec()] + [any_spec()] * 4,
        scratch_shapes=[pltpu.VMEM(v, bf16) for v in wide]
        + [pltpu.SemaphoreType.DMA, pltpu.SemaphoreType.DMA((5,))],
        compiler_params=params(),
        cost_estimate=cost(2.6 * rows * d * 3 * d),
    )(ids, *pieces, in_shard, x, gain1, taps, sel2, m1, m2, a_in, b_in)


def join_call(ids, pieces, relay, out_shard, y, x, gain2, sel2, a_out, b_out, a_gate, a_up):
    rows, d = x.shape
    table = piece_table(relay)
    n_pieces = len(pieces)
    pr = d // lax.axis_size("dp")
    c = a_out.shape[1]
    lo = pieces[0].shape[1] - out_shard.shape[1]

    def kernel(*refs):
        ids_ref = refs[0]
        p_refs = refs[1 : 1 + n_pieces]
        (out_ref, x_hbm, y_ref, g2_ref, sel_ref, a_out_ref, b_out_ref, a_gate_ref, a_up_ref) = refs[
            1 + n_pieces : 10 + n_pieces
        ]
        (zout_ref, hb_ref, n2_ref, zgu_ref, w_out_hbm, x_ref, h_ref, w_out, sem_out, sems) = refs[10 + n_pieces :]
        gather_copies(ids_ref, p_refs, table, pr, w_out, sem_out, out_ref, lo)
        [wait_x] = fetched([(x_hbm, x_ref)], sems)
        sel = sel_ref[...]
        zout_ref[...] = nn(y_ref[...], a_out_ref[...]).astype(bf16) * sel
        wait_x()
        pltpu.make_async_copy(w_out, w_out, sem_out).wait()
        [wait_store] = fetched([(w_out, w_out_hbm)], sems)

        def mid(j):
            o = nn(y_ref[...], w_out[:, col(j)]) + nn(zout_ref[...], b_out_ref[:, col(j)])
            h_ref[:, col(j)] = x_ref[:, col(j)].astype(f32) + o

        loop(d // BN, mid)
        g2 = g2_ref[...]

        def norm2(i):
            v = h_ref[row(i), :]
            hb_ref[row(i), :] = v.astype(bf16)
            r = lax.rsqrt(jnp.mean(v * v, axis=-1, keepdims=True) + eps_norm)
            n2_ref[row(i), :] = (v * r * g2).astype(bf16)

        loop(rows // ROWS, norm2)
        zgu_ref[:, :c] = nn(n2_ref[...], a_gate_ref[...]).astype(bf16) * sel
        zgu_ref[:, c:] = nn(n2_ref[...], a_up_ref[...]).astype(bf16) * sel
        wait_store()

    return pl.pallas_call(
        kernel,
        name="join",
        out_shape=[
            sds((rows, c), bf16), sds((rows, d), bf16), sds((rows, d), bf16), sds((rows, 2 * c), bf16),
            sds((d, d), bf16),
        ],
        in_specs=[smem_spec()] + [any_spec()] * (n_pieces + 2) + [vmem_spec()] * 7,
        out_specs=[vmem_spec()] * 4 + [any_spec()],
        scratch_shapes=[
            pltpu.VMEM((rows, d), bf16), pltpu.VMEM((rows, d), f32), pltpu.VMEM((d, d), bf16),
            pltpu.SemaphoreType.DMA, pltpu.SemaphoreType.DMA((1,)),
        ],
        compiler_params=params(),
        cost_estimate=cost(2.6 * rows * d * d),
    )(ids, *pieces, out_shard, x, y, gain2, sel2, a_out, b_out, a_gate, a_up)


def ffn_call(part, ids, pieces, relay, gate_shard, up_shard, down_shard, n2, dy, zgu, dzd,
             b_gate, b_up, a_down, earlier, *state):
    rows, d = n2.shape
    table = piece_table(relay)
    n_pieces = len(pieces)
    quarter = gate_shard.shape[1]
    width = quarter // PARTS
    fp = 4 * width
    pr = d // lax.axis_size("dp")
    dr = fp // lax.axis_size("dp")
    c = zgu.shape[1] // 2
    h_d = down_shard.shape[1]
    n_state = len(state)
    first = n_state == 1
    joins = earlier is not None
    n_join = int(joins)
    dps = lax.axis_size("dp")
    half_rows = rows // 2

    def kernel(*refs):
        ids_ref = refs[0]
        p_refs = refs[1 : 1 + n_pieces]
        rest = refs[1 + n_pieces :]
        (gs_ref, us_ref, ds_ref, bg_hbm, bu_hbm, ad_hbm, n2_hbm, dy_hbm, zgu_hbm, dzd_hbm) = rest[:10]
        earlier_ref = rest[10] if joins else None
        rest = rest[10 + n_join :]
        state_in = rest[:n_state]
        state_out = rest[n_state : n_state + 4]
        (grads_out, acc_ref, dn_ref, dz_ref, zd_ref, grads_ref, wgu, wd, nzg, nzu, dyz, act, dgu,
         da_all, g_all, sems) = rest[n_state + 4 :]
        state = (acc_ref, dn_ref, dz_ref, zd_ref)
        s = ids_ref[0]
        z = ids_ref[1]
        sem_d, sem_g, sem_y, sem_n, sem_b, sem_o = [sems.at[i] for i in range(6)]
        sem_s = sems.at[6:14]

        def put(buf, sem, src, r0, c0, ra=64):
            dst = buf.at[pl.ds(pl.multiple_of(r0, ra), src.shape[0]), pl.ds(pl.multiple_of(c0, 128), src.shape[1])]
            pltpu.make_async_copy(src, dst, sem).start()

        def pieces_to(fn):
            for p_ref, (mask, steps) in zip(p_refs, table):
                for k, t in enumerate(steps):
                    fn(p_ref, k * pr, s ^ mask, (z - t) & 3)

        put(dyz, sem_y, dy_hbm, 0, 0)
        put(dyz, sem_y, dzd_hbm, 0, d)
        for q in range(4):
            at = pl.ds(q * quarter + part * width, width)
            put(wd, sem_d, ds_ref.at[at, :], q * width, z * h_d)
            put(wd, sem_d, ad_hbm.at[at, :], q * width, d)
        half = dr - pr

        def put_down(p, r, s_, z_):
            at = 2 * width
            put(wd, sem_d, p.at[r : r + pr, at : at + h_d], s_ * dr, z_ * h_d)
            put(wd, sem_d, p.at[r : r + half, at + h_d :], s_ * dr + pr, z_ * h_d)
            put(wd, sem_d, p.at[r + half : r + pr, at + h_d :], s_ * dr + pr, z_ * h_d + width - h_d)

        pieces_to(put_down)
        put(nzg, sem_n, n2_hbm, 0, 0)
        put(nzg, sem_n, zgu_hbm.at[:, :c], 0, d)
        put(nzu, sem_n, n2_hbm, 0, 0)
        put(nzu, sem_n, zgu_hbm.at[:, c:], 0, d)
        mine = pl.ds(part * width, width)
        put(wgu, sem_g, gs_ref.at[:, mine], 0, z * width)
        put(wgu, sem_g, us_ref.at[:, mine], 0, fp + z * width)
        for q in range(4):
            at = pl.ds(q * quarter + part * width, width)
            put(wgu, sem_g, bg_hbm.at[:, at], d, q * width)
            put(wgu, sem_g, bu_hbm.at[:, at], d, fp + q * width)

        def put_up(p, r, s_, z_):
            put(wgu, sem_g, p.at[r : r + pr, :width], s_ * pr, z_ * width)
            put(wgu, sem_g, p.at[r : r + pr, width : 2 * width], s_ * pr, fp + z_ * width)

        pieces_to(put_up)
        if joins:
            load_earlier = pltpu.make_async_copy(earlier_ref, grads_ref.at[:, :, :3], sem_b)
            load_earlier.start()
        loads = [pltpu.make_async_copy(a, b, sem_s.at[k]) for k, (a, b) in enumerate(zip(state_in, state))]
        stores = [pltpu.make_async_copy(a, b, sem_s.at[4 + k]) for k, (a, b) in enumerate(zip(state, state_out))]
        for load in loads:
            load.start()

        pltpu.make_async_copy(dyz, dyz, sem_y).wait()
        dzd_t = dyz[:, d:].T
        pltpu.make_async_copy(wd, wd, sem_d).wait()

        def down(j):
            da_all[:, col(j)] = nt(dyz[...], wd[col(j), :])

        loop(fp // BN, down)
        pltpu.make_async_copy(nzg, nzg, sem_n).wait()
        pltpu.make_async_copy(nzu, nzu, sem_n).wait()
        pltpu.make_async_copy(wgu, wgu, sem_g).wait()
        zg_t = nzg[:, d:].T
        zu_t = nzu[:, d:].T
        blocks = fp // BN

        def up_col(j):
            return pl.ds(pl.multiple_of(fp + j * BN, BN), BN)

        def point(j):
            for i in range(2):
                rr = slice(i * half_rows, (i + 1) * half_rows)
                g = nn(nzg[rr, :], wgu[:, col(j)])
                u = nn(nzu[rr, :], wgu[:, up_col(j)])
                da = da_all[rr, col(j)]
                sg = jax.nn.sigmoid(g)
                gs = g * sg
                act[rr, col(j)] = (gs * u).astype(bf16)
                dgu[rr, up_col(j)] = (da * gs).astype(bf16)
                dgu[rr, col(j)] = (da * u * (sg + gs * (1.0 - sg))).astype(bf16)

        def weight_grads(j):
            g_all[0, :, col(j)] = nn(zg_t, dgu[:, col(j)])
            g_all[1, :, col(j)] = nn(zu_t, dgu[:, up_col(j)])
            g_all[2, :, col(j)] = nn(dzd_t, act[:, col(j)])

        point(0)

        def both(j):
            point(j + 1)
            weight_grads(j)

        loop(blocks - 1, both)
        weight_grads(blocks - 1)
        for k in range(3):
            for q in range(4):
                v = g_all[k, :, q * width : (q + 1) * width]
                grads_ref[:, q, 3 * n_join + k] = v.reshape(dps, c // dps, width).astype(bf16)
        if joins:
            load_earlier.wait()
        store_grads = pltpu.make_async_copy(grads_ref, grads_out, sem_o)
        store_grads.start()
        for load in loads:
            load.wait()
        zd = nn(act[...], wd[:, d:])
        dzg = nt(dgu[:, :fp], wgu[d:, :fp])
        dzu = nt(dgu[:, fp:], wgu[d:, fp:])
        if first:
            dz_ref[:, :c] = dzg
            dz_ref[:, c:] = dzu
            zd_ref[...] = zd
        else:
            dz_ref[:, :c] += dzg
            dz_ref[:, c:] += dzu
            zd_ref[...] += zd
        stores[2].start()
        stores[3].start()

        def out_block(j):
            acc_ref[:, col(j)] = (acc_ref[:, col(j)].astype(f32) + nn(act[...], wd[:, col(j)])).astype(bf16)

        loop(d // BN, out_block)
        stores[0].start()

        def dn_block(j):
            v = nt(dgu[...], wgu[col(j), :])
            dn_ref[:, col(j)] = (v if first else dn_ref[:, col(j)].astype(f32) + v).astype(bf16)

        loop(d // BN, dn_block)
        stores[1].start()
        store_grads.wait()
        for store in stores:
            store.wait()

    state_shapes = [((rows, d), bf16), ((rows, d), bf16), ((rows, 2 * c), f32), ((rows, c), f32)]
    grads_shape = (dps, 4, 3 * (1 + n_join), c // dps, width)
    n_any = n_pieces + 10 + n_join + n_state
    return pl.pallas_call(
        kernel,
        name=f"ffn{part}",
        out_shape=[sds(*v) for v in state_shapes] + [sds(grads_shape, bf16)],
        in_specs=[smem_spec()] + [any_spec()] * n_any,
        out_specs=[any_spec()] * 5,
        scratch_shapes=[pltpu.VMEM(*v) for v in state_shapes] + [
            pltpu.VMEM(grads_shape, bf16),
            pltpu.VMEM((d + c, 2 * fp), bf16), pltpu.VMEM((fp, d + c), bf16),
            pltpu.VMEM((rows, d + c), bf16), pltpu.VMEM((rows, d + c), bf16), pltpu.VMEM((rows, d + c), bf16),
            pltpu.VMEM((rows, fp), bf16), pltpu.VMEM((rows, 2 * fp), bf16), pltpu.VMEM((rows, fp), f32),
            pltpu.VMEM((3, c, fp), f32),
            pltpu.SemaphoreType.DMA((14,)),
        ],
        compiler_params=params(),
        cost_estimate=cost(2.6 * rows * d * 6 * fp),
    )(ids, *pieces, gate_shard, up_shard, down_shard, b_gate, b_up, a_down, n2, dy, zgu, dzd,
      *([earlier] if joins else []), *state)


def norm_back_rows(v, gain, dn):
    r = lax.rsqrt(jnp.mean(v * v, axis=-1, keepdims=True) + eps_norm)
    scaled = gain * dn
    return r * scaled - v * (r * r * r * jnp.mean(v * scaled, axis=-1, keepdims=True))


def spread(ref, at, v):
    dps, c = ref.shape[0], v.shape[0]
    n = v.shape[1] // 4
    for q in range(4):
        ref[:, q, :, at : at + n] = v[:, q * n : (q + 1) * n].reshape(dps, c // dps, n).astype(bf16)


def middle_call(acc, dn, dz_acc, zd_acc, h, n2, dy, y, zout, sel2, gain2, b_down, a_gate, a_up, b_out):
    rows, d = h.shape
    c = zout.shape[1]
    blocks = d // BN
    dps = lax.axis_size("dp")

    def kernel(dn_hbm, n2_hbm, dy_hbm, h_hbm, y_hbm, acc_hbm, dz_in, zd_in, zout_ref, sel_ref, g2_ref,
               b_down_ref, a_gate_ref, a_up_ref, b_out_ref, res_out, dhb_out, dzo, ga_ref,
               dn_ref, n2_ref, dy_ref, h_ref, y_ref, acc_ref, dh_ref, dhb, dzgu, zd, sems):
        wait_dn, wait_n2, wait_dy, wait_h, wait_y, wait_acc = fetched(
            [(dn_hbm, dn_ref), (n2_hbm, n2_ref), (dy_hbm, dy_ref), (h_hbm, h_ref), (y_hbm, y_ref), (acc_hbm, acc_ref)],
            sems,
        )
        sel = sel_ref[...]
        sel_f = sel.astype(f32)
        zd[...] = zd_in[...].astype(bf16) * sel
        dzgu[:, :c] = (dz_in[:, :c] * sel_f).astype(bf16)
        dzgu[:, c:] = (dz_in[:, c:] * sel_f).astype(bf16)
        wait_dn()

        def dns(j):
            v = nt(dzgu[:, :c], a_gate_ref[col(j), :]) + nt(dzgu[:, c:], a_up_ref[col(j), :])
            dh_ref[:, col(j)] = dn_ref[:, col(j)].astype(f32) + v

        loop(blocks, dns)
        wait_n2()
        g = nn(dzgu[...].T, n2_ref[...])
        spread(ga_ref, 2 * (d // 4), g[:c])
        spread(ga_ref, 3 * (d // 4), g[c:])
        wait_dy()
        wait_h()
        g2 = g2_ref[...]

        def norm2(i):
            v = dy_ref[row(i), :].astype(f32) + norm_back_rows(h_ref[row(i), :].astype(f32), g2, dh_ref[row(i), :])
            dhb[row(i), :] = v.astype(bf16)

        loop(rows // ROWS, norm2)
        store_dhb = pltpu.make_async_copy(dhb, dhb_out, sems.at[6])
        store_dhb.start()
        wait_acc()

        def results(j):
            v = acc_ref[:, col(j)].astype(f32) + nn(zd[...], b_down_ref[:, col(j)])
            acc_ref[:, col(j)] = v.astype(bf16)

        loop(blocks, results)
        store_res = pltpu.make_async_copy(acc_ref, res_out, sems.at[7])
        store_res.start()
        spread(ga_ref, d // 4, nn(zd[...].T, dy_ref[...]))
        dzo[...] = (nt(dhb[...], b_out_ref[...]) * sel_f).astype(bf16)
        spread(ga_ref, 0, nn(zout_ref[...].T, dhb[...]))
        wait_y()
        spread(ga_ref, 4 * (d // 4), nn(dzo[...].T, y_ref[...]))
        store_dhb.wait()
        store_res.wait()

    wide = pltpu.VMEM((rows, d), bf16)
    return pl.pallas_call(
        kernel,
        name="middle",
        out_shape=[
            sds((rows, d), bf16), sds((rows, d), bf16), sds((rows, c), bf16),
            sds((dps, 4, c // dps, 5 * (d // 4)), bf16),
        ],
        in_specs=[any_spec()] * 6 + [vmem_spec()] * 9,
        out_specs=[any_spec()] * 2 + [vmem_spec()] * 2,
        scratch_shapes=[
            *[wide] * 6, pltpu.VMEM((rows, d), f32), wide, pltpu.VMEM((rows, 2 * c), bf16),
            pltpu.VMEM((rows, c), bf16), pltpu.SemaphoreType.DMA((8,)),
        ],
        compiler_params=params(),
        cost_estimate=cost(2 * rows * d * 4 * d),
    )(dn, n2, dy, h, y, acc, dz_acc, zd_acc, zout, sel2, gain2, b_down, a_gate, a_up, b_out)


def back_call(dhb, dzo, mix, cv, zin, n1, sel2, m1, m2, taps, a_out, b_in, w_out):
    rows, d = dhb.shape
    c = zin.shape[1]
    blocks = d // BN
    dps = lax.axis_size("dp")

    def kernel(w_out_hbm, dhb_hbm, cv_hbm, mix_hbm, n1_hbm, dzo, zin_ref, sel_ref, m1_ref, m2_ref, taps_ref,
               a_out_ref, b_in_ref, dp_out, dzi_ref, gi_ref, w_out_ref, dhb, cv_ref, mix_ref, n1_ref, dp_ref, sems):
        wait_w, wait_dhb, wait_cv, wait_mix, wait_n1 = fetched(
            [(w_out_hbm, w_out_ref), (dhb_hbm, dhb), (cv_hbm, cv_ref), (mix_hbm, mix_ref), (n1_hbm, n1_ref)], sems
        )
        sel_f = sel_ref[...].astype(f32)
        m1 = m1_ref[...]
        m2 = m2_ref[...]
        wait_w()
        wait_dhb()
        wait_cv()
        wait_mix()

        def conv(j):
            dyc = nt(dhb[...], w_out_ref[col(j), :]) + nt(dzo[...], a_out_ref[col(j), :])
            dp_ref[:, col(blocks + j)] = (dyc * cv_ref[:, col(j)].astype(f32)).astype(bf16)
            dcv = dyc * mix_ref[:, col(blocks + j)].astype(f32)
            dbx = (
                taps_ref[2:3, col(j)] * dcv
                + taps_ref[1:2, col(j)] * pltpu.roll(dcv * m1, rows - 1, 0)
                + taps_ref[0:1, col(j)] * pltpu.roll(dcv * m2, rows - 2, 0)
            )
            dp_ref[:, col(j)] = (dbx * mix_ref[:, col(2 * blocks + j)].astype(f32)).astype(bf16)
            dp_ref[:, col(2 * blocks + j)] = (dbx * mix_ref[:, col(j)].astype(f32)).astype(bf16)

        loop(blocks, conv)
        store = pltpu.make_async_copy(dp_ref, dp_out, sems.at[5])
        store.start()
        dzi_ref[...] = (nt(dp_ref[...], b_in_ref[...]) * sel_f).astype(bf16)
        spread(gi_ref, 0, nn(zin_ref[...].T, dp_ref[...]))
        wait_n1()
        spread(gi_ref, 3 * (d // 4), nn(dzi_ref[...].T, n1_ref[...]))
        store.wait()

    wide, long = pltpu.VMEM((rows, d), bf16), pltpu.VMEM((rows, 3 * d), bf16)
    return pl.pallas_call(
        kernel,
        name="back",
        out_shape=[
            sds((rows, 3 * d), bf16), sds((rows, c), bf16), sds((dps, 4, c // dps, d), bf16),
        ],
        in_specs=[any_spec()] * 5 + [vmem_spec()] * 8,
        out_specs=[any_spec()] + [vmem_spec()] * 2,
        scratch_shapes=[pltpu.VMEM((d, d), bf16), wide, wide, long, wide, long, pltpu.SemaphoreType.DMA((6,))],
        compiler_params=params(),
        cost_estimate=cost(2 * rows * d * 4 * d),
    )(w_out, dhb, cv, mix, n1, dzo, zin, sel2, m1, m2, taps, a_out, b_in)


def last_call(dp, dzi, dh, x, gain1, a_in, w_in):
    rows, d = x.shape
    parts = 4

    def kernel(dp_hbm, w_in_hbm, dh_hbm, x_hbm, dzi_ref, g1_ref, a_in_ref, out_hbm, dp_ref, w_in_ref, dh_ref, x_ref,
               dn_ref, sems):
        n = d // parts
        wait_dp, *wait_w, wait_dh, wait_x = fetched(
            [(dp_hbm, dp_ref)]
            + [(w_in_hbm.at[k * n : (k + 1) * n], w_in_ref.at[k * n : (k + 1) * n]) for k in range(parts)]
            + [(dh_hbm, dh_ref), (x_hbm, x_ref)],
            sems,
        )
        wait_dp()
        for wait in wait_w:
            wait()

        def dns(j):
            dn_ref[:, col(j)] = nt(dp_ref[...], w_in_ref[col(j), :]) + nt(dzi_ref[...], a_in_ref[col(j), :])

        loop(d // BN, dns)
        g1 = g1_ref[...]
        wait_dh()
        wait_x()

        def norm1(i):
            v = dh_ref[row(i), :].astype(f32) + norm_back_rows(x_ref[row(i), :].astype(f32), g1, dn_ref[row(i), :])
            dh_ref[row(i), :] = v.astype(bf16)
            pltpu.make_async_copy(dh_ref.at[row(i)], out_hbm.at[row(i)], sems.at[parts + 3]).start()

        loop(rows // ROWS, norm1)
        pltpu.make_async_copy(dh_ref, out_hbm, sems.at[parts + 3]).wait()

    return pl.pallas_call(
        kernel,
        name="last",
        out_shape=sds((rows, d), bf16),
        in_specs=[any_spec()] * 4 + [vmem_spec()] * 3,
        out_specs=any_spec(),
        scratch_shapes=[
            pltpu.VMEM((rows, 3 * d), bf16), pltpu.VMEM((d, 3 * d), bf16), pltpu.VMEM((rows, d), bf16),
            pltpu.VMEM((rows, d), bf16), pltpu.VMEM((rows, d), f32), pltpu.SemaphoreType.DMA((parts + 4,)),
        ],
        compiler_params=params(),
        cost_estimate=cost(2 * rows * d * 4 * d),
    )(dp, w_in, dh, x, dzi, gain1, a_in)


def core_copies(arrays):
    return [swap_dp(a, CORE_BIT) for a in arrays]


def near(zs):
    return [swap_dp(zs, X_BIT), swap_dp(zs, Y_BIT), swap_dp(zs, X_BIT | Y_BIT)]


def far(xs, ys, relay):
    cut = xs.shape[0] // 3 * relay
    return [swap_dp(xs[:cut], Y_BIT), swap_dp(ys[cut:], X_BIT)]


def near_shares(values):
    return [values, *near(values)]


def all_shares(shares):
    return [*shares, *core_copies(shares)]


def finish_call(ids, shares, layout):
    masks = [m for m, _ in piece_table()]
    n = len(shares)
    r = shares[0].shape[-2]
    c = r * n
    widths = [sum(w for _, _, w in parts) for parts, _ in layout]

    def kernel(*refs):
        ids_ref, ins, outs, bufs = refs[0], refs[1 : 1 + n], refs[1 + n : 1 + n + len(layout)], refs[1 + n + len(layout) :]
        s = ids_ref[0]
        for k, (parts, flip) in enumerate(layout):
            target = bufs[k] if flip else outs[k]
            for share, mask in zip(ins, masks):
                at = pl.ds(pl.multiple_of((s ^ mask) * r, r), r)
                to = 0
                for lead, start, w in parts:
                    v = share[:, start : start + w] if lead is None else share[lead, :, start : start + w]
                    target[at, to : to + w] = v.astype(f32)
                    to += w
            if flip:
                outs[k][...] = bufs[k][...].T

    return pl.pallas_call(
        kernel,
        name="finish",
        out_shape=[sds((w, c) if flip else (c, w), f32) for w, (_, flip) in zip(widths, layout)],
        in_specs=[smem_spec()] + [vmem_spec()] * n,
        out_specs=[vmem_spec()] * len(layout),
        scratch_shapes=[pltpu.VMEM((c, w), f32) for w in widths],
        compiler_params=pltpu.CompilerParams(vmem_limit_bytes=16 * 2**20),
    )(ids, *shares)


def exchange(values, axis):
    flat = values.reshape(values.shape[0], -1, values.shape[-1])
    return lax.all_to_all(flat, axis, split_axis=0, concat_axis=0, tiled=True).reshape(values.shape)


def send_to_groups(sums):
    groups = lax.axis_size("group")
    out = [
        lax.ppermute(sums[t - 1], "group", [(i, (i + t) % groups) for i in range(groups)])
        for t in range(1, groups)
    ]
    return [*out, sums[-1]]


def add_up(parts):
    whole = parts[0].astype(f32)
    for p in parts[1:]:
        whole = whole + p.astype(f32)
    return whole.astype(bf16)


def local_pieces(
    tokens, cotangent, order, lengths, adapter_ids, norm_gain, ffn_gain, conv_weight,
    in_weight, out_weight, gate_weight, up_weight, down_weight,
    a_in, b_in, a_out, b_out, a_gate, b_gate, a_up, b_up, a_down, b_down,
):
    dp_count = lax.axis_size("dp")
    s = lax.axis_index("dp")
    z = lax.axis_index("group")
    ids = jnp.stack([s, z]).astype(jnp.int32)
    rows, d = tokens.shape
    order_row = order[0]
    counting = jnp.arange(dp_count, dtype=jnp.int32)
    inverse_row = jnp.sum(
        jnp.where(order_row[None, :] == counting[:, None], counting[None, :], 0), axis=1
    )
    width = gate_weight.shape[1] // PARTS
    packed = own_pieces(ids, in_weight, out_weight, gate_weight, up_weight, down_weight, dp_count)
    arrived = lax.all_to_all(cotangent, "dp", split_axis=0, concat_axis=0, tiled=True)
    io_width = in_weight.shape[1] + out_weight.shape[1]
    zs_io, *zs = from_planes(packed[0], [io_width, 3 * width])
    near_io = [swap_dp(zs_io, X_BIT), swap_dp(zs_io, Y_BIT)]
    near_io += far(*near_io, 1)
    zs += from_planes(after(packed[1], zs_io), [3 * width])
    io = [zs_io, *near_io]
    io = io + core_copies(io)
    dy = lax.all_to_all(
        picked(arrived, after(inverse_row, packed[0]), dp_count), "dp", split_axis=0, concat_axis=0,
        tiled=True,
    )

    sel, after_one, after_two = per_token_tables(
        lengths[:, 0, :][s], adapter_ids[:, 0, :][s], rows, a_in.shape[1], ADAPTER_RANK
    )
    sel2 = sel * adapter_scale
    gain1 = norm_gain[None, :]
    gain2 = ffn_gain[None, :]
    first = after(zs[0], dy, *near_io)
    nears = [swap_dp(first, X_BIT), swap_dp(first, Y_BIT)]
    n1, zin, mix, cv, y, w_in = front_call(
        after(ids, dy, zs[0]), io, 1, in_weight, tokens, gain1, conv_weight, sel2, after_one, after_two, a_in, b_in,
    )
    nears += far(*[after(v, zin) for v in nears], 2)
    groups = lax.axis_size("group")
    zs.append(others(ids, exchange(after(packed[2], zin).reshape(groups, -1, 3 * width), "group")))
    zout, h, n2, zgu, w_out = join_call(
        ids, io, 1, out_weight, y, tokens, gain2, sel2, a_out, b_out, a_gate, a_up,
    )
    dzd = (nt(dy, b_down) * sel2.astype(f32)).astype(bf16)
    state = (h,)
    previous = n2
    grads = []
    for j in range(PARTS):
        arrays = [zs[j], *[after(v, previous) for v in nears]]
        arrays = arrays + core_copies(arrays)
        if j + 1 < PARTS:
            nears = near(after(zs[j + 1], previous, *nears))
        if j == PARTS - 1:
            early = exchange(after(grads[-1], *arrays), "dp")
        *state, g = ffn_call(
            j, after(ids, *zs[j + 1 : j + 2]), arrays, 2 if j == 0 else None, gate_weight, up_weight,
            down_weight, n2, dy, zgu, dzd, b_gate, b_up, a_down, grads[0] if j == 1 else None, *state,
        )
        previous = state[2]
        grads.append(g)
    late = exchange(grads[-1], "dp")
    early_sums = totals_by_shift(ids, after(early, g))
    early = send_to_groups(early_sums)
    result, dhb, dzo, g_a = middle_call(
        *state, h, n2, dy, y, zout, sel2, after(gain2, early_sums[0]), b_down, a_gate, a_up, b_out
    )
    g_a = exchange(g_a, "dp")
    early = add_up([after(early[0], dzo), *early[1:]])
    late_sums = totals_by_shift(ids, after(late, dzo))
    late = send_to_groups(late_sums)
    dp, dzi, g_i = back_call(
        dhb, dzo, mix, cv, zin, n1, sel2, after_one, after_two, after(conv_weight, late_sums[0], early), a_out,
        b_in, w_out,
    )
    g_i = exchange(g_i, "dp")
    late = add_up([after(late[0], dzi), *late[1:]])
    ffn = near_shares(jnp.concatenate([early, late], axis=0))
    ga_sums = totals_by_shift(ids, after(g_a, dzi))
    g_a = send_to_groups(ga_sums)
    input_grad = last_call(dp, dzi, dhb, tokens, after(gain1, ga_sums[0]), a_in, w_in)
    gi_sums = totals_by_shift(ids, after(g_i, input_grad))
    g_i = send_to_groups(gi_sums)
    g_a = add_up([after(g_a[0], input_grad), *g_a[1:]])
    ffn = all_shares([after(v, input_grad) for v in ffn])
    q = d // lax.axis_size("group")
    layout = [([(3 * j + k, 0, width) for j in range(PARTS)], k == 2) for k in range(3)]
    g_gate_b, g_up_b, g_down_a = finish_call(after(ids, gi_sums[0]), ffn, layout)
    g_i = add_up(g_i)
    small = all_shares(near_shares(jnp.concatenate([g_a, g_i], axis=1)))
    layout = [([(None, k * q, q)], k >= 2) for k in range(5)]
    layout += [([(None, 5 * q, 3 * q)], False), ([(None, 8 * q, q)], True)]
    g_out_b, g_down_b, g_gate_a, g_up_a, g_out_a, g_in_b, g_in_a = finish_call(ids, small, layout)
    return (
        result, input_grad, g_in_a, g_in_b, g_out_a, g_out_b, g_gate_a, g_gate_b, g_up_a, g_up_b, g_down_a,
        g_down_b,
    )


def solution(mesh):
    in_specs = (
        P(("dp", "group"), None),
        P(("dp", "group"), None),
        P("group", None),
        P(None, "group", None),
        P(None, "group", None),
        P(),
        P(),
        P(),
        P(None, "group"),
        P(None, "group"),
        P(None, "group"),
        P(None, "group"),
        P(None, "group"),
        P(),
        P(),
        P(),
        P(),
        P(),
        P(),
        P(),
        P(),
        P(),
        P(),
    )
    out_specs = (
        P(("dp", "group"), None),
        P(("dp", "group"), None),
        P("group", None),
        P(None, "group"),
        P("group", None),
        P(None, "group"),
        P("group", None),
        P(None, "group"),
        P("group", None),
        P(None, "group"),
        P("group", None),
        P(None, "group"),
    )
    small = dict(mesh.shape) == {"dp": 8, "group": 4}
    return jax.shard_map(local_pieces if small else local, mesh=mesh, in_specs=in_specs, out_specs=out_specs, check_vma=False)
```

```python
import jax
import jax.numpy as jnp
from jax import lax
from jax.experimental import pallas as pl
from jax.experimental.pallas import tpu as pltpu
from jax.sharding import PartitionSpec as P

ADAPTER_RANK = 16


eps_norm = 1e-05
adapter_scale = 2.0


def matrix_product(left, right):
    return jnp.dot(left, right, preferred_element_type=jnp.float32)


def transposed_left_matmul(left, right):
    return lax.dot_general(
        left, right, (((0,), (0,)), ((), ())), preferred_element_type=jnp.float32
    )


def transposed_right_matmul(left, right):
    return lax.dot_general(
        left, right, (((1,), (1,)), ((), ())), preferred_element_type=jnp.float32
    )


def per_token_tables(
    sequence_length_row, adapter_index_row, count_of_rows, adapter_column_span, adapter_rank_size
):
    count = sequence_length_row.shape[0]
    earlier = jnp.arange(count)[:, None] <= jnp.arange(count)[None, :]
    finish = jnp.sum(jnp.where(earlier, sequence_length_row[:, None], 0), axis=0)
    starts = finish - sequence_length_row
    counter = jnp.arange(count_of_rows, dtype=jnp.int32)
    member = ((counter[:, None] >= starts[None, :]) & (counter[:, None] < finish[None, :])).astype(
        jnp.int32
    )
    beginning = jnp.sum(member * starts[None, :], axis=1)
    position = counter - beginning
    chosen = jnp.sum(member * adapter_index_row[None, :], axis=1)
    column_span = jnp.arange(adapter_column_span, dtype=jnp.int32) // adapter_rank_size
    select_adapter = (column_span[None, :] == chosen[:, None]).astype(jnp.bfloat16)
    after_one = (position >= 1).astype(jnp.float32)[:, None]
    after_two = (position >= 2).astype(jnp.float32)[:, None]
    return (select_adapter, after_one, after_two)


def delayed(values, amount):
    return jnp.concatenate(
        [jnp.zeros((amount, values.shape[1]), values.dtype), values[:-amount]], axis=0
    )


def advanced(values, amount):
    return jnp.concatenate(
        [values[amount:], jnp.zeros((amount, values.shape[1]), values.dtype)], axis=0
    )


def regroup(values, picks, pieces):
    size = values.shape[0] // pieces
    return jnp.concatenate(
        [lax.dynamic_slice_in_dim(values, picks[i] * size, size, 0) for i in range(pieces)], axis=0
    )


def gather_weight(shard):
    size = shard.shape[0] // lax.axis_size("dp")
    piece = lax.dynamic_slice_in_dim(shard, lax.axis_index("dp") * size, size, 0)
    stacked = lax.all_gather(piece, ("group", "dp"))
    return stacked.reshape(lax.axis_size("group"), shard.shape[0], shard.shape[1])


def wide_product(rows, stacked):
    out = jnp.einsum("rk,gkn->rgn", rows, stacked, preferred_element_type=jnp.float32)
    return out.reshape(rows.shape[0], -1)


def wide_product_back(grads, stacked):
    shaped = grads.reshape(grads.shape[0], stacked.shape[0], stacked.shape[2])
    return jnp.einsum("rgn,gkn->rk", shaped, stacked, preferred_element_type=jnp.float32)


def reduce_grads(terms):
    groups = lax.axis_size("group")
    parts = [t.astype(jnp.bfloat16).reshape(groups, -1, t.shape[1]) for t in terms]
    joined = jnp.concatenate(parts, axis=1)
    flat = joined.reshape(-1, joined.shape[2])
    mine = lax.psum_scatter(flat, ("group", "dp"), scatter_dimension=0, tiled=True)
    share = lax.all_gather(mine, "dp", tiled=True)
    out, at = [], 0
    for p in parts:
        out.append(share[at : at + p.shape[1]].astype(jnp.float32))
        at += p.shape[1]
    return out


def inverse_root(values):
    return lax.rsqrt(jnp.mean(values * values, axis=-1, keepdims=True) + eps_norm)


def norm_back(values, inverse, gain, incoming_gradient):
    scaled = gain * incoming_gradient
    return inverse * scaled - values * (inverse * inverse * inverse) * jnp.mean(
        values * scaled, axis=-1, keepdims=True
    )


def adapter_project(
    input_rows, frozen_weight, adapter_down_factor, adapter_up_factor, select_adapter
):
    reduced_sum = (
        matrix_product(input_rows, adapter_down_factor).astype(jnp.bfloat16) * select_adapter
    )
    return (
        wide_product(input_rows, frozen_weight)
        + adapter_scale * matrix_product(reduced_sum, adapter_up_factor),
        reduced_sum,
    )


def adapter_project_backward(
    incoming_gradient,
    input_rows,
    frozen_weight,
    adapter_down_factor,
    adapter_up_factor,
    reduced_sum,
    select_adapter,
):
    gradient_rank_space = incoming_gradient.astype(jnp.bfloat16)
    gradient_up_factor = adapter_scale * transposed_left_matmul(gradient_rank_space, reduced_sum)
    gradient_reduced_sum = (
        adapter_scale
        * transposed_right_matmul(gradient_rank_space, adapter_up_factor)
        * select_adapter
    ).astype(jnp.bfloat16)
    grad_down = transposed_left_matmul(input_rows, gradient_reduced_sum)
    input_gradients = wide_product_back(
        gradient_rank_space, frozen_weight
    ) + transposed_right_matmul(gradient_reduced_sum, adapter_down_factor)
    return (input_gradients, grad_down, gradient_up_factor)


def local(
    tokens,
    cotangent,
    order,
    lengths,
    adapter_ids,
    norm_gain,
    ffn_gain,
    conv_weight,
    in_weight,
    out_weight,
    gate_weight,
    up_weight,
    down_weight,
    input_first_factor,
    input_second_factor,
    output_first_factor,
    output_second_factor,
    gate_first_factor,
    gate_second_factor,
    up_first_factor,
    up_second_factor,
    down_first_factor,
    down_second_factor,
):
    dp_count = lax.axis_size("dp")
    dp_index = lax.axis_index("dp")
    count_of_rows = tokens.shape[0]
    model_width = tokens.shape[1]
    order_row = order[0]
    counting = jnp.arange(dp_count, dtype=jnp.int32)
    inverse_row = jnp.sum(
        jnp.where(order_row[None, :] == counting[:, None], counting[None, :], 0), axis=1
    )
    arrived = lax.all_to_all(cotangent, "dp", split_axis=0, concat_axis=0, tiled=True)
    cotangent = lax.all_to_all(
        regroup(arrived, inverse_row, dp_count), "dp", split_axis=0, concat_axis=0, tiled=True
    )
    pack_source = dp_index
    hidden_in = tokens
    sequence_length_row = lengths[:, 0, :][pack_source]
    adapter_index_row = adapter_ids[:, 0, :][pack_source]
    select_adapter, after_one, after_two = per_token_tables(
        sequence_length_row,
        adapter_index_row,
        count_of_rows,
        input_first_factor.shape[1],
        ADAPTER_RANK,
    )
    shards = (in_weight, out_weight, gate_weight, up_weight, down_weight)
    full_in, full_out, full_gate, full_up, full_down = [gather_weight(w) for w in shards]
    hidden32 = hidden_in.astype(jnp.float32)
    inverse_one = inverse_root(hidden32)
    normed = (hidden32 * inverse_one * norm_gain).astype(jnp.bfloat16)
    mixed_in, reduced_in = adapter_project(
        normed, full_in, input_first_factor, input_second_factor, select_adapter
    )
    input_gate = mixed_in[:, :model_width]
    output_gate = mixed_in[:, model_width : 2 * model_width]
    conv_input = mixed_in[:, 2 * model_width :]
    gated = input_gate * conv_input
    convolved = (
        conv_weight[2] * gated
        + conv_weight[1] * delayed(gated, 1) * after_one
        + conv_weight[0] * delayed(gated, 2) * after_two
    )
    mixer = (output_gate * convolved).astype(jnp.bfloat16)
    branch, reduced_out = adapter_project(
        mixer, full_out, output_first_factor, output_second_factor, select_adapter
    )
    middle = hidden32 + branch
    inverse_two = inverse_root(middle)
    normed_two = (middle * inverse_two * ffn_gain).astype(jnp.bfloat16)
    gate_pre, reduced_gate = adapter_project(
        normed_two, full_gate, gate_first_factor, gate_second_factor, select_adapter
    )
    up_pre, reduced_up = adapter_project(
        normed_two, full_up, up_first_factor, up_second_factor, select_adapter
    )
    sigmoid_gate = jax.nn.sigmoid(gate_pre)
    activated = (gate_pre * sigmoid_gate * up_pre).astype(jnp.bfloat16)
    ffn_out, reduced_down = adapter_project(
        activated, full_down, down_first_factor, down_second_factor, select_adapter
    )
    result = (middle + ffn_out).astype(jnp.bfloat16)
    back_in, back_out, back_gate, back_up, back_down = full_in, full_out, full_gate, full_up, full_down
    upstream32 = cotangent.astype(jnp.float32)
    grad_act, down_a_grad, down_b_grad = adapter_project_backward(
        upstream32,
        activated,
        back_down,
        down_first_factor,
        down_second_factor,
        reduced_down,
        select_adapter,
    )
    grad_gate_pre = grad_act * up_pre * (sigmoid_gate * (1.0 + gate_pre * (1.0 - sigmoid_gate)))
    grad_up_pre = grad_act * gate_pre * sigmoid_gate
    grad_from_gate, gate_a_grad, gate_b_grad = adapter_project_backward(
        grad_gate_pre,
        normed_two,
        back_gate,
        gate_first_factor,
        gate_second_factor,
        reduced_gate,
        select_adapter,
    )
    grad_from_up, up_a_grad, up_b_grad = adapter_project_backward(
        grad_up_pre,
        normed_two,
        back_up,
        up_first_factor,
        up_second_factor,
        reduced_up,
        select_adapter,
    )
    grad_middle = upstream32 + norm_back(
        middle, inverse_two, ffn_gain, grad_from_gate + grad_from_up
    )
    grad_mixer, out_a_grad, out_b_grad = adapter_project_backward(
        grad_middle,
        mixer,
        back_out,
        output_first_factor,
        output_second_factor,
        reduced_out,
        select_adapter,
    )
    grad_output_gate = grad_mixer * convolved
    grad_conv = grad_mixer * output_gate
    grad_gated = (
        conv_weight[2] * grad_conv
        + conv_weight[1] * advanced(grad_conv * after_one, 1)
        + conv_weight[0] * advanced(grad_conv * after_two, 2)
    )
    grad_mixed = jnp.concatenate(
        [grad_gated * conv_input, grad_output_gate, grad_gated * input_gate], axis=1
    )
    grad_normed, in_a_grad, in_b_grad = adapter_project_backward(
        grad_mixed,
        normed,
        back_in,
        input_first_factor,
        input_second_factor,
        reduced_in,
        select_adapter,
    )
    grad_input = (grad_middle + norm_back(hidden32, inverse_one, norm_gain, grad_normed)).astype(
        jnp.bfloat16
    )
    early = reduce_grads(
        [down_a_grad, down_b_grad, gate_a_grad, gate_b_grad, up_a_grad, up_b_grad, out_a_grad, out_b_grad]
    )
    late = reduce_grads([in_a_grad, in_b_grad])
    totals = (
        late[0], late[1].T, early[6], early[7].T, early[2], early[3].T, early[4], early[5].T,
        early[0], early[1].T,
    )
    return (
        result,
        grad_input,
        totals[0],
        totals[1],
        totals[2],
        totals[3],
        totals[4],
        totals[5],
        totals[6],
        totals[7],
        totals[8],
        totals[9],
    )


f32 = jnp.float32
bf16 = jnp.bfloat16
VMEM_BYTES = 60 * 2**20
PARTS = 3
X_BIT, Y_BIT, CORE_BIT = 2, 4, 1


def nn(a, b):
    return lax.dot_general(a, b, (((1,), (0,)), ((), ())), preferred_element_type=f32)


def nt(a, b):
    return lax.dot_general(a, b, (((1,), (1,)), ((), ())), preferred_element_type=f32)


def swap_dp(values, bit):
    return lax.ppermute(values, "dp", [(i, i ^ bit) for i in range(lax.axis_size("dp"))])


def stacked(parts, start, width):
    size = parts[0].shape[0]

    def kernel(*refs):
        out_ref, sems = refs[-2], refs[-1]
        copies = [
            pltpu.make_async_copy(
                refs[k].at[:, start : start + width], out_ref.at[k * size : (k + 1) * size], sems.at[k]
            )
            for k in range(len(parts))
        ]
        for copy in copies:
            copy.start()
        for copy in copies:
            copy.wait()

    return pl.pallas_call(
        kernel,
        name="stacked",
        out_shape=jax.ShapeDtypeStruct((len(parts) * size, width), parts[0].dtype),
        in_specs=[any_spec()] * len(parts),
        out_specs=vmem_spec(),
        scratch_shapes=[pltpu.SemaphoreType.DMA((len(parts),))],
        compiler_params=pltpu.CompilerParams(vmem_limit_bytes=4 * 2**20),
    )(*parts)


def others(ids, values):
    groups, size, width = values.shape

    def kernel(ids_ref, in_ref, out_ref, sem):
        for t in range(1, groups):
            q = lax.rem(ids_ref[1] + groups - t, groups)
            pltpu.make_async_copy(in_ref.at[q], out_ref.at[(t - 1) * size : t * size], sem).start()
        pltpu.make_async_copy(out_ref, out_ref, sem).wait()

    return pl.pallas_call(
        kernel,
        name="others",
        out_shape=sds(((groups - 1) * size, width), bf16),
        in_specs=[smem_spec(), any_spec()],
        out_specs=vmem_spec(),
        scratch_shapes=[pltpu.SemaphoreType.DMA],
        compiler_params=pltpu.CompilerParams(vmem_limit_bytes=4 * 2**20),
    )(ids, values)


def picked(values, picks, pieces):
    size = values.shape[0] // pieces

    def kernel(picks_ref, in_ref, out_ref, sem):
        for k in range(pieces):
            at = pl.multiple_of(picks_ref[k] * size, size)
            pltpu.make_async_copy(in_ref.at[pl.ds(at, size)], out_ref.at[k * size : (k + 1) * size], sem).start()
        pltpu.make_async_copy(out_ref, out_ref, sem).wait()

    return pl.pallas_call(
        kernel,
        name="picked",
        out_shape=jax.ShapeDtypeStruct(values.shape, values.dtype),
        in_specs=[smem_spec(), any_spec()],
        out_specs=vmem_spec(),
        scratch_shapes=[pltpu.SemaphoreType.DMA],
        compiler_params=pltpu.CompilerParams(vmem_limit_bytes=6 * 2**20),
    )(picks, values)


def totals_by_shift(ids, one, two):
    terms, groups = one.shape[0], one.shape[1]
    shape = list(one.shape[2:])
    along = 0 if len(shape) == 3 else len(shape) - 1
    cut = shape[along]
    shape[along] += two.shape[2 + along]

    def kernel(ids_ref, one_ref, two_ref, *out_refs):
        z = ids_ref[1]
        for t in range(groups):
            q = lax.rem(z + t, groups)
            for in_ref, at in ((one_ref, slice(0, cut)), (two_ref, slice(cut, shape[along]))):
                whole = in_ref[0, q].astype(f32)
                for k in range(1, terms):
                    whole = whole + in_ref[k, q].astype(f32)
                where = (at,) if along == 0 else (slice(None), at)
                out_refs[(t - 1) % groups][where] = whole.astype(bf16)

    return pl.pallas_call(
        kernel,
        name="totals",
        out_shape=[jax.ShapeDtypeStruct(tuple(shape), bf16)] * groups,
        in_specs=[smem_spec(), vmem_spec(), vmem_spec()],
        out_specs=[vmem_spec()] * groups,
        compiler_params=pltpu.CompilerParams(vmem_limit_bytes=16 * 2**20),
    )(ids, one, two)


def from_planes(joined, widths):
    groups = lax.axis_size("group")
    got = [
        lax.ppermute(joined, "group", [(i, (i + t) % groups) for i in range(groups)])
        for t in range(1, groups)
    ]
    out, at = [], 0
    for width in widths:
        out.append(stacked(got, at, width))
        at += width
    return out


def after(values, *others):
    return lax.optimization_barrier((values, *others))[0]


def piece_table(relay=None):
    both = X_BIT | Y_BIT
    table = [(m, (1, 2, 3)) for m in (0, X_BIT, Y_BIT)]
    if relay is None:
        table.append((both, (1, 2, 3)))
    else:
        table += [(both, tuple(range(1, relay + 1))), (both, tuple(range(relay + 1, 4)))]
    return table + [(m | CORE_BIT, steps) for m, steps in table]


def any_spec():
    return pl.BlockSpec(memory_space=pl.ANY)


def hbm_spec():
    return pl.BlockSpec(memory_space=pltpu.HBM)


def vmem_spec():
    return pl.BlockSpec(memory_space=pltpu.VMEM)


def smem_spec():
    return pl.BlockSpec(memory_space=pltpu.SMEM)


def params(size=VMEM_BYTES):
    return pltpu.CompilerParams(vmem_limit_bytes=size)


def cost(flops):
    return pl.CostEstimate(flops=int(flops) // 4096, transcendentals=0, bytes_accessed=0)


def sds(shape, dtype):
    return jax.ShapeDtypeStruct(shape, dtype)


BN = 256


def col(i):
    return pl.ds(pl.multiple_of(i * BN, BN), BN)


ROWS = 128


def row(i):
    return pl.ds(pl.multiple_of(i * ROWS, ROWS), ROWS)


def loop(n, body):
    def step(i, carry):
        body(i)
        return carry

    lax.fori_loop(0, n, step, 0)


def fetched(pairs, sems):
    copies = [pltpu.make_async_copy(a, b, sems.at[k]) for k, (a, b) in enumerate(pairs)]
    for copy in copies:
        copy.start()
    return [copy.wait for copy in copies]


def put_at(buf, sem, src, r0, c0):
    dst = buf.at[pl.ds(pl.multiple_of(r0, 64), src.shape[0]), pl.ds(pl.multiple_of(c0, 128), src.shape[1])]
    pltpu.make_async_copy(src, dst, sem).start()


def own_pieces(ids, in_shard, out_shard, gate_shard, up_shard, down_shard, dps):
    d = in_shard.shape[0]
    pr = d // dps
    quarter = gate_shard.shape[1]
    width = quarter // PARTS
    dr = 4 * width // dps
    per = width // dr
    h_i, h_o, h_d = in_shard.shape[1], out_shard.shape[1], down_shard.shape[1]
    copies = [1] * (PARTS - 1) + [lax.axis_size("group")]
    shapes = [(pr, h_i + h_o + 3 * width), (pr, 3 * width), (copies[-1] * pr, 3 * width)]

    def kernel(ids_ref, in_ref, out_ref, gate_ref, up_ref, down_ref, *rest):
        outs, sems = rest[:-1], rest[-1]
        s = ids_ref[0]
        mine = pl.ds(pl.multiple_of(s * pr, pr), pr)
        for j in range(PARTS):
            dst = outs[j]
            at = 0

            def put(src, r0=0, n=pr, width_=None):
                for k in range(copies[j]):
                    to = dst.at[k * pr + r0 : k * pr + r0 + n, at : at + width_]
                    pltpu.make_async_copy(src, to, sems.at[j]).start()

            if j == 0:
                put(in_ref.at[mine], width_=h_i)
                at = h_i
                put(out_ref.at[mine], width_=h_o)
                at = h_i + h_o
            cols = pl.ds(j * width, width)
            put(gate_ref.at[mine, cols], width_=width)
            at += width
            put(up_ref.at[mine, cols], width_=width)
            at += width
            top = pl.multiple_of((s // per) * quarter + j * width + (s % per) * dr, 64)
            put(down_ref.at[pl.ds(top, pr)], width_=h_d)
            at += h_d
            half = dr - pr
            put(down_ref.at[pl.ds(top + pr, half), : width - h_d], n=half, width_=width - h_d)
            put(down_ref.at[pl.ds(top + pr, half), width - h_d :], r0=half, n=half, width_=width - h_d)
        for j, dst in enumerate(outs):
            pltpu.make_async_copy(dst, dst, sems.at[j]).wait()

    return pl.pallas_call(
        kernel,
        name="own",
        out_shape=[sds(v, bf16) for v in shapes],
        in_specs=[smem_spec()] + [hbm_spec()] * 5,
        out_specs=[vmem_spec()] * PARTS,
        scratch_shapes=[pltpu.SemaphoreType.DMA((PARTS,))],
        compiler_params=pltpu.CompilerParams(vmem_limit_bytes=6 * 2**20),
    )(ids, in_shard, out_shard, gate_shard, up_shard, down_shard)


def gather_copies(ids_ref, p_refs, table, pr, buf, sem, shard_ref, lo):
    s, z = ids_ref[0], ids_ref[1]
    n = shard_ref.shape[1]
    put_at(buf, sem, shard_ref, 0, z * n)
    for p_ref, (mask, steps) in zip(p_refs, table):
        for k, t in enumerate(steps):
            put_at(buf, sem, p_ref.at[k * pr : (k + 1) * pr, lo : lo + n], (s ^ mask) * pr, ((z - t) & 3) * n)


def front_call(ids, pieces, relay, in_shard, x, gain1, taps, sel2, m1, m2, a_in, b_in):
    rows, d = x.shape
    table = piece_table(relay)
    n_pieces = len(pieces)
    pr = d // lax.axis_size("dp")
    c = a_in.shape[1]
    blocks = d // BN

    def kernel(*refs):
        ids_ref = refs[0]
        p_refs = refs[1 : 1 + n_pieces]
        (in_ref, x_ref, g1_ref, taps_ref, sel_ref, m1_ref, m2_ref, a_in_ref, b_in_ref) = refs[1 + n_pieces : 10 + n_pieces]
        (n1_out, zin_ref, mix_out, cv_out, y_out, w_out, n1_ref, mix_ref, cv_ref, y_ref, w_in,
         sem_in, sems) = refs[10 + n_pieces :]
        gather_copies(ids_ref, p_refs, table, pr, w_in, sem_in, in_ref, 0)
        g1 = g1_ref[...]

        def norm1(i):
            v = x_ref[row(i), :].astype(f32)
            r = lax.rsqrt(jnp.mean(v * v, axis=-1, keepdims=True) + eps_norm)
            n1_ref[row(i), :] = (v * r * g1).astype(bf16)

        loop(rows // ROWS, norm1)
        zin_ref[...] = nn(n1_ref[...], a_in_ref[...]).astype(bf16) * sel_ref[...]
        pltpu.make_async_copy(w_in, w_in, sem_in).wait()
        stores = fetched([(n1_ref, n1_out), (w_in, w_out)], sems)
        m1 = m1_ref[...]
        m2 = m2_ref[...]

        def mix(j):
            def part(k):
                cc = col(k * blocks + j)
                v = nn(n1_ref[...], w_in[:, cc]) + nn(zin_ref[...], b_in_ref[:, cc])
                mix_ref[:, cc] = v.astype(bf16)
                pltpu.make_async_copy(mix_ref.at[:, cc], mix_out.at[:, cc], sems.at[2]).start()
                return v

            bg = part(0)
            bx = bg * part(2)
            cv = (
                taps_ref[2:3, col(j)] * bx
                + taps_ref[1:2, col(j)] * pltpu.roll(bx, 1, 0) * m1
                + taps_ref[0:1, col(j)] * pltpu.roll(bx, 2, 0) * m2
            )
            cv_ref[:, col(j)] = cv.astype(bf16)
            pltpu.make_async_copy(cv_ref.at[:, col(j)], cv_out.at[:, col(j)], sems.at[3]).start()
            y_ref[:, col(j)] = (part(1) * cv).astype(bf16)
            pltpu.make_async_copy(y_ref.at[:, col(j)], y_out.at[:, col(j)], sems.at[4]).start()

        loop(blocks, mix)
        for wait in stores:
            wait()
        pltpu.make_async_copy(mix_ref, mix_out, sems.at[2]).wait()
        pltpu.make_async_copy(cv_ref, cv_out, sems.at[3]).wait()
        pltpu.make_async_copy(y_ref, y_out, sems.at[4]).wait()

    wide = [(rows, d), (rows, 3 * d), (rows, d), (rows, d), (d, 3 * d)]
    return pl.pallas_call(
        kernel,
        name="front",
        out_shape=[sds(wide[0], bf16), sds((rows, c), bf16)] + [sds(v, bf16) for v in wide[1:]],
        in_specs=[smem_spec()] + [any_spec()] * (n_pieces + 1) + [vmem_spec()] * 8,
        out_specs=[any_spec(), vmem_spec()] + [any_spec()] * 4,
        scratch_shapes=[pltpu.VMEM(v, bf16) for v in wide]
        + [pltpu.SemaphoreType.DMA, pltpu.SemaphoreType.DMA((5,))],
        compiler_params=params(),
        cost_estimate=cost(2.6 * rows * d * 3 * d),
    )(ids, *pieces, in_shard, x, gain1, taps, sel2, m1, m2, a_in, b_in)


def join_call(ids, pieces, relay, out_shard, y, x, gain2, sel2, a_out, b_out, a_gate, a_up):
    rows, d = x.shape
    table = piece_table(relay)
    n_pieces = len(pieces)
    pr = d // lax.axis_size("dp")
    c = a_out.shape[1]
    lo = pieces[0].shape[1] - out_shard.shape[1]

    def kernel(*refs):
        ids_ref = refs[0]
        p_refs = refs[1 : 1 + n_pieces]
        (out_ref, x_hbm, y_ref, g2_ref, sel_ref, a_out_ref, b_out_ref, a_gate_ref, a_up_ref) = refs[
            1 + n_pieces : 10 + n_pieces
        ]
        (zout_ref, hb_ref, n2_ref, zgu_ref, w_out_hbm, x_ref, h_ref, w_out, sem_out, sems) = refs[10 + n_pieces :]
        gather_copies(ids_ref, p_refs, table, pr, w_out, sem_out, out_ref, lo)
        [wait_x] = fetched([(x_hbm, x_ref)], sems)
        sel = sel_ref[...]
        zout_ref[...] = nn(y_ref[...], a_out_ref[...]).astype(bf16) * sel
        wait_x()
        pltpu.make_async_copy(w_out, w_out, sem_out).wait()
        [wait_store] = fetched([(w_out, w_out_hbm)], sems)

        def mid(j):
            o = nn(y_ref[...], w_out[:, col(j)]) + nn(zout_ref[...], b_out_ref[:, col(j)])
            h_ref[:, col(j)] = x_ref[:, col(j)].astype(f32) + o

        loop(d // BN, mid)
        g2 = g2_ref[...]

        def norm2(i):
            v = h_ref[row(i), :]
            hb_ref[row(i), :] = v.astype(bf16)
            r = lax.rsqrt(jnp.mean(v * v, axis=-1, keepdims=True) + eps_norm)
            n2_ref[row(i), :] = (v * r * g2).astype(bf16)

        loop(rows // ROWS, norm2)
        zgu_ref[:, :c] = nn(n2_ref[...], a_gate_ref[...]).astype(bf16) * sel
        zgu_ref[:, c:] = nn(n2_ref[...], a_up_ref[...]).astype(bf16) * sel
        wait_store()

    return pl.pallas_call(
        kernel,
        name="join",
        out_shape=[
            sds((rows, c), bf16), sds((rows, d), bf16), sds((rows, d), bf16), sds((rows, 2 * c), bf16),
            sds((d, d), bf16),
        ],
        in_specs=[smem_spec()] + [any_spec()] * (n_pieces + 2) + [vmem_spec()] * 7,
        out_specs=[vmem_spec()] * 4 + [any_spec()],
        scratch_shapes=[
            pltpu.VMEM((rows, d), bf16), pltpu.VMEM((rows, d), f32), pltpu.VMEM((d, d), bf16),
            pltpu.SemaphoreType.DMA, pltpu.SemaphoreType.DMA((1,)),
        ],
        compiler_params=params(),
        cost_estimate=cost(2.6 * rows * d * d),
    )(ids, *pieces, out_shard, x, y, gain2, sel2, a_out, b_out, a_gate, a_up)


def ffn_call(part, ids, pieces, relay, gate_shard, up_shard, down_shard, n2, dy, zgu, dzd,
             b_gate, b_up, a_down, earlier, *state):
    rows, d = n2.shape
    table = piece_table(relay)
    n_pieces = len(pieces)
    quarter = gate_shard.shape[1]
    width = quarter // PARTS
    fp = 4 * width
    pr = d // lax.axis_size("dp")
    dr = fp // lax.axis_size("dp")
    c = zgu.shape[1] // 2
    h_d = down_shard.shape[1]
    n_state = len(state)
    first = n_state == 1
    joins = earlier is not None
    n_join = int(joins)
    dps = lax.axis_size("dp")
    half_rows = rows // 2

    def kernel(*refs):
        ids_ref = refs[0]
        p_refs = refs[1 : 1 + n_pieces]
        rest = refs[1 + n_pieces :]
        (gs_ref, us_ref, ds_ref, bg_hbm, bu_hbm, ad_hbm, n2_hbm, dy_hbm, zgu_hbm, dzd_hbm) = rest[:10]
        earlier_ref = rest[10] if joins else None
        rest = rest[10 + n_join :]
        state_in = rest[:n_state]
        state_out = rest[n_state : n_state + 4]
        (grads_out, acc_ref, dn_ref, dz_ref, zd_ref, grads_ref, wgu, wd, nzg, nzu, dyz, act, dgu,
         da_all, g_all, sems) = rest[n_state + 4 :]
        state = (acc_ref, dn_ref, dz_ref, zd_ref)
        s = ids_ref[0]
        z = ids_ref[1]
        sem_d, sem_g, sem_y, sem_n, sem_b, sem_o = [sems.at[i] for i in range(6)]
        sem_s = sems.at[6:14]

        def put(buf, sem, src, r0, c0, ra=64):
            dst = buf.at[pl.ds(pl.multiple_of(r0, ra), src.shape[0]), pl.ds(pl.multiple_of(c0, 128), src.shape[1])]
            pltpu.make_async_copy(src, dst, sem).start()

        def pieces_to(fn):
            for p_ref, (mask, steps) in zip(p_refs, table):
                for k, t in enumerate(steps):
                    fn(p_ref, k * pr, s ^ mask, (z - t) & 3)

        put(dyz, sem_y, dy_hbm, 0, 0)
        put(dyz, sem_y, dzd_hbm, 0, d)
        for q in range(4):
            at = pl.ds(q * quarter + part * width, width)
            put(wd, sem_d, ds_ref.at[at, :], q * width, z * h_d)
            put(wd, sem_d, ad_hbm.at[at, :], q * width, d)
        half = dr - pr

        def put_down(p, r, s_, z_):
            at = 2 * width
            put(wd, sem_d, p.at[r : r + pr, at : at + h_d], s_ * dr, z_ * h_d)
            put(wd, sem_d, p.at[r : r + half, at + h_d :], s_ * dr + pr, z_ * h_d)
            put(wd, sem_d, p.at[r + half : r + pr, at + h_d :], s_ * dr + pr, z_ * h_d + width - h_d)

        pieces_to(put_down)
        put(nzg, sem_n, n2_hbm, 0, 0)
        put(nzg, sem_n, zgu_hbm.at[:, :c], 0, d)
        put(nzu, sem_n, n2_hbm, 0, 0)
        put(nzu, sem_n, zgu_hbm.at[:, c:], 0, d)
        mine = pl.ds(part * width, width)
        put(wgu, sem_g, gs_ref.at[:, mine], 0, z * width)
        put(wgu, sem_g, us_ref.at[:, mine], 0, fp + z * width)
        for q in range(4):
            at = pl.ds(q * quarter + part * width, width)
            put(wgu, sem_g, bg_hbm.at[:, at], d, q * width)
            put(wgu, sem_g, bu_hbm.at[:, at], d, fp + q * width)

        def put_up(p, r, s_, z_):
            put(wgu, sem_g, p.at[r : r + pr, :width], s_ * pr, z_ * width)
            put(wgu, sem_g, p.at[r : r + pr, width : 2 * width], s_ * pr, fp + z_ * width)

        pieces_to(put_up)
        if joins:
            load_earlier = pltpu.make_async_copy(earlier_ref, grads_ref.at[:, :, :3], sem_b)
            load_earlier.start()
        loads = [pltpu.make_async_copy(a, b, sem_s.at[k]) for k, (a, b) in enumerate(zip(state_in, state))]
        stores = [pltpu.make_async_copy(a, b, sem_s.at[4 + k]) for k, (a, b) in enumerate(zip(state, state_out))]
        for load in loads:
            load.start()

        pltpu.make_async_copy(dyz, dyz, sem_y).wait()
        dzd_t = dyz[:, d:].T
        pltpu.make_async_copy(wd, wd, sem_d).wait()

        def down(j):
            da_all[:, col(j)] = nt(dyz[...], wd[col(j), :])

        loop(fp // BN, down)
        pltpu.make_async_copy(nzg, nzg, sem_n).wait()
        pltpu.make_async_copy(nzu, nzu, sem_n).wait()
        pltpu.make_async_copy(wgu, wgu, sem_g).wait()
        zg_t = nzg[:, d:].T
        zu_t = nzu[:, d:].T
        blocks = fp // BN

        def up_col(j):
            return pl.ds(pl.multiple_of(fp + j * BN, BN), BN)

        def point(j):
            for i in range(2):
                rr = slice(i * half_rows, (i + 1) * half_rows)
                g = nn(nzg[rr, :], wgu[:, col(j)])
                u = nn(nzu[rr, :], wgu[:, up_col(j)])
                da = da_all[rr, col(j)]
                sg = jax.nn.sigmoid(g)
                gs = g * sg
                act[rr, col(j)] = (gs * u).astype(bf16)
                dgu[rr, up_col(j)] = (da * gs).astype(bf16)
                dgu[rr, col(j)] = (da * u * (sg + gs * (1.0 - sg))).astype(bf16)

        def weight_grads(j):
            g_all[0, :, col(j)] = nn(zg_t, dgu[:, col(j)])
            g_all[1, :, col(j)] = nn(zu_t, dgu[:, up_col(j)])
            g_all[2, :, col(j)] = nn(dzd_t, act[:, col(j)])

        point(0)

        def both(j):
            point(j + 1)
            weight_grads(j)

        loop(blocks - 1, both)
        weight_grads(blocks - 1)
        for k in range(3):
            for q in range(4):
                v = g_all[k, :, q * width : (q + 1) * width]
                grads_ref[:, q, 3 * n_join + k] = v.reshape(dps, c // dps, width).astype(bf16)
        if joins:
            load_earlier.wait()
        store_grads = pltpu.make_async_copy(grads_ref, grads_out, sem_o)
        store_grads.start()
        for load in loads:
            load.wait()
        zd = nn(act[...], wd[:, d:])
        dzg = nt(dgu[:, :fp], wgu[d:, :fp])
        dzu = nt(dgu[:, fp:], wgu[d:, fp:])
        if first:
            dz_ref[:, :c] = dzg
            dz_ref[:, c:] = dzu
            zd_ref[...] = zd
        else:
            dz_ref[:, :c] += dzg
            dz_ref[:, c:] += dzu
            zd_ref[...] += zd
        stores[2].start()
        stores[3].start()

        def out_block(j):
            acc_ref[:, col(j)] = (acc_ref[:, col(j)].astype(f32) + nn(act[...], wd[:, col(j)])).astype(bf16)

        loop(d // BN, out_block)
        stores[0].start()

        def dn_block(j):
            v = nt(dgu[...], wgu[col(j), :])
            dn_ref[:, col(j)] = (v if first else dn_ref[:, col(j)].astype(f32) + v).astype(bf16)

        loop(d // BN, dn_block)
        stores[1].start()
        store_grads.wait()
        for store in stores:
            store.wait()

    state_shapes = [((rows, d), bf16), ((rows, d), bf16), ((rows, 2 * c), f32), ((rows, c), f32)]
    grads_shape = (dps, 4, 3 * (1 + n_join), c // dps, width)
    n_any = n_pieces + 10 + n_join + n_state
    return pl.pallas_call(
        kernel,
        name=f"ffn{part}",
        out_shape=[sds(*v) for v in state_shapes] + [sds(grads_shape, bf16)],
        in_specs=[smem_spec()] + [any_spec()] * n_any,
        out_specs=[any_spec()] * 5,
        scratch_shapes=[pltpu.VMEM(*v) for v in state_shapes] + [
            pltpu.VMEM(grads_shape, bf16),
            pltpu.VMEM((d + c, 2 * fp), bf16), pltpu.VMEM((fp, d + c), bf16),
            pltpu.VMEM((rows, d + c), bf16), pltpu.VMEM((rows, d + c), bf16), pltpu.VMEM((rows, d + c), bf16),
            pltpu.VMEM((rows, fp), bf16), pltpu.VMEM((rows, 2 * fp), bf16), pltpu.VMEM((rows, fp), f32),
            pltpu.VMEM((3, c, fp), f32),
            pltpu.SemaphoreType.DMA((14,)),
        ],
        compiler_params=params(),
        cost_estimate=cost(2.6 * rows * d * 6 * fp),
    )(ids, *pieces, gate_shard, up_shard, down_shard, b_gate, b_up, a_down, n2, dy, zgu, dzd,
      *([earlier] if joins else []), *state)


def norm_back_rows(v, gain, dn):
    r = lax.rsqrt(jnp.mean(v * v, axis=-1, keepdims=True) + eps_norm)
    scaled = gain * dn
    return r * scaled - v * (r * r * r * jnp.mean(v * scaled, axis=-1, keepdims=True))


def spread(ref, at, v):
    dps, c = ref.shape[0], v.shape[0]
    n = v.shape[1] // 4
    for q in range(4):
        ref[:, q, :, at : at + n] = v[:, q * n : (q + 1) * n].reshape(dps, c // dps, n).astype(bf16)


def middle_call(acc, dn, dz_acc, zd_acc, h, n2, dy, y, zout, sel2, gain2, b_down, a_gate, a_up, b_out):
    rows, d = h.shape
    c = zout.shape[1]
    blocks = d // BN
    dps = lax.axis_size("dp")

    def kernel(dn_hbm, n2_hbm, dy_hbm, h_hbm, y_hbm, acc_hbm, dz_in, zd_in, zout_ref, sel_ref, g2_ref,
               b_down_ref, a_gate_ref, a_up_ref, b_out_ref, res_out, dhb_out, dzo, ga_ref,
               dn_ref, n2_ref, dy_ref, h_ref, y_ref, acc_ref, dh_ref, dhb, dzgu, zd, sems):
        wait_dn, wait_n2, wait_dy, wait_h, wait_y, wait_acc = fetched(
            [(dn_hbm, dn_ref), (n2_hbm, n2_ref), (dy_hbm, dy_ref), (h_hbm, h_ref), (y_hbm, y_ref), (acc_hbm, acc_ref)],
            sems,
        )
        sel = sel_ref[...]
        sel_f = sel.astype(f32)
        zd[...] = zd_in[...].astype(bf16) * sel
        dzgu[:, :c] = (dz_in[:, :c] * sel_f).astype(bf16)
        dzgu[:, c:] = (dz_in[:, c:] * sel_f).astype(bf16)
        wait_dn()

        def dns(j):
            v = nt(dzgu[:, :c], a_gate_ref[col(j), :]) + nt(dzgu[:, c:], a_up_ref[col(j), :])
            dh_ref[:, col(j)] = dn_ref[:, col(j)].astype(f32) + v

        loop(blocks, dns)
        wait_n2()
        g = nn(dzgu[...].T, n2_ref[...])
        spread(ga_ref, 2 * (d // 4), g[:c])
        spread(ga_ref, 3 * (d // 4), g[c:])
        wait_dy()
        wait_h()
        g2 = g2_ref[...]

        def norm2(i):
            v = dy_ref[row(i), :].astype(f32) + norm_back_rows(h_ref[row(i), :].astype(f32), g2, dh_ref[row(i), :])
            dhb[row(i), :] = v.astype(bf16)

        loop(rows // ROWS, norm2)
        store_dhb = pltpu.make_async_copy(dhb, dhb_out, sems.at[6])
        store_dhb.start()
        wait_acc()

        def results(j):
            v = acc_ref[:, col(j)].astype(f32) + nn(zd[...], b_down_ref[:, col(j)])
            acc_ref[:, col(j)] = v.astype(bf16)

        loop(blocks, results)
        store_res = pltpu.make_async_copy(acc_ref, res_out, sems.at[7])
        store_res.start()
        spread(ga_ref, d // 4, nn(zd[...].T, dy_ref[...]))
        dzo[...] = (nt(dhb[...], b_out_ref[...]) * sel_f).astype(bf16)
        spread(ga_ref, 0, nn(zout_ref[...].T, dhb[...]))
        wait_y()
        spread(ga_ref, 4 * (d // 4), nn(dzo[...].T, y_ref[...]))
        store_dhb.wait()
        store_res.wait()

    wide = pltpu.VMEM((rows, d), bf16)
    return pl.pallas_call(
        kernel,
        name="middle",
        out_shape=[
            sds((rows, d), bf16), sds((rows, d), bf16), sds((rows, c), bf16),
            sds((dps, 4, c // dps, 5 * (d // 4)), bf16),
        ],
        in_specs=[any_spec()] * 6 + [vmem_spec()] * 9,
        out_specs=[any_spec()] * 2 + [vmem_spec()] * 2,
        scratch_shapes=[
            *[wide] * 6, pltpu.VMEM((rows, d), f32), wide, pltpu.VMEM((rows, 2 * c), bf16),
            pltpu.VMEM((rows, c), bf16), pltpu.SemaphoreType.DMA((8,)),
        ],
        compiler_params=params(),
        cost_estimate=cost(2 * rows * d * 4 * d),
    )(dn, n2, dy, h, y, acc, dz_acc, zd_acc, zout, sel2, gain2, b_down, a_gate, a_up, b_out)


def back_call(dhb, dzo, mix, cv, zin, n1, sel2, m1, m2, taps, a_out, b_in, w_out):
    rows, d = dhb.shape
    c = zin.shape[1]
    blocks = d // BN
    dps = lax.axis_size("dp")

    def kernel(w_out_hbm, dhb_hbm, cv_hbm, mix_hbm, n1_hbm, dzo, zin_ref, sel_ref, m1_ref, m2_ref, taps_ref,
               a_out_ref, b_in_ref, dp_out, dzi_ref, gi_ref, w_out_ref, dhb, cv_ref, mix_ref, n1_ref, dp_ref, sems):
        wait_w, wait_dhb, wait_cv, wait_mix, wait_n1 = fetched(
            [(w_out_hbm, w_out_ref), (dhb_hbm, dhb), (cv_hbm, cv_ref), (mix_hbm, mix_ref), (n1_hbm, n1_ref)], sems
        )
        sel_f = sel_ref[...].astype(f32)
        m1 = m1_ref[...]
        m2 = m2_ref[...]
        wait_w()
        wait_dhb()
        wait_cv()
        wait_mix()

        def conv(j):
            dyc = nt(dhb[...], w_out_ref[col(j), :]) + nt(dzo[...], a_out_ref[col(j), :])
            dp_ref[:, col(blocks + j)] = (dyc * cv_ref[:, col(j)].astype(f32)).astype(bf16)
            dcv = dyc * mix_ref[:, col(blocks + j)].astype(f32)
            dbx = (
                taps_ref[2:3, col(j)] * dcv
                + taps_ref[1:2, col(j)] * pltpu.roll(dcv * m1, rows - 1, 0)
                + taps_ref[0:1, col(j)] * pltpu.roll(dcv * m2, rows - 2, 0)
            )
            dp_ref[:, col(j)] = (dbx * mix_ref[:, col(2 * blocks + j)].astype(f32)).astype(bf16)
            dp_ref[:, col(2 * blocks + j)] = (dbx * mix_ref[:, col(j)].astype(f32)).astype(bf16)

        loop(blocks, conv)
        store = pltpu.make_async_copy(dp_ref, dp_out, sems.at[5])
        store.start()
        dzi_ref[...] = (nt(dp_ref[...], b_in_ref[...]) * sel_f).astype(bf16)
        spread(gi_ref, 0, nn(zin_ref[...].T, dp_ref[...]))
        wait_n1()
        spread(gi_ref, 3 * (d // 4), nn(dzi_ref[...].T, n1_ref[...]))
        store.wait()

    wide, long = pltpu.VMEM((rows, d), bf16), pltpu.VMEM((rows, 3 * d), bf16)
    return pl.pallas_call(
        kernel,
        name="back",
        out_shape=[
            sds((rows, 3 * d), bf16), sds((rows, c), bf16), sds((dps, 4, c // dps, d), bf16),
        ],
        in_specs=[any_spec()] * 5 + [vmem_spec()] * 8,
        out_specs=[any_spec()] + [vmem_spec()] * 2,
        scratch_shapes=[pltpu.VMEM((d, d), bf16), wide, wide, long, wide, long, pltpu.SemaphoreType.DMA((6,))],
        compiler_params=params(),
        cost_estimate=cost(2 * rows * d * 4 * d),
    )(w_out, dhb, cv, mix, n1, dzo, zin, sel2, m1, m2, taps, a_out, b_in)


def last_call(dp, dzi, dh, x, gain1, a_in, w_in):
    rows, d = x.shape
    parts = 4

    def kernel(dp_hbm, w_in_hbm, dh_hbm, x_hbm, dzi_ref, g1_ref, a_in_ref, out_hbm, dp_ref, w_in_ref, dh_ref, x_ref,
               dn_ref, sems):
        n = d // parts
        wait_dp, *wait_w, wait_dh, wait_x = fetched(
            [(dp_hbm, dp_ref)]
            + [(w_in_hbm.at[k * n : (k + 1) * n], w_in_ref.at[k * n : (k + 1) * n]) for k in range(parts)]
            + [(dh_hbm, dh_ref), (x_hbm, x_ref)],
            sems,
        )
        wait_dp()
        for wait in wait_w:
            wait()

        def dns(j):
            dn_ref[:, col(j)] = nt(dp_ref[...], w_in_ref[col(j), :]) + nt(dzi_ref[...], a_in_ref[col(j), :])

        loop(d // BN, dns)
        g1 = g1_ref[...]
        wait_dh()
        wait_x()

        def norm1(i):
            v = dh_ref[row(i), :].astype(f32) + norm_back_rows(x_ref[row(i), :].astype(f32), g1, dn_ref[row(i), :])
            dh_ref[row(i), :] = v.astype(bf16)
            pltpu.make_async_copy(dh_ref.at[row(i)], out_hbm.at[row(i)], sems.at[parts + 3]).start()

        loop(rows // ROWS, norm1)
        pltpu.make_async_copy(dh_ref, out_hbm, sems.at[parts + 3]).wait()

    return pl.pallas_call(
        kernel,
        name="last",
        out_shape=sds((rows, d), bf16),
        in_specs=[any_spec()] * 4 + [vmem_spec()] * 3,
        out_specs=any_spec(),
        scratch_shapes=[
            pltpu.VMEM((rows, 3 * d), bf16), pltpu.VMEM((d, 3 * d), bf16), pltpu.VMEM((rows, d), bf16),
            pltpu.VMEM((rows, d), bf16), pltpu.VMEM((rows, d), f32), pltpu.SemaphoreType.DMA((parts + 4,)),
        ],
        compiler_params=params(),
        cost_estimate=cost(2 * rows * d * 4 * d),
    )(dp, w_in, dh, x, dzi, gain1, a_in)


def core_copies(arrays):
    return [swap_dp(a, CORE_BIT) for a in arrays]


def near(zs):
    return [swap_dp(zs, X_BIT), swap_dp(zs, Y_BIT), swap_dp(zs, X_BIT | Y_BIT)]


def far(xs, ys, relay):
    cut = xs.shape[0] // 3 * relay
    return [swap_dp(xs[:cut], Y_BIT), swap_dp(ys[cut:], X_BIT)]


def near_shares(values):
    return [values, *near(values)]


def all_shares(shares):
    return [*shares, *core_copies(shares)]


def finish_call(ids, shares, layout):
    masks = [m for m, _ in piece_table()]
    n = len(shares)
    r = shares[0].shape[-2]
    c = r * n
    widths = [sum(w for _, _, w in parts) for parts, _ in layout]

    def kernel(*refs):
        ids_ref, ins, outs, bufs = refs[0], refs[1 : 1 + n], refs[1 + n : 1 + n + len(layout)], refs[1 + n + len(layout) :]
        s = ids_ref[0]
        for k, (parts, flip) in enumerate(layout):
            target = bufs[k] if flip else outs[k]
            for share, mask in zip(ins, masks):
                at = pl.ds(pl.multiple_of((s ^ mask) * r, r), r)
                to = 0
                for lead, start, w in parts:
                    v = share[:, start : start + w] if lead is None else share[lead, :, start : start + w]
                    target[at, to : to + w] = v.astype(f32)
                    to += w
            if flip:
                outs[k][...] = bufs[k][...].T

    return pl.pallas_call(
        kernel,
        name="finish",
        out_shape=[sds((w, c) if flip else (c, w), f32) for w, (_, flip) in zip(widths, layout)],
        in_specs=[smem_spec()] + [vmem_spec()] * n,
        out_specs=[vmem_spec()] * len(layout),
        scratch_shapes=[pltpu.VMEM((c, w), f32) for w in widths],
        compiler_params=pltpu.CompilerParams(vmem_limit_bytes=16 * 2**20),
    )(ids, *shares)


def exchange(values, axis):
    flat = values.reshape(values.shape[0], -1, values.shape[-1])
    return lax.all_to_all(flat, axis, split_axis=0, concat_axis=0, tiled=True).reshape(values.shape)


def send_to_groups(sums):
    groups = lax.axis_size("group")
    out = [
        lax.ppermute(sums[t - 1], "group", [(i, (i + t) % groups) for i in range(groups)])
        for t in range(1, groups)
    ]
    return [*out, sums[-1]]


def add_up(parts):
    whole = parts[0].astype(f32)
    for p in parts[1:]:
        whole = whole + p.astype(f32)
    return whole.astype(bf16)


def local_pieces(
    tokens, cotangent, order, lengths, adapter_ids, norm_gain, ffn_gain, conv_weight,
    in_weight, out_weight, gate_weight, up_weight, down_weight,
    a_in, b_in, a_out, b_out, a_gate, b_gate, a_up, b_up, a_down, b_down,
):
    dp_count = lax.axis_size("dp")
    s = lax.axis_index("dp")
    z = lax.axis_index("group")
    ids = jnp.stack([s, z]).astype(jnp.int32)
    rows, d = tokens.shape
    order_row = order[0]
    counting = jnp.arange(dp_count, dtype=jnp.int32)
    inverse_row = jnp.sum(
        jnp.where(order_row[None, :] == counting[:, None], counting[None, :], 0), axis=1
    )
    width = gate_weight.shape[1] // PARTS
    sel, after_one, after_two = per_token_tables(
        lengths[:, 0, :][s], adapter_ids[:, 0, :][s], rows, a_in.shape[1], ADAPTER_RANK
    )
    sel2 = sel * adapter_scale
    packed = own_pieces(ids, in_weight, out_weight, gate_weight, up_weight, down_weight, dp_count)
    arrived = lax.all_to_all(cotangent, "dp", split_axis=0, concat_axis=0, tiled=True)
    io_width = in_weight.shape[1] + out_weight.shape[1]
    zs_io, *zs = from_planes(packed[0], [io_width, 3 * width])
    near_io = [swap_dp(zs_io, X_BIT), swap_dp(zs_io, Y_BIT)]
    near_io += far(*near_io, 1)
    zs += from_planes(after(packed[1], zs_io), [3 * width])
    io = [zs_io, *near_io]
    io = io + core_copies(io)
    dy = lax.all_to_all(
        picked(arrived, after(inverse_row, packed[0], sel2, after_one, after_two), dp_count), "dp", split_axis=0, concat_axis=0,
        tiled=True,
    )

    gain1 = norm_gain[None, :]
    gain2 = ffn_gain[None, :]
    first = after(zs[0], dy, *near_io)
    nears = [swap_dp(first, X_BIT), swap_dp(first, Y_BIT)]
    n1, zin, mix, cv, y, w_in = front_call(
        after(ids, dy, zs[0]), io, 1, in_weight, tokens, gain1, conv_weight, sel2, after_one, after_two, a_in, b_in,
    )
    nears += far(*[after(v, zin) for v in nears], 2)
    groups = lax.axis_size("group")
    zs.append(others(ids, exchange(after(packed[2], zin).reshape(groups, -1, 3 * width), "group")))
    zout, h, n2, zgu, w_out = join_call(
        ids, io, 1, out_weight, y, tokens, gain2, sel2, a_out, b_out, a_gate, a_up,
    )
    dzd = (nt(dy, b_down) * sel2.astype(f32)).astype(bf16)
    state = (h,)
    previous = n2
    grads = []
    for j in range(PARTS):
        arrays = [zs[j], *[after(v, previous) for v in nears]]
        arrays = arrays + core_copies(arrays)
        if j + 1 < PARTS:
            nears = near(after(zs[j + 1], previous, *nears))
        if j == PARTS - 1:
            early = exchange(after(grads[-1], *arrays), "dp")
        *state, g = ffn_call(
            j, after(ids, *zs[j + 1 : j + 2]), arrays, 2 if j == 0 else None, gate_weight, up_weight,
            down_weight, n2, dy, zgu, dzd, b_gate, b_up, a_down, grads[0] if j == 1 else None, *state,
        )
        previous = state[2]
        grads.append(g)
    late = exchange(grads[-1], "dp")
    result, dhb, dzo, g_a = middle_call(
        *state, h, n2, dy, y, zout, sel2, after(gain2, early), b_down, a_gate, a_up, b_out
    )
    ffn_sums = totals_by_shift(ids, early, after(late, dzo))
    g_a = exchange(g_a, "dp")
    ffn = send_to_groups(ffn_sums)
    dp, dzi, g_i = back_call(
        dhb, dzo, mix, cv, zin, n1, sel2, after_one, after_two, after(conv_weight, ffn_sums[0]), a_out, b_in, w_out,
    )
    g_i = exchange(g_i, "dp")
    input_grad = last_call(dp, dzi, dhb, tokens, after(gain1, g_a), a_in, w_in)
    sums = totals_by_shift(ids, g_a, after(g_i, input_grad))
    small = send_to_groups(sums)
    ffn = all_shares(near_shares(add_up([after(ffn[0], input_grad, sums[0]), *ffn[1:]])))
    q = d // lax.axis_size("group")
    layout = [([(3 * j + k, 0, width) for j in range(PARTS)], k == 2) for k in range(3)]
    g_gate_b, g_up_b, g_down_a = finish_call(after(ids, sums[0]), ffn, layout)
    small = all_shares(near_shares(add_up(small)))
    layout = [([(None, k * q, q)], k >= 2) for k in range(5)]
    layout += [([(None, 5 * q, 3 * q)], False), ([(None, 8 * q, q)], True)]
    g_out_b, g_down_b, g_gate_a, g_up_a, g_out_a, g_in_b, g_in_a = finish_call(ids, small, layout)
    return (
        result, input_grad, g_in_a, g_in_b, g_out_a, g_out_b, g_gate_a, g_gate_b, g_up_a, g_up_b, g_down_a,
        g_down_b,
    )


def solution(mesh):
    in_specs = (
        P(("dp", "group"), None),
        P(("dp", "group"), None),
        P("group", None),
        P(None, "group", None),
        P(None, "group", None),
        P(),
        P(),
        P(),
        P(None, "group"),
        P(None, "group"),
        P(None, "group"),
        P(None, "group"),
        P(None, "group"),
        P(),
        P(),
        P(),
        P(),
        P(),
        P(),
        P(),
        P(),
        P(),
        P(),
    )
    out_specs = (
        P(("dp", "group"), None),
        P(("dp", "group"), None),
        P("group", None),
        P(None, "group"),
        P("group", None),
        P(None, "group"),
        P("group", None),
        P(None, "group"),
        P("group", None),
        P(None, "group"),
        P("group", None),
        P(None, "group"),
    )
    small = dict(mesh.shape) == {"dp": 8, "group": 4}
    return jax.shard_map(local_pieces if small else local, mesh=mesh, in_specs=in_specs, out_specs=out_specs, check_vma=False)
```

```python
import jax
import jax.numpy as jnp
from jax import lax
from jax.experimental import pallas as pl
from jax.experimental.pallas import tpu as pltpu
from jax.sharding import PartitionSpec as P

ADAPTER_RANK = 16


eps_norm = 1e-05
adapter_scale = 2.0


def matrix_product(left, right):
    return jnp.dot(left, right, preferred_element_type=jnp.float32)


def transposed_left_matmul(left, right):
    return lax.dot_general(
        left, right, (((0,), (0,)), ((), ())), preferred_element_type=jnp.float32
    )


def transposed_right_matmul(left, right):
    return lax.dot_general(
        left, right, (((1,), (1,)), ((), ())), preferred_element_type=jnp.float32
    )


def per_token_tables(
    sequence_length_row, adapter_index_row, count_of_rows, adapter_column_span, adapter_rank_size
):
    count = sequence_length_row.shape[0]
    earlier = jnp.arange(count)[:, None] <= jnp.arange(count)[None, :]
    finish = jnp.sum(jnp.where(earlier, sequence_length_row[:, None], 0), axis=0)
    starts = finish - sequence_length_row
    counter = jnp.arange(count_of_rows, dtype=jnp.int32)
    member = ((counter[:, None] >= starts[None, :]) & (counter[:, None] < finish[None, :])).astype(
        jnp.int32
    )
    beginning = jnp.sum(member * starts[None, :], axis=1)
    position = counter - beginning
    chosen = jnp.sum(member * adapter_index_row[None, :], axis=1)
    column_span = jnp.arange(adapter_column_span, dtype=jnp.int32) // adapter_rank_size
    select_adapter = (column_span[None, :] == chosen[:, None]).astype(jnp.bfloat16)
    after_one = (position >= 1).astype(jnp.float32)[:, None]
    after_two = (position >= 2).astype(jnp.float32)[:, None]
    return (select_adapter, after_one, after_two)


def delayed(values, amount):
    return jnp.concatenate(
        [jnp.zeros((amount, values.shape[1]), values.dtype), values[:-amount]], axis=0
    )


def advanced(values, amount):
    return jnp.concatenate(
        [values[amount:], jnp.zeros((amount, values.shape[1]), values.dtype)], axis=0
    )


def regroup(values, picks, pieces):
    size = values.shape[0] // pieces
    return jnp.concatenate(
        [lax.dynamic_slice_in_dim(values, picks[i] * size, size, 0) for i in range(pieces)], axis=0
    )


def gather_weight(shard):
    size = shard.shape[0] // lax.axis_size("dp")
    piece = lax.dynamic_slice_in_dim(shard, lax.axis_index("dp") * size, size, 0)
    stacked = lax.all_gather(piece, ("group", "dp"))
    return stacked.reshape(lax.axis_size("group"), shard.shape[0], shard.shape[1])


def wide_product(rows, stacked):
    out = jnp.einsum("rk,gkn->rgn", rows, stacked, preferred_element_type=jnp.float32)
    return out.reshape(rows.shape[0], -1)


def wide_product_back(grads, stacked):
    shaped = grads.reshape(grads.shape[0], stacked.shape[0], stacked.shape[2])
    return jnp.einsum("rgn,gkn->rk", shaped, stacked, preferred_element_type=jnp.float32)


def reduce_grads(terms):
    groups = lax.axis_size("group")
    parts = [t.astype(jnp.bfloat16).reshape(groups, -1, t.shape[1]) for t in terms]
    joined = jnp.concatenate(parts, axis=1)
    flat = joined.reshape(-1, joined.shape[2])
    mine = lax.psum_scatter(flat, ("group", "dp"), scatter_dimension=0, tiled=True)
    share = lax.all_gather(mine, "dp", tiled=True)
    out, at = [], 0
    for p in parts:
        out.append(share[at : at + p.shape[1]].astype(jnp.float32))
        at += p.shape[1]
    return out


def inverse_root(values):
    return lax.rsqrt(jnp.mean(values * values, axis=-1, keepdims=True) + eps_norm)


def norm_back(values, inverse, gain, incoming_gradient):
    scaled = gain * incoming_gradient
    return inverse * scaled - values * (inverse * inverse * inverse) * jnp.mean(
        values * scaled, axis=-1, keepdims=True
    )


def adapter_project(
    input_rows, frozen_weight, adapter_down_factor, adapter_up_factor, select_adapter
):
    reduced_sum = (
        matrix_product(input_rows, adapter_down_factor).astype(jnp.bfloat16) * select_adapter
    )
    return (
        wide_product(input_rows, frozen_weight)
        + adapter_scale * matrix_product(reduced_sum, adapter_up_factor),
        reduced_sum,
    )


def adapter_project_backward(
    incoming_gradient,
    input_rows,
    frozen_weight,
    adapter_down_factor,
    adapter_up_factor,
    reduced_sum,
    select_adapter,
):
    gradient_rank_space = incoming_gradient.astype(jnp.bfloat16)
    gradient_up_factor = adapter_scale * transposed_left_matmul(gradient_rank_space, reduced_sum)
    gradient_reduced_sum = (
        adapter_scale
        * transposed_right_matmul(gradient_rank_space, adapter_up_factor)
        * select_adapter
    ).astype(jnp.bfloat16)
    grad_down = transposed_left_matmul(input_rows, gradient_reduced_sum)
    input_gradients = wide_product_back(
        gradient_rank_space, frozen_weight
    ) + transposed_right_matmul(gradient_reduced_sum, adapter_down_factor)
    return (input_gradients, grad_down, gradient_up_factor)


def local(
    tokens,
    cotangent,
    order,
    lengths,
    adapter_ids,
    norm_gain,
    ffn_gain,
    conv_weight,
    in_weight,
    out_weight,
    gate_weight,
    up_weight,
    down_weight,
    input_first_factor,
    input_second_factor,
    output_first_factor,
    output_second_factor,
    gate_first_factor,
    gate_second_factor,
    up_first_factor,
    up_second_factor,
    down_first_factor,
    down_second_factor,
):
    dp_count = lax.axis_size("dp")
    dp_index = lax.axis_index("dp")
    count_of_rows = tokens.shape[0]
    model_width = tokens.shape[1]
    order_row = order[0]
    counting = jnp.arange(dp_count, dtype=jnp.int32)
    inverse_row = jnp.sum(
        jnp.where(order_row[None, :] == counting[:, None], counting[None, :], 0), axis=1
    )
    arrived = lax.all_to_all(cotangent, "dp", split_axis=0, concat_axis=0, tiled=True)
    cotangent = lax.all_to_all(
        regroup(arrived, inverse_row, dp_count), "dp", split_axis=0, concat_axis=0, tiled=True
    )
    pack_source = dp_index
    hidden_in = tokens
    sequence_length_row = lengths[:, 0, :][pack_source]
    adapter_index_row = adapter_ids[:, 0, :][pack_source]
    select_adapter, after_one, after_two = per_token_tables(
        sequence_length_row,
        adapter_index_row,
        count_of_rows,
        input_first_factor.shape[1],
        ADAPTER_RANK,
    )
    shards = (in_weight, out_weight, gate_weight, up_weight, down_weight)
    full_in, full_out, full_gate, full_up, full_down = [gather_weight(w) for w in shards]
    hidden32 = hidden_in.astype(jnp.float32)
    inverse_one = inverse_root(hidden32)
    normed = (hidden32 * inverse_one * norm_gain).astype(jnp.bfloat16)
    mixed_in, reduced_in = adapter_project(
        normed, full_in, input_first_factor, input_second_factor, select_adapter
    )
    input_gate = mixed_in[:, :model_width]
    output_gate = mixed_in[:, model_width : 2 * model_width]
    conv_input = mixed_in[:, 2 * model_width :]
    gated = input_gate * conv_input
    convolved = (
        conv_weight[2] * gated
        + conv_weight[1] * delayed(gated, 1) * after_one
        + conv_weight[0] * delayed(gated, 2) * after_two
    )
    mixer = (output_gate * convolved).astype(jnp.bfloat16)
    branch, reduced_out = adapter_project(
        mixer, full_out, output_first_factor, output_second_factor, select_adapter
    )
    middle = hidden32 + branch
    inverse_two = inverse_root(middle)
    normed_two = (middle * inverse_two * ffn_gain).astype(jnp.bfloat16)
    gate_pre, reduced_gate = adapter_project(
        normed_two, full_gate, gate_first_factor, gate_second_factor, select_adapter
    )
    up_pre, reduced_up = adapter_project(
        normed_two, full_up, up_first_factor, up_second_factor, select_adapter
    )
    sigmoid_gate = jax.nn.sigmoid(gate_pre)
    activated = (gate_pre * sigmoid_gate * up_pre).astype(jnp.bfloat16)
    ffn_out, reduced_down = adapter_project(
        activated, full_down, down_first_factor, down_second_factor, select_adapter
    )
    result = (middle + ffn_out).astype(jnp.bfloat16)
    back_in, back_out, back_gate, back_up, back_down = full_in, full_out, full_gate, full_up, full_down
    upstream32 = cotangent.astype(jnp.float32)
    grad_act, down_a_grad, down_b_grad = adapter_project_backward(
        upstream32,
        activated,
        back_down,
        down_first_factor,
        down_second_factor,
        reduced_down,
        select_adapter,
    )
    grad_gate_pre = grad_act * up_pre * (sigmoid_gate * (1.0 + gate_pre * (1.0 - sigmoid_gate)))
    grad_up_pre = grad_act * gate_pre * sigmoid_gate
    grad_from_gate, gate_a_grad, gate_b_grad = adapter_project_backward(
        grad_gate_pre,
        normed_two,
        back_gate,
        gate_first_factor,
        gate_second_factor,
        reduced_gate,
        select_adapter,
    )
    grad_from_up, up_a_grad, up_b_grad = adapter_project_backward(
        grad_up_pre,
        normed_two,
        back_up,
        up_first_factor,
        up_second_factor,
        reduced_up,
        select_adapter,
    )
    grad_middle = upstream32 + norm_back(
        middle, inverse_two, ffn_gain, grad_from_gate + grad_from_up
    )
    grad_mixer, out_a_grad, out_b_grad = adapter_project_backward(
        grad_middle,
        mixer,
        back_out,
        output_first_factor,
        output_second_factor,
        reduced_out,
        select_adapter,
    )
    grad_output_gate = grad_mixer * convolved
    grad_conv = grad_mixer * output_gate
    grad_gated = (
        conv_weight[2] * grad_conv
        + conv_weight[1] * advanced(grad_conv * after_one, 1)
        + conv_weight[0] * advanced(grad_conv * after_two, 2)
    )
    grad_mixed = jnp.concatenate(
        [grad_gated * conv_input, grad_output_gate, grad_gated * input_gate], axis=1
    )
    grad_normed, in_a_grad, in_b_grad = adapter_project_backward(
        grad_mixed,
        normed,
        back_in,
        input_first_factor,
        input_second_factor,
        reduced_in,
        select_adapter,
    )
    grad_input = (grad_middle + norm_back(hidden32, inverse_one, norm_gain, grad_normed)).astype(
        jnp.bfloat16
    )
    early = reduce_grads(
        [down_a_grad, down_b_grad, gate_a_grad, gate_b_grad, up_a_grad, up_b_grad, out_a_grad, out_b_grad]
    )
    late = reduce_grads([in_a_grad, in_b_grad])
    totals = (
        late[0], late[1].T, early[6], early[7].T, early[2], early[3].T, early[4], early[5].T,
        early[0], early[1].T,
    )
    return (
        result,
        grad_input,
        totals[0],
        totals[1],
        totals[2],
        totals[3],
        totals[4],
        totals[5],
        totals[6],
        totals[7],
        totals[8],
        totals[9],
    )


f32 = jnp.float32
bf16 = jnp.bfloat16
VMEM_BYTES = 60 * 2**20
PARTS = 3
X_BIT, Y_BIT, CORE_BIT = 2, 4, 1


def nn(a, b):
    return lax.dot_general(a, b, (((1,), (0,)), ((), ())), preferred_element_type=f32)


def nt(a, b):
    return lax.dot_general(a, b, (((1,), (1,)), ((), ())), preferred_element_type=f32)


def swap_dp(values, bit):
    return lax.ppermute(values, "dp", [(i, i ^ bit) for i in range(lax.axis_size("dp"))])


def stacked(parts, start, width):
    size = parts[0].shape[0]

    def kernel(*refs):
        out_ref, sems = refs[-2], refs[-1]
        copies = [
            pltpu.make_async_copy(
                refs[k].at[:, start : start + width], out_ref.at[k * size : (k + 1) * size], sems.at[k]
            )
            for k in range(len(parts))
        ]
        for copy in copies:
            copy.start()
        for copy in copies:
            copy.wait()

    return pl.pallas_call(
        kernel,
        name="stacked",
        out_shape=jax.ShapeDtypeStruct((len(parts) * size, width), parts[0].dtype),
        in_specs=[any_spec()] * len(parts),
        out_specs=vmem_spec(),
        scratch_shapes=[pltpu.SemaphoreType.DMA((len(parts),))],
        compiler_params=pltpu.CompilerParams(vmem_limit_bytes=4 * 2**20),
    )(*parts)


def others(ids, values):
    groups, size, width = values.shape

    def kernel(ids_ref, in_ref, out_ref, sem):
        for t in range(1, groups):
            q = lax.rem(ids_ref[1] + groups - t, groups)
            pltpu.make_async_copy(in_ref.at[q], out_ref.at[(t - 1) * size : t * size], sem).start()
        pltpu.make_async_copy(out_ref, out_ref, sem).wait()

    return pl.pallas_call(
        kernel,
        name="others",
        out_shape=sds(((groups - 1) * size, width), bf16),
        in_specs=[smem_spec(), any_spec()],
        out_specs=vmem_spec(),
        scratch_shapes=[pltpu.SemaphoreType.DMA],
        compiler_params=pltpu.CompilerParams(vmem_limit_bytes=4 * 2**20),
    )(ids, values)


def picked(values, picks, pieces):
    size = values.shape[0] // pieces

    def kernel(picks_ref, in_ref, out_ref, sem):
        for k in range(pieces):
            at = pl.multiple_of(picks_ref[k] * size, size)
            pltpu.make_async_copy(in_ref.at[pl.ds(at, size)], out_ref.at[k * size : (k + 1) * size], sem).start()
        pltpu.make_async_copy(out_ref, out_ref, sem).wait()

    return pl.pallas_call(
        kernel,
        name="picked",
        out_shape=jax.ShapeDtypeStruct(values.shape, values.dtype),
        in_specs=[smem_spec(), any_spec()],
        out_specs=vmem_spec(),
        scratch_shapes=[pltpu.SemaphoreType.DMA],
        compiler_params=pltpu.CompilerParams(vmem_limit_bytes=6 * 2**20),
    )(picks, values)


def totals_by_shift(ids, one, two):
    terms, groups = one.shape[0], one.shape[1]
    shape = list(one.shape[2:])
    along = 0 if len(shape) == 3 else len(shape) - 1
    cut = shape[along]
    shape[along] += two.shape[2 + along]

    def kernel(ids_ref, one_ref, two_ref, *out_refs):
        z = ids_ref[1]
        for t in range(groups):
            q = lax.rem(z + t, groups)
            for in_ref, at in ((one_ref, slice(0, cut)), (two_ref, slice(cut, shape[along]))):
                whole = in_ref[0, q].astype(f32)
                for k in range(1, terms):
                    whole = whole + in_ref[k, q].astype(f32)
                where = (at,) if along == 0 else (slice(None), at)
                out_refs[(t - 1) % groups][where] = whole.astype(bf16)

    return pl.pallas_call(
        kernel,
        name="totals",
        out_shape=[jax.ShapeDtypeStruct(tuple(shape), bf16)] * groups,
        in_specs=[smem_spec(), vmem_spec(), vmem_spec()],
        out_specs=[vmem_spec()] * groups,
        compiler_params=pltpu.CompilerParams(vmem_limit_bytes=16 * 2**20),
    )(ids, one, two)


def from_planes(joined, widths):
    groups = lax.axis_size("group")
    got = [
        lax.ppermute(joined, "group", [(i, (i + t) % groups) for i in range(groups)])
        for t in range(1, groups)
    ]
    out, at = [], 0
    for width in widths:
        out.append(stacked(got, at, width))
        at += width
    return out


def after(values, *others):
    return lax.optimization_barrier((values, *others))[0]


def piece_table(relay=None):
    both = X_BIT | Y_BIT
    table = [(m, (1, 2, 3)) for m in (0, X_BIT, Y_BIT)]
    if relay is None:
        table.append((both, (1, 2, 3)))
    else:
        table += [(both, tuple(range(1, relay + 1))), (both, tuple(range(relay + 1, 4)))]
    return table + [(m | CORE_BIT, steps) for m, steps in table]


def any_spec():
    return pl.BlockSpec(memory_space=pl.ANY)


def hbm_spec():
    return pl.BlockSpec(memory_space=pltpu.HBM)


def vmem_spec():
    return pl.BlockSpec(memory_space=pltpu.VMEM)


def smem_spec():
    return pl.BlockSpec(memory_space=pltpu.SMEM)


def params(size=VMEM_BYTES):
    return pltpu.CompilerParams(vmem_limit_bytes=size)


def cost(flops):
    return pl.CostEstimate(flops=int(flops) // 4096, transcendentals=0, bytes_accessed=0)


def sds(shape, dtype):
    return jax.ShapeDtypeStruct(shape, dtype)


BN = 256


def col(i):
    return pl.ds(pl.multiple_of(i * BN, BN), BN)


ROWS = 128


def row(i):
    return pl.ds(pl.multiple_of(i * ROWS, ROWS), ROWS)


def loop(n, body):
    def step(i, carry):
        body(i)
        return carry

    lax.fori_loop(0, n, step, 0)


def fetched(pairs, sems):
    copies = [pltpu.make_async_copy(a, b, sems.at[k]) for k, (a, b) in enumerate(pairs)]
    for copy in copies:
        copy.start()
    return [copy.wait for copy in copies]


def put_at(buf, sem, src, r0, c0):
    dst = buf.at[pl.ds(pl.multiple_of(r0, 64), src.shape[0]), pl.ds(pl.multiple_of(c0, 128), src.shape[1])]
    pltpu.make_async_copy(src, dst, sem).start()


def own_pieces(ids, in_shard, out_shard, gate_shard, up_shard, down_shard, dps, parts):
    d = in_shard.shape[0]
    pr = d // dps
    quarter = gate_shard.shape[1]
    width = quarter // PARTS
    dr = 4 * width // dps
    per = width // dr
    h_i, h_o, h_d = in_shard.shape[1], out_shard.shape[1], down_shard.shape[1]
    copies = [lax.axis_size("group") if j else 1 for j in range(PARTS)]
    shapes = [(copies[j] * pr, 3 * width if j else h_i + h_o + 3 * width) for j in parts]

    def kernel(ids_ref, in_ref, out_ref, gate_ref, up_ref, down_ref, *rest):
        outs, sems = rest[:-1], rest[-1]
        s = ids_ref[0]
        mine = pl.ds(pl.multiple_of(s * pr, pr), pr)
        for j, dst in zip(parts, outs):
            at = 0

            def put(src, r0=0, n=pr, width_=None):
                for k in range(copies[j]):
                    to = dst.at[k * pr + r0 : k * pr + r0 + n, at : at + width_]
                    pltpu.make_async_copy(src, to, sems.at[j]).start()

            if j == 0:
                put(in_ref.at[mine], width_=h_i)
                at = h_i
                put(out_ref.at[mine], width_=h_o)
                at = h_i + h_o
            cols = pl.ds(j * width, width)
            put(gate_ref.at[mine, cols], width_=width)
            at += width
            put(up_ref.at[mine, cols], width_=width)
            at += width
            top = pl.multiple_of((s // per) * quarter + j * width + (s % per) * dr, 64)
            put(down_ref.at[pl.ds(top, pr)], width_=h_d)
            at += h_d
            half = dr - pr
            put(down_ref.at[pl.ds(top + pr, half), : width - h_d], n=half, width_=width - h_d)
            put(down_ref.at[pl.ds(top + pr, half), width - h_d :], r0=half, n=half, width_=width - h_d)
        for j, dst in zip(parts, outs):
            pltpu.make_async_copy(dst, dst, sems.at[j]).wait()

    return pl.pallas_call(
        kernel,
        name="own",
        out_shape=[sds(v, bf16) for v in shapes],
        in_specs=[smem_spec()] + [hbm_spec()] * 5,
        out_specs=[vmem_spec()] * len(parts),
        scratch_shapes=[pltpu.SemaphoreType.DMA((PARTS,))],
        compiler_params=params(),
    )(ids, in_shard, out_shard, gate_shard, up_shard, down_shard)


def gather_copies(ids_ref, p_refs, table, pr, buf, sem, shard_ref, lo):
    s, z = ids_ref[0], ids_ref[1]
    n = shard_ref.shape[1]
    put_at(buf, sem, shard_ref, 0, z * n)
    for p_ref, (mask, steps) in zip(p_refs, table):
        for k, t in enumerate(steps):
            put_at(buf, sem, p_ref.at[k * pr : (k + 1) * pr, lo : lo + n], (s ^ mask) * pr, ((z - t) & 3) * n)


def front_call(ids, pieces, relay, in_shard, x, gain1, taps, sel2, m1, m2, a_in, b_in):
    rows, d = x.shape
    table = piece_table(relay)
    n_pieces = len(pieces)
    pr = d // lax.axis_size("dp")
    c = a_in.shape[1]
    blocks = d // BN

    def kernel(*refs):
        ids_ref = refs[0]
        p_refs = refs[1 : 1 + n_pieces]
        (in_ref, x_ref, g1_ref, taps_ref, sel_ref, m1_ref, m2_ref, a_in_ref, b_in_ref) = refs[1 + n_pieces : 10 + n_pieces]
        (n1_out, zin_ref, mix_out, cv_out, y_out, w_out, n1_ref, mix_ref, cv_ref, y_ref, w_in,
         sem_in, sems) = refs[10 + n_pieces :]
        gather_copies(ids_ref, p_refs, table, pr, w_in, sem_in, in_ref, 0)
        g1 = g1_ref[...]

        def norm1(i):
            v = x_ref[row(i), :].astype(f32)
            r = lax.rsqrt(jnp.mean(v * v, axis=-1, keepdims=True) + eps_norm)
            n1_ref[row(i), :] = (v * r * g1).astype(bf16)

        loop(rows // ROWS, norm1)
        zin_ref[...] = nn(n1_ref[...], a_in_ref[...]).astype(bf16) * sel_ref[...]
        pltpu.make_async_copy(w_in, w_in, sem_in).wait()
        stores = fetched([(n1_ref, n1_out), (w_in, w_out)], sems)
        m1 = m1_ref[...]
        m2 = m2_ref[...]

        def mix(j):
            def part(k):
                cc = col(k * blocks + j)
                v = nn(n1_ref[...], w_in[:, cc]) + nn(zin_ref[...], b_in_ref[:, cc])
                mix_ref[:, cc] = v.astype(bf16)
                pltpu.make_async_copy(mix_ref.at[:, cc], mix_out.at[:, cc], sems.at[2]).start()
                return v

            bg = part(0)
            bx = bg * part(2)
            cv = (
                taps_ref[2:3, col(j)] * bx
                + taps_ref[1:2, col(j)] * pltpu.roll(bx, 1, 0) * m1
                + taps_ref[0:1, col(j)] * pltpu.roll(bx, 2, 0) * m2
            )
            cv_ref[:, col(j)] = cv.astype(bf16)
            pltpu.make_async_copy(cv_ref.at[:, col(j)], cv_out.at[:, col(j)], sems.at[3]).start()
            y_ref[:, col(j)] = (part(1) * cv).astype(bf16)
            pltpu.make_async_copy(y_ref.at[:, col(j)], y_out.at[:, col(j)], sems.at[4]).start()

        loop(blocks, mix)
        for wait in stores:
            wait()
        pltpu.make_async_copy(mix_ref, mix_out, sems.at[2]).wait()
        pltpu.make_async_copy(cv_ref, cv_out, sems.at[3]).wait()
        pltpu.make_async_copy(y_ref, y_out, sems.at[4]).wait()

    wide = [(rows, d), (rows, 3 * d), (rows, d), (rows, d), (d, 3 * d)]
    return pl.pallas_call(
        kernel,
        name="front",
        out_shape=[sds(wide[0], bf16), sds((rows, c), bf16)] + [sds(v, bf16) for v in wide[1:]],
        in_specs=[smem_spec()] + [any_spec()] * (n_pieces + 1) + [vmem_spec()] * 8,
        out_specs=[any_spec(), vmem_spec()] + [any_spec()] * 4,
        scratch_shapes=[pltpu.VMEM(v, bf16) for v in wide]
        + [pltpu.SemaphoreType.DMA, pltpu.SemaphoreType.DMA((5,))],
        compiler_params=params(),
        cost_estimate=cost(2.6 * rows * d * 3 * d),
    )(ids, *pieces, in_shard, x, gain1, taps, sel2, m1, m2, a_in, b_in)


def join_call(ids, pieces, relay, out_shard, y, x, dy, gain2, sel2, a_out, b_out, a_gate, a_up, b_down):
    rows, d = x.shape
    table = piece_table(relay)
    n_pieces = len(pieces)
    pr = d // lax.axis_size("dp")
    c = a_out.shape[1]
    lo = pieces[0].shape[1] - out_shard.shape[1]

    def kernel(*refs):
        ids_ref = refs[0]
        p_refs = refs[1 : 1 + n_pieces]
        (out_ref, x_hbm, dy_hbm, y_ref, g2_ref, sel_ref, a_out_ref, b_out_ref, a_gate_ref, a_up_ref, b_down_ref) = refs[
            1 + n_pieces : 12 + n_pieces
        ]
        (zout_ref, hb_ref, n2_ref, zgu_ref, dzd_ref, w_out_hbm, x_ref, dy_ref, h_ref, w_out, sem_out, sems) = refs[
            12 + n_pieces :
        ]
        gather_copies(ids_ref, p_refs, table, pr, w_out, sem_out, out_ref, lo)
        wait_x, wait_dy = fetched([(x_hbm, x_ref), (dy_hbm, dy_ref)], sems)
        sel = sel_ref[...]
        zout_ref[...] = nn(y_ref[...], a_out_ref[...]).astype(bf16) * sel
        wait_x()
        pltpu.make_async_copy(w_out, w_out, sem_out).wait()
        store = pltpu.make_async_copy(w_out, w_out_hbm, sems.at[2])
        store.start()
        wait_dy()
        dzd_ref[...] = (nt(dy_ref[...], b_down_ref[...]) * sel.astype(f32)).astype(bf16)

        def mid(j):
            o = nn(y_ref[...], w_out[:, col(j)]) + nn(zout_ref[...], b_out_ref[:, col(j)])
            h_ref[:, col(j)] = x_ref[:, col(j)].astype(f32) + o

        loop(d // BN, mid)
        g2 = g2_ref[...]

        def norm2(i):
            v = h_ref[row(i), :]
            hb_ref[row(i), :] = v.astype(bf16)
            r = lax.rsqrt(jnp.mean(v * v, axis=-1, keepdims=True) + eps_norm)
            n2_ref[row(i), :] = (v * r * g2).astype(bf16)

        loop(rows // ROWS, norm2)
        zgu_ref[:, :c] = nn(n2_ref[...], a_gate_ref[...]).astype(bf16) * sel
        zgu_ref[:, c:] = nn(n2_ref[...], a_up_ref[...]).astype(bf16) * sel
        store.wait()

    return pl.pallas_call(
        kernel,
        name="join",
        out_shape=[
            sds((rows, c), bf16), sds((rows, d), bf16), sds((rows, d), bf16), sds((rows, 2 * c), bf16),
            sds((rows, c), bf16), sds((d, d), bf16),
        ],
        in_specs=[smem_spec()] + [any_spec()] * (n_pieces + 3) + [vmem_spec()] * 8,
        out_specs=[vmem_spec()] * 5 + [any_spec()],
        scratch_shapes=[
            pltpu.VMEM((rows, d), bf16), pltpu.VMEM((rows, d), bf16), pltpu.VMEM((rows, d), f32), pltpu.VMEM((d, d), bf16),
            pltpu.SemaphoreType.DMA, pltpu.SemaphoreType.DMA((3,)),
        ],
        compiler_params=params(),
        cost_estimate=cost(2.6 * rows * d * d),
    )(ids, *pieces, out_shard, x, dy, y, gain2, sel2, a_out, b_out, a_gate, a_up, b_down)


def ffn_call(part, ids, pieces, relay, gate_shard, up_shard, down_shard, n2, dy, zgu, dzd,
             b_gate, b_up, a_down, earlier, *state):
    rows, d = n2.shape
    table = piece_table(relay)
    n_pieces = len(pieces)
    quarter = gate_shard.shape[1]
    width = quarter // PARTS
    fp = 4 * width
    pr = d // lax.axis_size("dp")
    dr = fp // lax.axis_size("dp")
    c = zgu.shape[1] // 2
    h_d = down_shard.shape[1]
    n_state = len(state)
    first = n_state == 1
    joins = earlier is not None
    n_join = int(joins)
    dps = lax.axis_size("dp")
    half_rows = rows // 2

    def kernel(*refs):
        ids_ref = refs[0]
        p_refs = refs[1 : 1 + n_pieces]
        rest = refs[1 + n_pieces :]
        (gs_ref, us_ref, ds_ref, bg_hbm, bu_hbm, ad_hbm, n2_hbm, dy_hbm, zgu_hbm, dzd_hbm) = rest[:10]
        earlier_ref = rest[10] if joins else None
        rest = rest[10 + n_join :]
        state_in = rest[:n_state]
        state_out = rest[n_state : n_state + 4]
        (grads_out, acc_ref, dn_ref, dz_ref, zd_ref, grads_ref, wgu, wd, nzg, nzu, dyz, act, dgu,
         da_all, g_all, sems) = rest[n_state + 4 :]
        state = (acc_ref, dn_ref, dz_ref, zd_ref)
        s = ids_ref[0]
        z = ids_ref[1]
        sem_d, sem_g, sem_y, sem_n, sem_b, sem_o = [sems.at[i] for i in range(6)]
        sem_s = sems.at[6:14]

        def put(buf, sem, src, r0, c0, ra=64):
            dst = buf.at[pl.ds(pl.multiple_of(r0, ra), src.shape[0]), pl.ds(pl.multiple_of(c0, 128), src.shape[1])]
            pltpu.make_async_copy(src, dst, sem).start()

        def pieces_to(fn):
            for p_ref, (mask, steps) in zip(p_refs, table):
                for k, t in enumerate(steps):
                    fn(p_ref, k * pr, s ^ mask, (z - t) & 3)

        put(dyz, sem_y, dy_hbm, 0, 0)
        put(dyz, sem_y, dzd_hbm, 0, d)
        for q in range(4):
            at = pl.ds(q * quarter + part * width, width)
            put(wd, sem_d, ds_ref.at[at, :], q * width, z * h_d)
            put(wd, sem_d, ad_hbm.at[at, :], q * width, d)
        half = dr - pr

        def put_down(p, r, s_, z_):
            at = 2 * width
            put(wd, sem_d, p.at[r : r + pr, at : at + h_d], s_ * dr, z_ * h_d)
            put(wd, sem_d, p.at[r : r + half, at + h_d :], s_ * dr + pr, z_ * h_d)
            put(wd, sem_d, p.at[r + half : r + pr, at + h_d :], s_ * dr + pr, z_ * h_d + width - h_d)

        pieces_to(put_down)
        put(nzg, sem_n, n2_hbm, 0, 0)
        put(nzg, sem_n, zgu_hbm.at[:, :c], 0, d)
        put(nzu, sem_n, n2_hbm, 0, 0)
        put(nzu, sem_n, zgu_hbm.at[:, c:], 0, d)
        mine = pl.ds(part * width, width)
        put(wgu, sem_g, gs_ref.at[:, mine], 0, z * width)
        put(wgu, sem_g, us_ref.at[:, mine], 0, fp + z * width)
        for q in range(4):
            at = pl.ds(q * quarter + part * width, width)
            put(wgu, sem_g, bg_hbm.at[:, at], d, q * width)
            put(wgu, sem_g, bu_hbm.at[:, at], d, fp + q * width)

        def put_up(p, r, s_, z_):
            put(wgu, sem_g, p.at[r : r + pr, :width], s_ * pr, z_ * width)
            put(wgu, sem_g, p.at[r : r + pr, width : 2 * width], s_ * pr, fp + z_ * width)

        pieces_to(put_up)
        if joins:
            load_earlier = pltpu.make_async_copy(earlier_ref, grads_ref.at[:, :, :3], sem_b)
            load_earlier.start()
        loads = [pltpu.make_async_copy(a, b, sem_s.at[k]) for k, (a, b) in enumerate(zip(state_in, state))]
        stores = [pltpu.make_async_copy(a, b, sem_s.at[4 + k]) for k, (a, b) in enumerate(zip(state, state_out))]
        for load in loads:
            load.start()

        pltpu.make_async_copy(dyz, dyz, sem_y).wait()
        dzd_t = dyz[:, d:].T
        pltpu.make_async_copy(wd, wd, sem_d).wait()

        def down(j):
            da_all[:, col(j)] = nt(dyz[...], wd[col(j), :])

        loop(fp // BN, down)
        pltpu.make_async_copy(nzg, nzg, sem_n).wait()
        pltpu.make_async_copy(nzu, nzu, sem_n).wait()
        pltpu.make_async_copy(wgu, wgu, sem_g).wait()
        zg_t = nzg[:, d:].T
        zu_t = nzu[:, d:].T
        blocks = fp // BN

        def up_col(j):
            return pl.ds(pl.multiple_of(fp + j * BN, BN), BN)

        def point(j):
            for i in range(2):
                rr = slice(i * half_rows, (i + 1) * half_rows)
                g = nn(nzg[rr, :], wgu[:, col(j)])
                u = nn(nzu[rr, :], wgu[:, up_col(j)])
                da = da_all[rr, col(j)]
                sg = jax.nn.sigmoid(g)
                gs = g * sg
                act[rr, col(j)] = (gs * u).astype(bf16)
                dgu[rr, up_col(j)] = (da * gs).astype(bf16)
                dgu[rr, col(j)] = (da * u * (sg + gs * (1.0 - sg))).astype(bf16)

        def weight_grads(j):
            g_all[0, :, col(j)] = nn(zg_t, dgu[:, col(j)])
            g_all[1, :, col(j)] = nn(zu_t, dgu[:, up_col(j)])
            g_all[2, :, col(j)] = nn(dzd_t, act[:, col(j)])

        point(0)

        def both(j):
            point(j + 1)
            weight_grads(j)

        loop(blocks - 1, both)
        weight_grads(blocks - 1)
        for k in range(3):
            for q in range(4):
                v = g_all[k, :, q * width : (q + 1) * width]
                grads_ref[:, q, 3 * n_join + k] = v.reshape(dps, c // dps, width).astype(bf16)
        if joins:
            load_earlier.wait()
        store_grads = pltpu.make_async_copy(grads_ref, grads_out, sem_o)
        store_grads.start()
        for load in loads:
            load.wait()
        zd = nn(act[...], wd[:, d:])
        dzg = nt(dgu[:, :fp], wgu[d:, :fp])
        dzu = nt(dgu[:, fp:], wgu[d:, fp:])
        if first:
            dz_ref[:, :c] = dzg
            dz_ref[:, c:] = dzu
            zd_ref[...] = zd
        else:
            dz_ref[:, :c] += dzg
            dz_ref[:, c:] += dzu
            zd_ref[...] += zd
        stores[2].start()
        stores[3].start()

        def out_block(j):
            acc_ref[:, col(j)] = (acc_ref[:, col(j)].astype(f32) + nn(act[...], wd[:, col(j)])).astype(bf16)

        loop(d // BN, out_block)
        stores[0].start()

        def dn_block(j):
            v = nt(dgu[...], wgu[col(j), :])
            dn_ref[:, col(j)] = (v if first else dn_ref[:, col(j)].astype(f32) + v).astype(bf16)

        loop(d // BN, dn_block)
        stores[1].start()
        store_grads.wait()
        for store in stores:
            store.wait()

    state_shapes = [((rows, d), bf16), ((rows, d), bf16), ((rows, 2 * c), f32), ((rows, c), f32)]
    grads_shape = (dps, 4, 3 * (1 + n_join), c // dps, width)
    n_any = n_pieces + 10 + n_join + n_state
    return pl.pallas_call(
        kernel,
        name=f"ffn{part}",
        out_shape=[sds(*v) for v in state_shapes] + [sds(grads_shape, bf16)],
        in_specs=[smem_spec()] + [any_spec()] * n_any,
        out_specs=[any_spec()] * 5,
        scratch_shapes=[pltpu.VMEM(*v) for v in state_shapes] + [
            pltpu.VMEM(grads_shape, bf16),
            pltpu.VMEM((d + c, 2 * fp), bf16), pltpu.VMEM((fp, d + c), bf16),
            pltpu.VMEM((rows, d + c), bf16), pltpu.VMEM((rows, d + c), bf16), pltpu.VMEM((rows, d + c), bf16),
            pltpu.VMEM((rows, fp), bf16), pltpu.VMEM((rows, 2 * fp), bf16), pltpu.VMEM((rows, fp), f32),
            pltpu.VMEM((3, c, fp), f32),
            pltpu.SemaphoreType.DMA((14,)),
        ],
        compiler_params=params(),
        cost_estimate=cost(2.6 * rows * d * 6 * fp),
    )(ids, *pieces, gate_shard, up_shard, down_shard, b_gate, b_up, a_down, n2, dy, zgu, dzd,
      *([earlier] if joins else []), *state)


def norm_back_rows(v, gain, dn):
    r = lax.rsqrt(jnp.mean(v * v, axis=-1, keepdims=True) + eps_norm)
    scaled = gain * dn
    return r * scaled - v * (r * r * r * jnp.mean(v * scaled, axis=-1, keepdims=True))


def spread(ref, at, v):
    dps, c = ref.shape[0], v.shape[0]
    n = v.shape[1] // 4
    for q in range(4):
        ref[:, q, :, at : at + n] = v[:, q * n : (q + 1) * n].reshape(dps, c // dps, n).astype(bf16)


def middle_call(acc, dn, dz_acc, zd_acc, h, n2, dy, y, zout, sel2, gain2, b_down, a_gate, a_up, b_out):
    rows, d = h.shape
    c = zout.shape[1]
    blocks = d // BN
    dps = lax.axis_size("dp")

    def kernel(dn_hbm, n2_hbm, dy_hbm, h_hbm, y_hbm, acc_hbm, dz_in, zd_in, zout_ref, sel_ref, g2_ref,
               b_down_ref, a_gate_ref, a_up_ref, b_out_ref, res_out, dhb_out, dzo, ga_ref,
               dn_ref, n2_ref, dy_ref, h_ref, y_ref, acc_ref, dh_ref, dhb, dzgu, zd, sems):
        wait_dn, wait_n2, wait_dy, wait_h, wait_y, wait_acc = fetched(
            [(dn_hbm, dn_ref), (n2_hbm, n2_ref), (dy_hbm, dy_ref), (h_hbm, h_ref), (y_hbm, y_ref), (acc_hbm, acc_ref)],
            sems,
        )
        sel = sel_ref[...]
        sel_f = sel.astype(f32)
        zd[...] = zd_in[...].astype(bf16) * sel
        dzgu[:, :c] = (dz_in[:, :c] * sel_f).astype(bf16)
        dzgu[:, c:] = (dz_in[:, c:] * sel_f).astype(bf16)
        wait_dn()

        def dns(j):
            v = nt(dzgu[:, :c], a_gate_ref[col(j), :]) + nt(dzgu[:, c:], a_up_ref[col(j), :])
            dh_ref[:, col(j)] = dn_ref[:, col(j)].astype(f32) + v

        loop(blocks, dns)
        wait_n2()
        g = nn(dzgu[...].T, n2_ref[...])
        spread(ga_ref, 2 * (d // 4), g[:c])
        spread(ga_ref, 3 * (d // 4), g[c:])
        wait_dy()
        wait_h()
        g2 = g2_ref[...]

        def norm2(i):
            v = dy_ref[row(i), :].astype(f32) + norm_back_rows(h_ref[row(i), :].astype(f32), g2, dh_ref[row(i), :])
            dhb[row(i), :] = v.astype(bf16)

        loop(rows // ROWS, norm2)
        store_dhb = pltpu.make_async_copy(dhb, dhb_out, sems.at[6])
        store_dhb.start()
        wait_acc()

        def results(j):
            v = acc_ref[:, col(j)].astype(f32) + nn(zd[...], b_down_ref[:, col(j)])
            acc_ref[:, col(j)] = v.astype(bf16)

        loop(blocks, results)
        store_res = pltpu.make_async_copy(acc_ref, res_out, sems.at[7])
        store_res.start()
        spread(ga_ref, d // 4, nn(zd[...].T, dy_ref[...]))
        dzo[...] = (nt(dhb[...], b_out_ref[...]) * sel_f).astype(bf16)
        spread(ga_ref, 0, nn(zout_ref[...].T, dhb[...]))
        wait_y()
        spread(ga_ref, 4 * (d // 4), nn(dzo[...].T, y_ref[...]))
        store_dhb.wait()
        store_res.wait()

    wide = pltpu.VMEM((rows, d), bf16)
    return pl.pallas_call(
        kernel,
        name="middle",
        out_shape=[
            sds((rows, d), bf16), sds((rows, d), bf16), sds((rows, c), bf16),
            sds((dps, 4, c // dps, 5 * (d // 4)), bf16),
        ],
        in_specs=[any_spec()] * 6 + [vmem_spec()] * 9,
        out_specs=[any_spec()] * 2 + [vmem_spec()] * 2,
        scratch_shapes=[
            *[wide] * 6, pltpu.VMEM((rows, d), f32), wide, pltpu.VMEM((rows, 2 * c), bf16),
            pltpu.VMEM((rows, c), bf16), pltpu.SemaphoreType.DMA((8,)),
        ],
        compiler_params=params(),
        cost_estimate=cost(2 * rows * d * 4 * d),
    )(dn, n2, dy, h, y, acc, dz_acc, zd_acc, zout, sel2, gain2, b_down, a_gate, a_up, b_out)


def back_call(dhb, dzo, mix, cv, zin, n1, sel2, m1, m2, taps, a_out, b_in, w_out):
    rows, d = dhb.shape
    c = zin.shape[1]
    blocks = d // BN
    dps = lax.axis_size("dp")

    def kernel(w_out_hbm, dhb_hbm, cv_hbm, mix_hbm, n1_hbm, dzo, zin_ref, sel_ref, m1_ref, m2_ref, taps_ref,
               a_out_ref, b_in_ref, dp_out, dzi_ref, gi_ref, w_out_ref, dhb, cv_ref, mix_ref, n1_ref, dp_ref, sems):
        wait_w, wait_dhb, wait_cv, wait_mix, wait_n1 = fetched(
            [(w_out_hbm, w_out_ref), (dhb_hbm, dhb), (cv_hbm, cv_ref), (mix_hbm, mix_ref), (n1_hbm, n1_ref)], sems
        )
        sel_f = sel_ref[...].astype(f32)
        m1 = m1_ref[...]
        m2 = m2_ref[...]
        wait_w()
        wait_dhb()
        wait_cv()
        wait_mix()

        def conv(j):
            dyc = nt(dhb[...], w_out_ref[col(j), :]) + nt(dzo[...], a_out_ref[col(j), :])
            dp_ref[:, col(blocks + j)] = (dyc * cv_ref[:, col(j)].astype(f32)).astype(bf16)
            dcv = dyc * mix_ref[:, col(blocks + j)].astype(f32)
            dbx = (
                taps_ref[2:3, col(j)] * dcv
                + taps_ref[1:2, col(j)] * pltpu.roll(dcv * m1, rows - 1, 0)
                + taps_ref[0:1, col(j)] * pltpu.roll(dcv * m2, rows - 2, 0)
            )
            dp_ref[:, col(j)] = (dbx * mix_ref[:, col(2 * blocks + j)].astype(f32)).astype(bf16)
            dp_ref[:, col(2 * blocks + j)] = (dbx * mix_ref[:, col(j)].astype(f32)).astype(bf16)

        loop(blocks, conv)
        store = pltpu.make_async_copy(dp_ref, dp_out, sems.at[5])
        store.start()
        dzi_ref[...] = (nt(dp_ref[...], b_in_ref[...]) * sel_f).astype(bf16)
        spread(gi_ref, 0, nn(zin_ref[...].T, dp_ref[...]))
        wait_n1()
        spread(gi_ref, 3 * (d // 4), nn(dzi_ref[...].T, n1_ref[...]))
        store.wait()

    wide, long = pltpu.VMEM((rows, d), bf16), pltpu.VMEM((rows, 3 * d), bf16)
    return pl.pallas_call(
        kernel,
        name="back",
        out_shape=[
            sds((rows, 3 * d), bf16), sds((rows, c), bf16), sds((dps, 4, c // dps, d), bf16),
        ],
        in_specs=[any_spec()] * 5 + [vmem_spec()] * 8,
        out_specs=[any_spec()] + [vmem_spec()] * 2,
        scratch_shapes=[pltpu.VMEM((d, d), bf16), wide, wide, long, wide, long, pltpu.SemaphoreType.DMA((6,))],
        compiler_params=params(),
        cost_estimate=cost(2 * rows * d * 4 * d),
    )(w_out, dhb, cv, mix, n1, dzo, zin, sel2, m1, m2, taps, a_out, b_in)


def last_call(dp, dzi, dh, x, gain1, a_in, w_in):
    rows, d = x.shape
    parts = 4

    def kernel(dp_hbm, w_in_hbm, dh_hbm, x_hbm, dzi_ref, g1_ref, a_in_ref, out_hbm, dp_ref, w_in_ref, dh_ref, x_ref,
               dn_ref, sems):
        n = d // parts
        wait_dp, *wait_w, wait_dh, wait_x = fetched(
            [(dp_hbm, dp_ref)]
            + [(w_in_hbm.at[k * n : (k + 1) * n], w_in_ref.at[k * n : (k + 1) * n]) for k in range(parts)]
            + [(dh_hbm, dh_ref), (x_hbm, x_ref)],
            sems,
        )
        wait_dp()
        for wait in wait_w:
            wait()

        def dns(j):
            dn_ref[:, col(j)] = nt(dp_ref[...], w_in_ref[col(j), :]) + nt(dzi_ref[...], a_in_ref[col(j), :])

        loop(d // BN, dns)
        g1 = g1_ref[...]
        wait_dh()
        wait_x()

        def norm1(i):
            v = dh_ref[row(i), :].astype(f32) + norm_back_rows(x_ref[row(i), :].astype(f32), g1, dn_ref[row(i), :])
            dh_ref[row(i), :] = v.astype(bf16)
            pltpu.make_async_copy(dh_ref.at[row(i)], out_hbm.at[row(i)], sems.at[parts + 3]).start()

        loop(rows // ROWS, norm1)
        pltpu.make_async_copy(dh_ref, out_hbm, sems.at[parts + 3]).wait()

    return pl.pallas_call(
        kernel,
        name="last",
        out_shape=sds((rows, d), bf16),
        in_specs=[any_spec()] * 4 + [vmem_spec()] * 3,
        out_specs=any_spec(),
        scratch_shapes=[
            pltpu.VMEM((rows, 3 * d), bf16), pltpu.VMEM((d, 3 * d), bf16), pltpu.VMEM((rows, d), bf16),
            pltpu.VMEM((rows, d), bf16), pltpu.VMEM((rows, d), f32), pltpu.SemaphoreType.DMA((parts + 4,)),
        ],
        compiler_params=params(),
        cost_estimate=cost(2 * rows * d * 4 * d),
    )(dp, w_in, dh, x, dzi, gain1, a_in)


def core_copies(arrays):
    return [swap_dp(a, CORE_BIT) for a in arrays]


def near(zs):
    return [swap_dp(zs, X_BIT), swap_dp(zs, Y_BIT), swap_dp(zs, X_BIT | Y_BIT)]


def far(xs, ys, relay):
    cut = xs.shape[0] // 3 * relay
    return [swap_dp(xs[:cut], Y_BIT), swap_dp(ys[cut:], X_BIT)]


def near_shares(values):
    return [values, *near(values)]


def all_shares(shares):
    return [*shares, *core_copies(shares)]


def finish_call(ids, shares, layout):
    masks = [m for m, _ in piece_table()]
    n = len(shares)
    r = shares[0].shape[-2]
    c = r * n
    widths = [sum(w for _, _, w in parts) for parts, _ in layout]

    def kernel(*refs):
        ids_ref, ins, outs, bufs = refs[0], refs[1 : 1 + n], refs[1 + n : 1 + n + len(layout)], refs[1 + n + len(layout) :]
        s = ids_ref[0]
        for k, (parts, flip) in enumerate(layout):
            target = bufs[k] if flip else outs[k]
            for share, mask in zip(ins, masks):
                at = pl.ds(pl.multiple_of((s ^ mask) * r, r), r)
                to = 0
                for lead, start, w in parts:
                    v = share[:, start : start + w] if lead is None else share[lead, :, start : start + w]
                    target[at, to : to + w] = v.astype(f32)
                    to += w
            if flip:
                outs[k][...] = bufs[k][...].T

    return pl.pallas_call(
        kernel,
        name="finish",
        out_shape=[sds((w, c) if flip else (c, w), f32) for w, (_, flip) in zip(widths, layout)],
        in_specs=[smem_spec()] + [vmem_spec()] * n,
        out_specs=[vmem_spec()] * len(layout),
        scratch_shapes=[pltpu.VMEM((c, w), f32) for w in widths],
        compiler_params=pltpu.CompilerParams(vmem_limit_bytes=16 * 2**20),
    )(ids, *shares)


def exchange(values, axis):
    flat = values.reshape(values.shape[0], -1, values.shape[-1])
    return lax.all_to_all(flat, axis, split_axis=0, concat_axis=0, tiled=True).reshape(values.shape)


def send_to_groups(sums):
    groups = lax.axis_size("group")
    out = [
        lax.ppermute(sums[t - 1], "group", [(i, (i + t) % groups) for i in range(groups)])
        for t in range(1, groups)
    ]
    return [*out, sums[-1]]


def add_up(parts):
    whole = parts[0].astype(f32)
    for p in parts[1:]:
        whole = whole + p.astype(f32)
    return whole.astype(bf16)


def local_pieces(
    tokens, cotangent, order, lengths, adapter_ids, norm_gain, ffn_gain, conv_weight,
    in_weight, out_weight, gate_weight, up_weight, down_weight,
    a_in, b_in, a_out, b_out, a_gate, b_gate, a_up, b_up, a_down, b_down,
):
    dp_count = lax.axis_size("dp")
    s = lax.axis_index("dp")
    z = lax.axis_index("group")
    ids = jnp.stack([s, z]).astype(jnp.int32)
    rows, d = tokens.shape
    order_row = order[0]
    counting = jnp.arange(dp_count, dtype=jnp.int32)
    inverse_row = jnp.sum(
        jnp.where(order_row[None, :] == counting[:, None], counting[None, :], 0), axis=1
    )
    width = gate_weight.shape[1] // PARTS
    sel, after_one, after_two = per_token_tables(
        lengths[:, 0, :][s], adapter_ids[:, 0, :][s], rows, a_in.shape[1], ADAPTER_RANK
    )
    sel2 = sel * adapter_scale
    shards = (in_weight, out_weight, gate_weight, up_weight, down_weight)
    packed = own_pieces(ids, *shards, dp_count, (0,))
    packed = [*packed, *own_pieces(after(ids, packed[0]), *shards, dp_count, tuple(range(1, PARTS)))]
    arrived = lax.all_to_all(cotangent, "dp", split_axis=0, concat_axis=0, tiled=True)
    io_width = in_weight.shape[1] + out_weight.shape[1]
    zs_io, *zs = from_planes(packed[0], [io_width, 3 * width])
    near_io = [swap_dp(zs_io, X_BIT), swap_dp(zs_io, Y_BIT)]
    near_io += far(*near_io, 1)
    io = [zs_io, *near_io]
    io = io + core_copies(io)
    dy = lax.all_to_all(
        picked(arrived, after(inverse_row, packed[1], sel2, after_one, after_two), dp_count), "dp", split_axis=0, concat_axis=0,
        tiled=True,
    )

    gain1 = norm_gain[None, :]
    gain2 = ffn_gain[None, :]
    groups = lax.axis_size("group")

    def over_planes(pieces):
        return others(ids, exchange(pieces.reshape(groups, -1, 3 * width), "group"))

    zs.append(over_planes(after(packed[1], *near_io)))
    first = after(zs[0], dy, *near_io)
    nears = [swap_dp(first, X_BIT), swap_dp(first, Y_BIT)]
    n1, zin, mix, cv, y, w_in = front_call(
        after(ids, dy, zs[0]), io, 1, in_weight, tokens, gain1, conv_weight, sel2, after_one, after_two, a_in, b_in,
    )
    nears += far(*[after(v, zin) for v in nears], 2)
    zs.append(over_planes(after(packed[2], zin, zs[1])))
    zout, h, n2, zgu, dzd, w_out = join_call(
        ids, io, 1, out_weight, y, tokens, dy, gain2, sel2, a_out, b_out, a_gate, a_up, b_down,
    )
    state = (h,)
    previous = n2
    grads = []
    for j in range(PARTS):
        arrays = [zs[j], *[after(v, previous) for v in nears]]
        arrays = arrays + core_copies(arrays)
        if j + 1 < PARTS:
            nears = near(after(zs[j + 1], previous, *nears))
        if j == PARTS - 1:
            early = exchange(after(grads[-1], *nears), "dp")
        *state, g = ffn_call(
            j, after(ids, *zs[j + 1 : j + 2]), arrays, 2 if j == 0 else None, gate_weight, up_weight,
            down_weight, n2, dy, zgu, dzd, b_gate, b_up, a_down, grads[0] if j == 1 else None, *state,
        )
        previous = state[2]
        grads.append(g)
    late = exchange(grads[-1], "dp")
    result, dhb, dzo, g_a = middle_call(
        *state, h, n2, dy, y, zout, sel2, after(gain2, early), b_down, a_gate, a_up, b_out
    )
    ffn_sums = totals_by_shift(ids, early, after(late, dzo))
    g_a = exchange(g_a, "dp")
    ffn = send_to_groups(ffn_sums)
    dp, dzi, g_i = back_call(
        dhb, dzo, mix, cv, zin, n1, sel2, after_one, after_two, after(conv_weight, ffn_sums[0]), a_out, b_in, w_out,
    )
    g_i = exchange(g_i, "dp")
    input_grad = last_call(dp, dzi, dhb, tokens, after(gain1, g_a), a_in, w_in)
    sums = totals_by_shift(ids, g_a, after(g_i, input_grad))
    small = send_to_groups(sums)
    ffn = all_shares(near_shares(add_up([after(ffn[0], input_grad, sums[0]), *ffn[1:]])))
    q = d // lax.axis_size("group")
    layout = [([(3 * j + k, 0, width) for j in range(PARTS)], k == 2) for k in range(3)]
    g_gate_b, g_up_b, g_down_a = finish_call(after(ids, sums[0]), ffn, layout)
    small = all_shares(near_shares(add_up(small)))
    layout = [([(None, k * q, q)], k >= 2) for k in range(5)]
    layout += [([(None, 5 * q, 3 * q)], False), ([(None, 8 * q, q)], True)]
    g_out_b, g_down_b, g_gate_a, g_up_a, g_out_a, g_in_b, g_in_a = finish_call(ids, small, layout)
    return (
        result, input_grad, g_in_a, g_in_b, g_out_a, g_out_b, g_gate_a, g_gate_b, g_up_a, g_up_b, g_down_a,
        g_down_b,
    )


def solution(mesh):
    in_specs = (
        P(("dp", "group"), None),
        P(("dp", "group"), None),
        P("group", None),
        P(None, "group", None),
        P(None, "group", None),
        P(),
        P(),
        P(),
        P(None, "group"),
        P(None, "group"),
        P(None, "group"),
        P(None, "group"),
        P(None, "group"),
        P(),
        P(),
        P(),
        P(),
        P(),
        P(),
        P(),
        P(),
        P(),
        P(),
    )
    out_specs = (
        P(("dp", "group"), None),
        P(("dp", "group"), None),
        P("group", None),
        P(None, "group"),
        P("group", None),
        P(None, "group"),
        P("group", None),
        P(None, "group"),
        P("group", None),
        P(None, "group"),
        P("group", None),
        P(None, "group"),
    )
    small = dict(mesh.shape) == {"dp": 8, "group": 4}
    return jax.shard_map(local_pieces if small else local, mesh=mesh, in_specs=in_specs, out_specs=out_specs, check_vma=False)
```

```python
import jax
import jax.numpy as jnp
from jax import lax
from jax.experimental import pallas as pl
from jax.experimental.pallas import tpu as pltpu
from jax.sharding import PartitionSpec as P

ADAPTER_RANK = 16


eps_norm = 1e-05
adapter_scale = 2.0


def matrix_product(left, right):
    return jnp.dot(left, right, preferred_element_type=jnp.float32)


def transposed_left_matmul(left, right):
    return lax.dot_general(
        left, right, (((0,), (0,)), ((), ())), preferred_element_type=jnp.float32
    )


def transposed_right_matmul(left, right):
    return lax.dot_general(
        left, right, (((1,), (1,)), ((), ())), preferred_element_type=jnp.float32
    )


def per_token_tables(
    sequence_length_row, adapter_index_row, count_of_rows, adapter_column_span, adapter_rank_size
):
    count = sequence_length_row.shape[0]
    earlier = jnp.arange(count)[:, None] <= jnp.arange(count)[None, :]
    finish = jnp.sum(jnp.where(earlier, sequence_length_row[:, None], 0), axis=0)
    starts = finish - sequence_length_row
    counter = jnp.arange(count_of_rows, dtype=jnp.int32)
    member = ((counter[:, None] >= starts[None, :]) & (counter[:, None] < finish[None, :])).astype(
        jnp.int32
    )
    beginning = jnp.sum(member * starts[None, :], axis=1)
    position = counter - beginning
    chosen = jnp.sum(member * adapter_index_row[None, :], axis=1)
    column_span = jnp.arange(adapter_column_span, dtype=jnp.int32) // adapter_rank_size
    select_adapter = (column_span[None, :] == chosen[:, None]).astype(jnp.bfloat16)
    after_one = (position >= 1).astype(jnp.float32)[:, None]
    after_two = (position >= 2).astype(jnp.float32)[:, None]
    return (select_adapter, after_one, after_two)


def delayed(values, amount):
    return jnp.concatenate(
        [jnp.zeros((amount, values.shape[1]), values.dtype), values[:-amount]], axis=0
    )


def advanced(values, amount):
    return jnp.concatenate(
        [values[amount:], jnp.zeros((amount, values.shape[1]), values.dtype)], axis=0
    )


def regroup(values, picks, pieces):
    size = values.shape[0] // pieces
    return jnp.concatenate(
        [lax.dynamic_slice_in_dim(values, picks[i] * size, size, 0) for i in range(pieces)], axis=0
    )


def gather_weight(shard):
    size = shard.shape[0] // lax.axis_size("dp")
    piece = lax.dynamic_slice_in_dim(shard, lax.axis_index("dp") * size, size, 0)
    stacked = lax.all_gather(piece, ("group", "dp"))
    return stacked.reshape(lax.axis_size("group"), shard.shape[0], shard.shape[1])


def wide_product(rows, stacked):
    out = jnp.einsum("rk,gkn->rgn", rows, stacked, preferred_element_type=jnp.float32)
    return out.reshape(rows.shape[0], -1)


def wide_product_back(grads, stacked):
    shaped = grads.reshape(grads.shape[0], stacked.shape[0], stacked.shape[2])
    return jnp.einsum("rgn,gkn->rk", shaped, stacked, preferred_element_type=jnp.float32)


def reduce_grads(terms):
    groups = lax.axis_size("group")
    parts = [t.astype(jnp.bfloat16).reshape(groups, -1, t.shape[1]) for t in terms]
    joined = jnp.concatenate(parts, axis=1)
    flat = joined.reshape(-1, joined.shape[2])
    mine = lax.psum_scatter(flat, ("group", "dp"), scatter_dimension=0, tiled=True)
    share = lax.all_gather(mine, "dp", tiled=True)
    out, at = [], 0
    for p in parts:
        out.append(share[at : at + p.shape[1]].astype(jnp.float32))
        at += p.shape[1]
    return out


def inverse_root(values):
    return lax.rsqrt(jnp.mean(values * values, axis=-1, keepdims=True) + eps_norm)


def norm_back(values, inverse, gain, incoming_gradient):
    scaled = gain * incoming_gradient
    return inverse * scaled - values * (inverse * inverse * inverse) * jnp.mean(
        values * scaled, axis=-1, keepdims=True
    )


def adapter_project(
    input_rows, frozen_weight, adapter_down_factor, adapter_up_factor, select_adapter
):
    reduced_sum = (
        matrix_product(input_rows, adapter_down_factor).astype(jnp.bfloat16) * select_adapter
    )
    return (
        wide_product(input_rows, frozen_weight)
        + adapter_scale * matrix_product(reduced_sum, adapter_up_factor),
        reduced_sum,
    )


def adapter_project_backward(
    incoming_gradient,
    input_rows,
    frozen_weight,
    adapter_down_factor,
    adapter_up_factor,
    reduced_sum,
    select_adapter,
):
    gradient_rank_space = incoming_gradient.astype(jnp.bfloat16)
    gradient_up_factor = adapter_scale * transposed_left_matmul(gradient_rank_space, reduced_sum)
    gradient_reduced_sum = (
        adapter_scale
        * transposed_right_matmul(gradient_rank_space, adapter_up_factor)
        * select_adapter
    ).astype(jnp.bfloat16)
    grad_down = transposed_left_matmul(input_rows, gradient_reduced_sum)
    input_gradients = wide_product_back(
        gradient_rank_space, frozen_weight
    ) + transposed_right_matmul(gradient_reduced_sum, adapter_down_factor)
    return (input_gradients, grad_down, gradient_up_factor)


def local(
    tokens,
    cotangent,
    order,
    lengths,
    adapter_ids,
    norm_gain,
    ffn_gain,
    conv_weight,
    in_weight,
    out_weight,
    gate_weight,
    up_weight,
    down_weight,
    input_first_factor,
    input_second_factor,
    output_first_factor,
    output_second_factor,
    gate_first_factor,
    gate_second_factor,
    up_first_factor,
    up_second_factor,
    down_first_factor,
    down_second_factor,
):
    dp_count = lax.axis_size("dp")
    dp_index = lax.axis_index("dp")
    count_of_rows = tokens.shape[0]
    model_width = tokens.shape[1]
    order_row = order[0]
    counting = jnp.arange(dp_count, dtype=jnp.int32)
    inverse_row = jnp.sum(
        jnp.where(order_row[None, :] == counting[:, None], counting[None, :], 0), axis=1
    )
    arrived = lax.all_to_all(cotangent, "dp", split_axis=0, concat_axis=0, tiled=True)
    cotangent = lax.all_to_all(
        regroup(arrived, inverse_row, dp_count), "dp", split_axis=0, concat_axis=0, tiled=True
    )
    pack_source = dp_index
    hidden_in = tokens
    sequence_length_row = lengths[:, 0, :][pack_source]
    adapter_index_row = adapter_ids[:, 0, :][pack_source]
    select_adapter, after_one, after_two = per_token_tables(
        sequence_length_row,
        adapter_index_row,
        count_of_rows,
        input_first_factor.shape[1],
        ADAPTER_RANK,
    )
    shards = (in_weight, out_weight, gate_weight, up_weight, down_weight)
    full_in, full_out, full_gate, full_up, full_down = [gather_weight(w) for w in shards]
    hidden32 = hidden_in.astype(jnp.float32)
    inverse_one = inverse_root(hidden32)
    normed = (hidden32 * inverse_one * norm_gain).astype(jnp.bfloat16)
    mixed_in, reduced_in = adapter_project(
        normed, full_in, input_first_factor, input_second_factor, select_adapter
    )
    input_gate = mixed_in[:, :model_width]
    output_gate = mixed_in[:, model_width : 2 * model_width]
    conv_input = mixed_in[:, 2 * model_width :]
    gated = input_gate * conv_input
    convolved = (
        conv_weight[2] * gated
        + conv_weight[1] * delayed(gated, 1) * after_one
        + conv_weight[0] * delayed(gated, 2) * after_two
    )
    mixer = (output_gate * convolved).astype(jnp.bfloat16)
    branch, reduced_out = adapter_project(
        mixer, full_out, output_first_factor, output_second_factor, select_adapter
    )
    middle = hidden32 + branch
    inverse_two = inverse_root(middle)
    normed_two = (middle * inverse_two * ffn_gain).astype(jnp.bfloat16)
    gate_pre, reduced_gate = adapter_project(
        normed_two, full_gate, gate_first_factor, gate_second_factor, select_adapter
    )
    up_pre, reduced_up = adapter_project(
        normed_two, full_up, up_first_factor, up_second_factor, select_adapter
    )
    sigmoid_gate = jax.nn.sigmoid(gate_pre)
    activated = (gate_pre * sigmoid_gate * up_pre).astype(jnp.bfloat16)
    ffn_out, reduced_down = adapter_project(
        activated, full_down, down_first_factor, down_second_factor, select_adapter
    )
    result = (middle + ffn_out).astype(jnp.bfloat16)
    back_in, back_out, back_gate, back_up, back_down = full_in, full_out, full_gate, full_up, full_down
    upstream32 = cotangent.astype(jnp.float32)
    grad_act, down_a_grad, down_b_grad = adapter_project_backward(
        upstream32,
        activated,
        back_down,
        down_first_factor,
        down_second_factor,
        reduced_down,
        select_adapter,
    )
    grad_gate_pre = grad_act * up_pre * (sigmoid_gate * (1.0 + gate_pre * (1.0 - sigmoid_gate)))
    grad_up_pre = grad_act * gate_pre * sigmoid_gate
    grad_from_gate, gate_a_grad, gate_b_grad = adapter_project_backward(
        grad_gate_pre,
        normed_two,
        back_gate,
        gate_first_factor,
        gate_second_factor,
        reduced_gate,
        select_adapter,
    )
    grad_from_up, up_a_grad, up_b_grad = adapter_project_backward(
        grad_up_pre,
        normed_two,
        back_up,
        up_first_factor,
        up_second_factor,
        reduced_up,
        select_adapter,
    )
    grad_middle = upstream32 + norm_back(
        middle, inverse_two, ffn_gain, grad_from_gate + grad_from_up
    )
    grad_mixer, out_a_grad, out_b_grad = adapter_project_backward(
        grad_middle,
        mixer,
        back_out,
        output_first_factor,
        output_second_factor,
        reduced_out,
        select_adapter,
    )
    grad_output_gate = grad_mixer * convolved
    grad_conv = grad_mixer * output_gate
    grad_gated = (
        conv_weight[2] * grad_conv
        + conv_weight[1] * advanced(grad_conv * after_one, 1)
        + conv_weight[0] * advanced(grad_conv * after_two, 2)
    )
    grad_mixed = jnp.concatenate(
        [grad_gated * conv_input, grad_output_gate, grad_gated * input_gate], axis=1
    )
    grad_normed, in_a_grad, in_b_grad = adapter_project_backward(
        grad_mixed,
        normed,
        back_in,
        input_first_factor,
        input_second_factor,
        reduced_in,
        select_adapter,
    )
    grad_input = (grad_middle + norm_back(hidden32, inverse_one, norm_gain, grad_normed)).astype(
        jnp.bfloat16
    )
    early = reduce_grads(
        [down_a_grad, down_b_grad, gate_a_grad, gate_b_grad, up_a_grad, up_b_grad, out_a_grad, out_b_grad]
    )
    late = reduce_grads([in_a_grad, in_b_grad])
    totals = (
        late[0], late[1].T, early[6], early[7].T, early[2], early[3].T, early[4], early[5].T,
        early[0], early[1].T,
    )
    return (
        result,
        grad_input,
        totals[0],
        totals[1],
        totals[2],
        totals[3],
        totals[4],
        totals[5],
        totals[6],
        totals[7],
        totals[8],
        totals[9],
    )


f32 = jnp.float32
bf16 = jnp.bfloat16
VMEM_BYTES = 60 * 2**20
PARTS = 3
X_BIT, Y_BIT, CORE_BIT = 2, 4, 1


def nn(a, b):
    return lax.dot_general(a, b, (((1,), (0,)), ((), ())), preferred_element_type=f32)


def nt(a, b):
    return lax.dot_general(a, b, (((1,), (1,)), ((), ())), preferred_element_type=f32)


def swap_dp(values, bit):
    return lax.ppermute(values, "dp", [(i, i ^ bit) for i in range(lax.axis_size("dp"))])


def stacked(parts, start, width):
    size = parts[0].shape[0]

    def kernel(*refs):
        out_ref, sems = refs[-2], refs[-1]
        copies = [
            pltpu.make_async_copy(
                refs[k].at[:, start : start + width], out_ref.at[k * size : (k + 1) * size], sems.at[k]
            )
            for k in range(len(parts))
        ]
        for copy in copies:
            copy.start()
        for copy in copies:
            copy.wait()

    return pl.pallas_call(
        kernel,
        name="stacked",
        out_shape=jax.ShapeDtypeStruct((len(parts) * size, width), parts[0].dtype),
        in_specs=[any_spec()] * len(parts),
        out_specs=vmem_spec(),
        scratch_shapes=[pltpu.SemaphoreType.DMA((len(parts),))],
        compiler_params=pltpu.CompilerParams(vmem_limit_bytes=4 * 2**20),
    )(*parts)


def others(ids, values):
    groups, size, width = values.shape

    def kernel(ids_ref, in_ref, out_ref, sem):
        for t in range(1, groups):
            q = lax.rem(ids_ref[1] + groups - t, groups)
            pltpu.make_async_copy(in_ref.at[q], out_ref.at[(t - 1) * size : t * size], sem).start()
        pltpu.make_async_copy(out_ref, out_ref, sem).wait()

    return pl.pallas_call(
        kernel,
        name="others",
        out_shape=sds(((groups - 1) * size, width), bf16),
        in_specs=[smem_spec(), any_spec()],
        out_specs=vmem_spec(),
        scratch_shapes=[pltpu.SemaphoreType.DMA],
        compiler_params=pltpu.CompilerParams(vmem_limit_bytes=4 * 2**20),
    )(ids, values)


def picked(values, picks, pieces):
    size = values.shape[0] // pieces

    def kernel(picks_ref, in_ref, out_ref, sem):
        for k in range(pieces):
            at = pl.multiple_of(picks_ref[k] * size, size)
            pltpu.make_async_copy(in_ref.at[pl.ds(at, size)], out_ref.at[k * size : (k + 1) * size], sem).start()
        pltpu.make_async_copy(out_ref, out_ref, sem).wait()

    return pl.pallas_call(
        kernel,
        name="picked",
        out_shape=jax.ShapeDtypeStruct(values.shape, values.dtype),
        in_specs=[smem_spec(), any_spec()],
        out_specs=vmem_spec(),
        scratch_shapes=[pltpu.SemaphoreType.DMA],
        compiler_params=pltpu.CompilerParams(vmem_limit_bytes=6 * 2**20),
    )(picks, values)


def totals_by_shift(ids, one, two):
    terms, groups = one.shape[0], one.shape[1]
    shape = list(one.shape[2:])
    along = 0 if len(shape) == 3 else len(shape) - 1
    cut = shape[along]
    shape[along] += two.shape[2 + along]

    def kernel(ids_ref, one_ref, two_ref, *out_refs):
        z = ids_ref[1]
        for t in range(groups):
            q = lax.rem(z + t, groups)
            for in_ref, at in ((one_ref, slice(0, cut)), (two_ref, slice(cut, shape[along]))):
                whole = in_ref[0, q].astype(f32)
                for k in range(1, terms):
                    whole = whole + in_ref[k, q].astype(f32)
                where = (at,) if along == 0 else (slice(None), at)
                out_refs[(t - 1) % groups][where] = whole.astype(bf16)

    return pl.pallas_call(
        kernel,
        name="totals",
        out_shape=[jax.ShapeDtypeStruct(tuple(shape), bf16)] * groups,
        in_specs=[smem_spec(), vmem_spec(), vmem_spec()],
        out_specs=[vmem_spec()] * groups,
        compiler_params=pltpu.CompilerParams(vmem_limit_bytes=16 * 2**20),
    )(ids, one, two)


def from_planes(joined, widths):
    groups = lax.axis_size("group")
    got = [
        lax.ppermute(joined, "group", [(i, (i + t) % groups) for i in range(groups)])
        for t in range(1, groups)
    ]
    out, at = [], 0
    for width in widths:
        out.append(stacked(got, at, width))
        at += width
    return out


def after(values, *others):
    return lax.optimization_barrier((values, *others))[0]


def piece_table(relay=None):
    both = X_BIT | Y_BIT
    table = [(m, (1, 2, 3)) for m in (0, X_BIT, Y_BIT)]
    if relay is None:
        table.append((both, (1, 2, 3)))
    else:
        table += [(both, tuple(range(1, relay + 1))), (both, tuple(range(relay + 1, 4)))]
    return table + [(m | CORE_BIT, steps) for m, steps in table]


def any_spec():
    return pl.BlockSpec(memory_space=pl.ANY)


def hbm_spec():
    return pl.BlockSpec(memory_space=pltpu.HBM)


def vmem_spec():
    return pl.BlockSpec(memory_space=pltpu.VMEM)


def smem_spec():
    return pl.BlockSpec(memory_space=pltpu.SMEM)


def params(size=VMEM_BYTES):
    return pltpu.CompilerParams(vmem_limit_bytes=size)


def cost(flops):
    return pl.CostEstimate(flops=int(flops) // 4096, transcendentals=0, bytes_accessed=0)


def sds(shape, dtype):
    return jax.ShapeDtypeStruct(shape, dtype)


BN = 256


def col(i):
    return pl.ds(pl.multiple_of(i * BN, BN), BN)


ROWS = 128


def row(i):
    return pl.ds(pl.multiple_of(i * ROWS, ROWS), ROWS)


def loop(n, body):
    def step(i, carry):
        body(i)
        return carry

    lax.fori_loop(0, n, step, 0)


def fetched(pairs, sems):
    copies = [pltpu.make_async_copy(a, b, sems.at[k]) for k, (a, b) in enumerate(pairs)]
    for copy in copies:
        copy.start()
    return [copy.wait for copy in copies]


def put_at(buf, sem, src, r0, c0):
    dst = buf.at[pl.ds(pl.multiple_of(r0, 64), src.shape[0]), pl.ds(pl.multiple_of(c0, 128), src.shape[1])]
    pltpu.make_async_copy(src, dst, sem).start()


def own_pieces(ids, in_shard, out_shard, gate_shard, up_shard, down_shard, dps, parts):
    d = in_shard.shape[0]
    pr = d // dps
    quarter = gate_shard.shape[1]
    width = quarter // PARTS
    dr = 4 * width // dps
    per = width // dr
    h_i, h_o, h_d = in_shard.shape[1], out_shard.shape[1], down_shard.shape[1]
    copies = [lax.axis_size("group") if j else 1 for j in range(PARTS)]
    shapes = [(copies[j] * pr, 3 * width if j else h_i + h_o + 3 * width) for j in parts]

    def kernel(ids_ref, in_ref, out_ref, gate_ref, up_ref, down_ref, *rest):
        outs, sems = rest[:-1], rest[-1]
        s = ids_ref[0]
        mine = pl.ds(pl.multiple_of(s * pr, pr), pr)
        for j, dst in zip(parts, outs):
            at = 0

            def put(src, r0=0, n=pr, width_=None):
                for k in range(copies[j]):
                    to = dst.at[k * pr + r0 : k * pr + r0 + n, at : at + width_]
                    pltpu.make_async_copy(src, to, sems.at[j]).start()

            if j == 0:
                put(in_ref.at[mine], width_=h_i)
                at = h_i
                put(out_ref.at[mine], width_=h_o)
                at = h_i + h_o
            cols = pl.ds(j * width, width)
            put(gate_ref.at[mine, cols], width_=width)
            at += width
            put(up_ref.at[mine, cols], width_=width)
            at += width
            top = pl.multiple_of((s // per) * quarter + j * width + (s % per) * dr, 64)
            put(down_ref.at[pl.ds(top, pr)], width_=h_d)
            at += h_d
            half = dr - pr
            put(down_ref.at[pl.ds(top + pr, half), : width - h_d], n=half, width_=width - h_d)
            put(down_ref.at[pl.ds(top + pr, half), width - h_d :], r0=half, n=half, width_=width - h_d)
        for j, dst in zip(parts, outs):
            pltpu.make_async_copy(dst, dst, sems.at[j]).wait()

    return pl.pallas_call(
        kernel,
        name="own",
        out_shape=[sds(v, bf16) for v in shapes],
        in_specs=[smem_spec()] + [hbm_spec()] * 5,
        out_specs=[vmem_spec()] * len(parts),
        scratch_shapes=[pltpu.SemaphoreType.DMA((PARTS,))],
        compiler_params=params(),
    )(ids, in_shard, out_shard, gate_shard, up_shard, down_shard)


def gather_copies(ids_ref, p_refs, table, pr, buf, sem, shard_ref, lo):
    s, z = ids_ref[0], ids_ref[1]
    n = shard_ref.shape[1]
    put_at(buf, sem, shard_ref, 0, z * n)
    for p_ref, (mask, steps) in zip(p_refs, table):
        for k, t in enumerate(steps):
            put_at(buf, sem, p_ref.at[k * pr : (k + 1) * pr, lo : lo + n], (s ^ mask) * pr, ((z - t) & 3) * n)


def front_call(ids, pieces, relay, in_shard, x, gain1, taps, sel2, m1, m2, a_in, b_in):
    rows, d = x.shape
    table = piece_table(relay)
    n_pieces = len(pieces)
    pr = d // lax.axis_size("dp")
    c = a_in.shape[1]
    blocks = d // BN

    def kernel(*refs):
        ids_ref = refs[0]
        p_refs = refs[1 : 1 + n_pieces]
        (in_ref, x_ref, g1_ref, taps_ref, sel_ref, m1_ref, m2_ref, a_in_ref, b_in_ref) = refs[1 + n_pieces : 10 + n_pieces]
        (n1_out, zin_ref, mix_out, cv_out, y_out, w_out, n1_ref, mix_ref, cv_ref, y_ref, w_in,
         sem_in, sems) = refs[10 + n_pieces :]
        gather_copies(ids_ref, p_refs, table, pr, w_in, sem_in, in_ref, 0)
        g1 = g1_ref[...]

        def norm1(i):
            v = x_ref[row(i), :].astype(f32)
            r = lax.rsqrt(jnp.mean(v * v, axis=-1, keepdims=True) + eps_norm)
            n1_ref[row(i), :] = (v * r * g1).astype(bf16)

        loop(rows // ROWS, norm1)
        zin_ref[...] = nn(n1_ref[...], a_in_ref[...]).astype(bf16) * sel_ref[...]
        pltpu.make_async_copy(w_in, w_in, sem_in).wait()
        stores = fetched([(n1_ref, n1_out), (w_in, w_out)], sems)
        m1 = m1_ref[...]
        m2 = m2_ref[...]

        def mix(j):
            def part(k):
                cc = col(k * blocks + j)
                v = nn(n1_ref[...], w_in[:, cc]) + nn(zin_ref[...], b_in_ref[:, cc])
                mix_ref[:, cc] = v.astype(bf16)
                pltpu.make_async_copy(mix_ref.at[:, cc], mix_out.at[:, cc], sems.at[2]).start()
                return v

            bg = part(0)
            bx = bg * part(2)
            cv = (
                taps_ref[2:3, col(j)] * bx
                + taps_ref[1:2, col(j)] * pltpu.roll(bx, 1, 0) * m1
                + taps_ref[0:1, col(j)] * pltpu.roll(bx, 2, 0) * m2
            )
            cv_ref[:, col(j)] = cv.astype(bf16)
            pltpu.make_async_copy(cv_ref.at[:, col(j)], cv_out.at[:, col(j)], sems.at[3]).start()
            y_ref[:, col(j)] = (part(1) * cv).astype(bf16)
            pltpu.make_async_copy(y_ref.at[:, col(j)], y_out.at[:, col(j)], sems.at[4]).start()

        loop(blocks, mix)
        for wait in stores:
            wait()
        pltpu.make_async_copy(mix_ref, mix_out, sems.at[2]).wait()
        pltpu.make_async_copy(cv_ref, cv_out, sems.at[3]).wait()
        pltpu.make_async_copy(y_ref, y_out, sems.at[4]).wait()

    wide = [(rows, d), (rows, 3 * d), (rows, d), (rows, d), (d, 3 * d)]
    return pl.pallas_call(
        kernel,
        name="front",
        out_shape=[sds(wide[0], bf16), sds((rows, c), bf16)] + [sds(v, bf16) for v in wide[1:]],
        in_specs=[smem_spec()] + [any_spec()] * (n_pieces + 1) + [vmem_spec()] * 8,
        out_specs=[any_spec(), vmem_spec()] + [any_spec()] * 4,
        scratch_shapes=[pltpu.VMEM(v, bf16) for v in wide]
        + [pltpu.SemaphoreType.DMA, pltpu.SemaphoreType.DMA((5,))],
        compiler_params=params(),
        cost_estimate=cost(2.6 * rows * d * 3 * d),
    )(ids, *pieces, in_shard, x, gain1, taps, sel2, m1, m2, a_in, b_in)


def join_call(ids, pieces, relay, out_shard, y, x, dy, gain2, sel2, a_out, b_out, a_gate, a_up, b_down):
    rows, d = x.shape
    table = piece_table(relay)
    n_pieces = len(pieces)
    pr = d // lax.axis_size("dp")
    c = a_out.shape[1]
    lo = pieces[0].shape[1] - out_shard.shape[1]

    def kernel(*refs):
        ids_ref = refs[0]
        p_refs = refs[1 : 1 + n_pieces]
        (out_ref, x_hbm, dy_hbm, y_ref, g2_ref, sel_ref, a_out_ref, b_out_ref, a_gate_ref, a_up_ref, b_down_ref) = refs[
            1 + n_pieces : 12 + n_pieces
        ]
        (zout_ref, hb_ref, n2_ref, zgu_ref, dzd_ref, w_out_hbm, x_ref, dy_ref, h_ref, w_out, sem_out, sems) = refs[
            12 + n_pieces :
        ]
        gather_copies(ids_ref, p_refs, table, pr, w_out, sem_out, out_ref, lo)
        wait_x, wait_dy = fetched([(x_hbm, x_ref), (dy_hbm, dy_ref)], sems)
        sel = sel_ref[...]
        zout_ref[...] = nn(y_ref[...], a_out_ref[...]).astype(bf16) * sel
        wait_x()
        pltpu.make_async_copy(w_out, w_out, sem_out).wait()
        store = pltpu.make_async_copy(w_out, w_out_hbm, sems.at[2])
        store.start()
        wait_dy()
        dzd_ref[...] = (nt(dy_ref[...], b_down_ref[...]) * sel.astype(f32)).astype(bf16)

        def mid(j):
            o = nn(y_ref[...], w_out[:, col(j)]) + nn(zout_ref[...], b_out_ref[:, col(j)])
            h_ref[:, col(j)] = x_ref[:, col(j)].astype(f32) + o

        loop(d // BN, mid)
        g2 = g2_ref[...]

        def norm2(i):
            v = h_ref[row(i), :]
            hb_ref[row(i), :] = v.astype(bf16)
            r = lax.rsqrt(jnp.mean(v * v, axis=-1, keepdims=True) + eps_norm)
            n2_ref[row(i), :] = (v * r * g2).astype(bf16)

        loop(rows // ROWS, norm2)
        zgu_ref[:, :c] = nn(n2_ref[...], a_gate_ref[...]).astype(bf16) * sel
        zgu_ref[:, c:] = nn(n2_ref[...], a_up_ref[...]).astype(bf16) * sel
        store.wait()

    return pl.pallas_call(
        kernel,
        name="join",
        out_shape=[
            sds((rows, c), bf16), sds((rows, d), bf16), sds((rows, d), bf16), sds((rows, 2 * c), bf16),
            sds((rows, c), bf16), sds((d, d), bf16),
        ],
        in_specs=[smem_spec()] + [any_spec()] * (n_pieces + 3) + [vmem_spec()] * 8,
        out_specs=[vmem_spec()] * 5 + [any_spec()],
        scratch_shapes=[
            pltpu.VMEM((rows, d), bf16), pltpu.VMEM((rows, d), bf16), pltpu.VMEM((rows, d), f32), pltpu.VMEM((d, d), bf16),
            pltpu.SemaphoreType.DMA, pltpu.SemaphoreType.DMA((3,)),
        ],
        compiler_params=params(),
        cost_estimate=cost(2.6 * rows * d * d),
    )(ids, *pieces, out_shard, x, dy, y, gain2, sel2, a_out, b_out, a_gate, a_up, b_down)


def ffn_call(part, ids, pieces, relay, gate_shard, up_shard, down_shard, n2, dy, zgu, dzd,
             b_gate, b_up, a_down, earlier, *state):
    rows, d = n2.shape
    table = piece_table(relay)
    n_pieces = len(pieces)
    quarter = gate_shard.shape[1]
    width = quarter // PARTS
    fp = 4 * width
    pr = d // lax.axis_size("dp")
    dr = fp // lax.axis_size("dp")
    c = zgu.shape[1] // 2
    h_d = down_shard.shape[1]
    n_state = len(state)
    first = n_state == 1
    joins = earlier is not None
    n_join = int(joins)
    dps = lax.axis_size("dp")
    half_rows = rows // 2

    def kernel(*refs):
        ids_ref = refs[0]
        p_refs = refs[1 : 1 + n_pieces]
        rest = refs[1 + n_pieces :]
        (gs_ref, us_ref, ds_ref, bg_hbm, bu_hbm, ad_hbm, n2_hbm, dy_hbm, zgu_hbm, dzd_hbm) = rest[:10]
        earlier_ref = rest[10] if joins else None
        rest = rest[10 + n_join :]
        state_in = rest[:n_state]
        state_out = rest[n_state : n_state + 4]
        (grads_out, acc_ref, dn_ref, dz_ref, zd_ref, grads_ref, wgu, wd, nzg, nzu, dyz, act, dgu,
         da_all, g_all, sems) = rest[n_state + 4 :]
        state = (acc_ref, dn_ref, dz_ref, zd_ref)
        s = ids_ref[0]
        z = ids_ref[1]
        sem_d, sem_g, sem_y, sem_n, sem_b, sem_o = [sems.at[i] for i in range(6)]
        sem_s = sems.at[6:14]

        def put(buf, sem, src, r0, c0, ra=64):
            dst = buf.at[pl.ds(pl.multiple_of(r0, ra), src.shape[0]), pl.ds(pl.multiple_of(c0, 128), src.shape[1])]
            pltpu.make_async_copy(src, dst, sem).start()

        def pieces_to(fn):
            for p_ref, (mask, steps) in zip(p_refs, table):
                for k, t in enumerate(steps):
                    fn(p_ref, k * pr, s ^ mask, (z - t) & 3)

        put(dyz, sem_y, dy_hbm, 0, 0)
        put(dyz, sem_y, dzd_hbm, 0, d)
        for q in range(4):
            at = pl.ds(q * quarter + part * width, width)
            put(wd, sem_d, ds_ref.at[at, :], q * width, z * h_d)
            put(wd, sem_d, ad_hbm.at[at, :], q * width, d)
        half = dr - pr

        def put_down(p, r, s_, z_):
            at = 2 * width
            put(wd, sem_d, p.at[r : r + pr, at : at + h_d], s_ * dr, z_ * h_d)
            put(wd, sem_d, p.at[r : r + half, at + h_d :], s_ * dr + pr, z_ * h_d)
            put(wd, sem_d, p.at[r + half : r + pr, at + h_d :], s_ * dr + pr, z_ * h_d + width - h_d)

        pieces_to(put_down)
        put(nzg, sem_n, n2_hbm, 0, 0)
        put(nzg, sem_n, zgu_hbm.at[:, :c], 0, d)
        put(nzu, sem_n, n2_hbm, 0, 0)
        put(nzu, sem_n, zgu_hbm.at[:, c:], 0, d)
        mine = pl.ds(part * width, width)
        put(wgu, sem_g, gs_ref.at[:, mine], 0, z * width)
        put(wgu, sem_g, us_ref.at[:, mine], 0, fp + z * width)
        for q in range(4):
            at = pl.ds(q * quarter + part * width, width)
            put(wgu, sem_g, bg_hbm.at[:, at], d, q * width)
            put(wgu, sem_g, bu_hbm.at[:, at], d, fp + q * width)

        def put_up(p, r, s_, z_):
            put(wgu, sem_g, p.at[r : r + pr, :width], s_ * pr, z_ * width)
            put(wgu, sem_g, p.at[r : r + pr, width : 2 * width], s_ * pr, fp + z_ * width)

        pieces_to(put_up)
        if joins:
            load_earlier = pltpu.make_async_copy(earlier_ref, grads_ref.at[:, :, :3], sem_b)
            load_earlier.start()
        loads = [pltpu.make_async_copy(a, b, sem_s.at[k]) for k, (a, b) in enumerate(zip(state_in, state))]
        stores = [pltpu.make_async_copy(a, b, sem_s.at[4 + k]) for k, (a, b) in enumerate(zip(state, state_out))]
        for load in loads:
            load.start()

        pltpu.make_async_copy(dyz, dyz, sem_y).wait()
        dzd_t = dyz[:, d:].T
        pltpu.make_async_copy(wd, wd, sem_d).wait()

        def down(j):
            da_all[:, col(j)] = nt(dyz[...], wd[col(j), :])

        loop(fp // BN, down)
        pltpu.make_async_copy(nzg, nzg, sem_n).wait()
        pltpu.make_async_copy(nzu, nzu, sem_n).wait()
        pltpu.make_async_copy(wgu, wgu, sem_g).wait()
        zg_t = nzg[:, d:].T
        zu_t = nzu[:, d:].T
        blocks = fp // BN

        def up_col(j):
            return pl.ds(pl.multiple_of(fp + j * BN, BN), BN)

        def point(j):
            for i in range(2):
                rr = slice(i * half_rows, (i + 1) * half_rows)
                g = nn(nzg[rr, :], wgu[:, col(j)])
                u = nn(nzu[rr, :], wgu[:, up_col(j)])
                da = da_all[rr, col(j)]
                sg = jax.nn.sigmoid(g)
                gs = g * sg
                act[rr, col(j)] = (gs * u).astype(bf16)
                dgu[rr, up_col(j)] = (da * gs).astype(bf16)
                dgu[rr, col(j)] = (da * u * (sg + gs * (1.0 - sg))).astype(bf16)

        def weight_grads(j):
            g_all[0, :, col(j)] = nn(zg_t, dgu[:, col(j)])
            g_all[1, :, col(j)] = nn(zu_t, dgu[:, up_col(j)])
            g_all[2, :, col(j)] = nn(dzd_t, act[:, col(j)])

        point(0)

        def both(j):
            point(j + 1)
            weight_grads(j)

        loop(blocks - 1, both)
        weight_grads(blocks - 1)
        for k in range(3):
            for q in range(4):
                v = g_all[k, :, q * width : (q + 1) * width]
                grads_ref[:, q, 3 * n_join + k] = v.reshape(dps, c // dps, width).astype(bf16)
        if joins:
            load_earlier.wait()
        store_grads = pltpu.make_async_copy(grads_ref, grads_out, sem_o)
        store_grads.start()
        for load in loads:
            load.wait()
        zd = nn(act[...], wd[:, d:])
        dzg = nt(dgu[:, :fp], wgu[d:, :fp])
        dzu = nt(dgu[:, fp:], wgu[d:, fp:])
        if first:
            dz_ref[:, :c] = dzg
            dz_ref[:, c:] = dzu
            zd_ref[...] = zd
        else:
            dz_ref[:, :c] += dzg
            dz_ref[:, c:] += dzu
            zd_ref[...] += zd
        stores[2].start()
        stores[3].start()

        def out_block(j):
            acc_ref[:, col(j)] = (acc_ref[:, col(j)].astype(f32) + nn(act[...], wd[:, col(j)])).astype(bf16)

        loop(d // BN, out_block)
        stores[0].start()

        def dn_block(j):
            v = nt(dgu[...], wgu[col(j), :])
            dn_ref[:, col(j)] = (v if first else dn_ref[:, col(j)].astype(f32) + v).astype(bf16)

        loop(d // BN, dn_block)
        stores[1].start()
        store_grads.wait()
        for store in stores:
            store.wait()

    state_shapes = [((rows, d), bf16), ((rows, d), bf16), ((rows, 2 * c), f32), ((rows, c), f32)]
    grads_shape = (dps, 4, 3 * (1 + n_join), c // dps, width)
    n_any = n_pieces + 10 + n_join + n_state
    return pl.pallas_call(
        kernel,
        name=f"ffn{part}",
        out_shape=[sds(*v) for v in state_shapes] + [sds(grads_shape, bf16)],
        in_specs=[smem_spec()] + [any_spec()] * n_any,
        out_specs=[any_spec()] * 5,
        scratch_shapes=[pltpu.VMEM(*v) for v in state_shapes] + [
            pltpu.VMEM(grads_shape, bf16),
            pltpu.VMEM((d + c, 2 * fp), bf16), pltpu.VMEM((fp, d + c), bf16),
            pltpu.VMEM((rows, d + c), bf16), pltpu.VMEM((rows, d + c), bf16), pltpu.VMEM((rows, d + c), bf16),
            pltpu.VMEM((rows, fp), bf16), pltpu.VMEM((rows, 2 * fp), bf16), pltpu.VMEM((rows, fp), f32),
            pltpu.VMEM((3, c, fp), f32),
            pltpu.SemaphoreType.DMA((14,)),
        ],
        compiler_params=params(),
        cost_estimate=cost(2.6 * rows * d * 6 * fp),
    )(ids, *pieces, gate_shard, up_shard, down_shard, b_gate, b_up, a_down, n2, dy, zgu, dzd,
      *([earlier] if joins else []), *state)


def norm_back_rows(v, gain, dn):
    r = lax.rsqrt(jnp.mean(v * v, axis=-1, keepdims=True) + eps_norm)
    scaled = gain * dn
    return r * scaled - v * (r * r * r * jnp.mean(v * scaled, axis=-1, keepdims=True))


def spread(ref, at, v):
    dps, c = ref.shape[0], v.shape[0]
    n = v.shape[1] // 4
    for q in range(4):
        ref[:, q, :, at : at + n] = v[:, q * n : (q + 1) * n].reshape(dps, c // dps, n).astype(bf16)


def middle_call(acc, dn, dz_acc, zd_acc, h, n2, dy, y, zout, sel2, gain2, b_down, a_gate, a_up, b_out):
    rows, d = h.shape
    c = zout.shape[1]
    blocks = d // BN
    dps = lax.axis_size("dp")

    def kernel(dn_hbm, n2_hbm, dy_hbm, h_hbm, y_hbm, acc_hbm, dz_in, zd_in, zout_ref, sel_ref, g2_ref,
               b_down_ref, a_gate_ref, a_up_ref, b_out_ref, res_out, dhb_out, dzo, ga_ref,
               dn_ref, n2_ref, dy_ref, h_ref, y_ref, acc_ref, dh_ref, dhb, dzgu, zd, sems):
        wait_dn, wait_n2, wait_dy, wait_h, wait_y, wait_acc = fetched(
            [(dn_hbm, dn_ref), (n2_hbm, n2_ref), (dy_hbm, dy_ref), (h_hbm, h_ref), (y_hbm, y_ref), (acc_hbm, acc_ref)],
            sems,
        )
        sel = sel_ref[...]
        sel_f = sel.astype(f32)
        zd[...] = zd_in[...].astype(bf16) * sel
        dzgu[:, :c] = (dz_in[:, :c] * sel_f).astype(bf16)
        dzgu[:, c:] = (dz_in[:, c:] * sel_f).astype(bf16)
        wait_dn()

        def dns(j):
            v = nt(dzgu[:, :c], a_gate_ref[col(j), :]) + nt(dzgu[:, c:], a_up_ref[col(j), :])
            dh_ref[:, col(j)] = dn_ref[:, col(j)].astype(f32) + v

        loop(blocks, dns)
        wait_n2()
        g = nn(dzgu[...].T, n2_ref[...])
        spread(ga_ref, 2 * (d // 4), g[:c])
        spread(ga_ref, 3 * (d // 4), g[c:])
        wait_dy()
        wait_h()
        g2 = g2_ref[...]

        def norm2(i):
            v = dy_ref[row(i), :].astype(f32) + norm_back_rows(h_ref[row(i), :].astype(f32), g2, dh_ref[row(i), :])
            dhb[row(i), :] = v.astype(bf16)

        loop(rows // ROWS, norm2)
        store_dhb = pltpu.make_async_copy(dhb, dhb_out, sems.at[6])
        store_dhb.start()
        wait_acc()

        def results(j):
            v = acc_ref[:, col(j)].astype(f32) + nn(zd[...], b_down_ref[:, col(j)])
            acc_ref[:, col(j)] = v.astype(bf16)

        loop(blocks, results)
        store_res = pltpu.make_async_copy(acc_ref, res_out, sems.at[7])
        store_res.start()
        spread(ga_ref, d // 4, nn(zd[...].T, dy_ref[...]))
        dzo[...] = (nt(dhb[...], b_out_ref[...]) * sel_f).astype(bf16)
        spread(ga_ref, 0, nn(zout_ref[...].T, dhb[...]))
        wait_y()
        spread(ga_ref, 4 * (d // 4), nn(dzo[...].T, y_ref[...]))
        store_dhb.wait()
        store_res.wait()

    wide = pltpu.VMEM((rows, d), bf16)
    return pl.pallas_call(
        kernel,
        name="middle",
        out_shape=[
            sds((rows, d), bf16), sds((rows, d), bf16), sds((rows, c), bf16),
            sds((dps, 4, c // dps, 5 * (d // 4)), bf16),
        ],
        in_specs=[any_spec()] * 6 + [vmem_spec()] * 9,
        out_specs=[any_spec()] * 2 + [vmem_spec()] * 2,
        scratch_shapes=[
            *[wide] * 6, pltpu.VMEM((rows, d), f32), wide, pltpu.VMEM((rows, 2 * c), bf16),
            pltpu.VMEM((rows, c), bf16), pltpu.SemaphoreType.DMA((8,)),
        ],
        compiler_params=params(),
        cost_estimate=cost(2 * rows * d * 4 * d),
    )(dn, n2, dy, h, y, acc, dz_acc, zd_acc, zout, sel2, gain2, b_down, a_gate, a_up, b_out)


def back_call(dhb, dzo, mix, cv, zin, n1, sel2, m1, m2, taps, a_out, b_in, w_out):
    rows, d = dhb.shape
    c = zin.shape[1]
    blocks = d // BN
    dps = lax.axis_size("dp")

    def kernel(w_out_hbm, dhb_hbm, cv_hbm, mix_hbm, n1_hbm, dzo, zin_ref, sel_ref, m1_ref, m2_ref, taps_ref,
               a_out_ref, b_in_ref, dp_out, dzi_ref, gi_ref, w_out_ref, dhb, cv_ref, mix_ref, n1_ref, dp_ref, sems):
        wait_w, wait_dhb, wait_cv, wait_mix, wait_n1 = fetched(
            [(w_out_hbm, w_out_ref), (dhb_hbm, dhb), (cv_hbm, cv_ref), (mix_hbm, mix_ref), (n1_hbm, n1_ref)], sems
        )
        sel_f = sel_ref[...].astype(f32)
        m1 = m1_ref[...]
        m2 = m2_ref[...]
        wait_w()
        wait_dhb()
        wait_cv()
        wait_mix()

        def conv(j):
            dyc = nt(dhb[...], w_out_ref[col(j), :]) + nt(dzo[...], a_out_ref[col(j), :])
            dp_ref[:, col(blocks + j)] = (dyc * cv_ref[:, col(j)].astype(f32)).astype(bf16)
            dcv = dyc * mix_ref[:, col(blocks + j)].astype(f32)
            dbx = (
                taps_ref[2:3, col(j)] * dcv
                + taps_ref[1:2, col(j)] * pltpu.roll(dcv * m1, rows - 1, 0)
                + taps_ref[0:1, col(j)] * pltpu.roll(dcv * m2, rows - 2, 0)
            )
            dp_ref[:, col(j)] = (dbx * mix_ref[:, col(2 * blocks + j)].astype(f32)).astype(bf16)
            dp_ref[:, col(2 * blocks + j)] = (dbx * mix_ref[:, col(j)].astype(f32)).astype(bf16)

        loop(blocks, conv)
        store = pltpu.make_async_copy(dp_ref, dp_out, sems.at[5])
        store.start()
        dzi_ref[...] = (nt(dp_ref[...], b_in_ref[...]) * sel_f).astype(bf16)
        spread(gi_ref, 0, nn(zin_ref[...].T, dp_ref[...]))
        wait_n1()
        spread(gi_ref, 3 * (d // 4), nn(dzi_ref[...].T, n1_ref[...]))
        store.wait()

    wide, long = pltpu.VMEM((rows, d), bf16), pltpu.VMEM((rows, 3 * d), bf16)
    return pl.pallas_call(
        kernel,
        name="back",
        out_shape=[
            sds((rows, 3 * d), bf16), sds((rows, c), bf16), sds((dps, 4, c // dps, d), bf16),
        ],
        in_specs=[any_spec()] * 5 + [vmem_spec()] * 8,
        out_specs=[any_spec()] + [vmem_spec()] * 2,
        scratch_shapes=[pltpu.VMEM((d, d), bf16), wide, wide, long, wide, long, pltpu.SemaphoreType.DMA((6,))],
        compiler_params=params(),
        cost_estimate=cost(2 * rows * d * 4 * d),
    )(w_out, dhb, cv, mix, n1, dzo, zin, sel2, m1, m2, taps, a_out, b_in)


def last_call(dp, dzi, dh, x, gain1, a_in, w_in):
    rows, d = x.shape
    parts = 4

    def kernel(dp_hbm, w_in_hbm, dh_hbm, x_hbm, dzi_ref, g1_ref, a_in_ref, out_hbm, dp_ref, w_in_ref, dh_ref, x_ref,
               dn_ref, sems):
        n = d // parts
        wait_dp, *wait_w, wait_dh, wait_x = fetched(
            [(dp_hbm, dp_ref)]
            + [(w_in_hbm.at[k * n : (k + 1) * n], w_in_ref.at[k * n : (k + 1) * n]) for k in range(parts)]
            + [(dh_hbm, dh_ref), (x_hbm, x_ref)],
            sems,
        )
        wait_dp()
        for wait in wait_w:
            wait()

        def dns(j):
            dn_ref[:, col(j)] = nt(dp_ref[...], w_in_ref[col(j), :]) + nt(dzi_ref[...], a_in_ref[col(j), :])

        loop(d // BN, dns)
        g1 = g1_ref[...]
        wait_dh()
        wait_x()

        def norm1(i):
            v = dh_ref[row(i), :].astype(f32) + norm_back_rows(x_ref[row(i), :].astype(f32), g1, dn_ref[row(i), :])
            dh_ref[row(i), :] = v.astype(bf16)
            pltpu.make_async_copy(dh_ref.at[row(i)], out_hbm.at[row(i)], sems.at[parts + 3]).start()

        loop(rows // ROWS, norm1)
        pltpu.make_async_copy(dh_ref, out_hbm, sems.at[parts + 3]).wait()

    return pl.pallas_call(
        kernel,
        name="last",
        out_shape=sds((rows, d), bf16),
        in_specs=[any_spec()] * 4 + [vmem_spec()] * 3,
        out_specs=any_spec(),
        scratch_shapes=[
            pltpu.VMEM((rows, 3 * d), bf16), pltpu.VMEM((d, 3 * d), bf16), pltpu.VMEM((rows, d), bf16),
            pltpu.VMEM((rows, d), bf16), pltpu.VMEM((rows, d), f32), pltpu.SemaphoreType.DMA((parts + 4,)),
        ],
        compiler_params=params(),
        cost_estimate=cost(2 * rows * d * 4 * d),
    )(dp, w_in, dh, x, dzi, gain1, a_in)


def core_copies(arrays):
    return [swap_dp(a, CORE_BIT) for a in arrays]


def near(zs):
    return [swap_dp(zs, X_BIT), swap_dp(zs, Y_BIT), swap_dp(zs, X_BIT | Y_BIT)]


def far(xs, ys, relay):
    cut = xs.shape[0] // 3 * relay
    return [swap_dp(xs[:cut], Y_BIT), swap_dp(ys[cut:], X_BIT)]


def near_shares(values):
    return [values, *near(values)]


def all_shares(shares):
    return [*shares, *core_copies(shares)]


def finish_call(ids, shares, layout):
    masks = [m for m, _ in piece_table()]
    n = len(shares)
    r = shares[0].shape[-2]
    c = r * n
    widths = [sum(w for _, _, w in parts) for parts, _ in layout]

    def kernel(*refs):
        ids_ref, ins, outs, bufs = refs[0], refs[1 : 1 + n], refs[1 + n : 1 + n + len(layout)], refs[1 + n + len(layout) :]
        s = ids_ref[0]
        for k, (parts, flip) in enumerate(layout):
            target = bufs[k] if flip else outs[k]
            for share, mask in zip(ins, masks):
                at = pl.ds(pl.multiple_of((s ^ mask) * r, r), r)
                to = 0
                for lead, start, w in parts:
                    v = share[:, start : start + w] if lead is None else share[lead, :, start : start + w]
                    target[at, to : to + w] = v.astype(f32)
                    to += w
            if flip:
                outs[k][...] = bufs[k][...].T

    return pl.pallas_call(
        kernel,
        name="finish",
        out_shape=[sds((w, c) if flip else (c, w), f32) for w, (_, flip) in zip(widths, layout)],
        in_specs=[smem_spec()] + [vmem_spec()] * n,
        out_specs=[vmem_spec()] * len(layout),
        scratch_shapes=[pltpu.VMEM((c, w), f32) for w in widths],
        compiler_params=pltpu.CompilerParams(vmem_limit_bytes=16 * 2**20),
    )(ids, *shares)


def exchange(values, axis):
    flat = values.reshape(values.shape[0], -1, values.shape[-1])
    return lax.all_to_all(flat, axis, split_axis=0, concat_axis=0, tiled=True).reshape(values.shape)


def send_to_groups(sums):
    groups = lax.axis_size("group")
    out = [
        lax.ppermute(sums[t - 1], "group", [(i, (i + t) % groups) for i in range(groups)])
        for t in range(1, groups)
    ]
    return [*out, sums[-1]]


def add_up(parts):
    whole = parts[0].astype(f32)
    for p in parts[1:]:
        whole = whole + p.astype(f32)
    return whole.astype(bf16)


def local_pieces(
    tokens, cotangent, order, lengths, adapter_ids, norm_gain, ffn_gain, conv_weight,
    in_weight, out_weight, gate_weight, up_weight, down_weight,
    a_in, b_in, a_out, b_out, a_gate, b_gate, a_up, b_up, a_down, b_down,
):
    dp_count = lax.axis_size("dp")
    s = lax.axis_index("dp")
    z = lax.axis_index("group")
    ids = jnp.stack([s, z]).astype(jnp.int32)
    rows, d = tokens.shape
    order_row = order[0]
    counting = jnp.arange(dp_count, dtype=jnp.int32)
    inverse_row = jnp.sum(
        jnp.where(order_row[None, :] == counting[:, None], counting[None, :], 0), axis=1
    )
    width = gate_weight.shape[1] // PARTS
    sel, after_one, after_two = per_token_tables(
        lengths[:, 0, :][s], adapter_ids[:, 0, :][s], rows, a_in.shape[1], ADAPTER_RANK
    )
    sel2 = sel * adapter_scale
    shards = (in_weight, out_weight, gate_weight, up_weight, down_weight)
    packed = own_pieces(ids, *shards, dp_count, (0,))
    packed = [*packed, *own_pieces(after(ids, packed[0]), *shards, dp_count, tuple(range(1, PARTS)))]
    arrived = lax.all_to_all(cotangent, "dp", split_axis=0, concat_axis=0, tiled=True)
    io_width = in_weight.shape[1] + out_weight.shape[1]
    zs_io, *zs = from_planes(packed[0], [io_width, 3 * width])
    near_io = [swap_dp(zs_io, X_BIT), swap_dp(zs_io, Y_BIT)]
    near_io += far(*near_io, 1)
    io = [zs_io, *near_io]
    io = io + core_copies(io)
    dy = lax.all_to_all(
        picked(arrived, after(inverse_row, packed[1], sel2, after_one, after_two), dp_count), "dp", split_axis=0, concat_axis=0,
        tiled=True,
    )

    gain1 = norm_gain[None, :]
    gain2 = ffn_gain[None, :]
    groups = lax.axis_size("group")

    def over_planes(pieces):
        return others(ids, exchange(pieces.reshape(groups, -1, 3 * width), "group"))

    zs.append(over_planes(after(packed[1], *near_io)))
    first = after(zs[0], dy, *near_io)
    nears = near(first)
    n1, zin, mix, cv, y, w_in = front_call(
        after(ids, dy, zs[0]), io, 1, in_weight, tokens, gain1, conv_weight, sel2, after_one, after_two, a_in, b_in,
    )
    zs.append(over_planes(after(packed[2], zin, zs[1])))
    zout, h, n2, zgu, dzd, w_out = join_call(
        ids, io, 1, out_weight, y, tokens, dy, gain2, sel2, a_out, b_out, a_gate, a_up, b_down,
    )
    state = (h,)
    previous = n2
    grads = []
    for j in range(PARTS):
        arrays = [zs[j], *[after(v, previous) for v in nears]]
        arrays = arrays + core_copies(arrays)
        if j + 1 < PARTS:
            nears = near(after(zs[j + 1], previous, *nears))
        if j == PARTS - 1:
            early = exchange(after(grads[-1], *nears), "dp")
        *state, g = ffn_call(
            j, after(ids, *zs[j + 1 : j + 2]), arrays, None, gate_weight, up_weight,
            down_weight, n2, dy, zgu, dzd, b_gate, b_up, a_down, grads[0] if j == 1 else None, *state,
        )
        previous = state[2]
        grads.append(g)
    late = exchange(grads[-1], "dp")
    result, dhb, dzo, g_a = middle_call(
        *state, h, n2, dy, y, zout, sel2, after(gain2, early), b_down, a_gate, a_up, b_out
    )
    ffn_sums = totals_by_shift(ids, early, after(late, dzo))
    g_a = exchange(g_a, "dp")
    ffn = send_to_groups(ffn_sums)
    dp, dzi, g_i = back_call(
        dhb, dzo, mix, cv, zin, n1, sel2, after_one, after_two, after(conv_weight, ffn_sums[0]), a_out, b_in, w_out,
    )
    g_i = exchange(g_i, "dp")
    input_grad = last_call(dp, dzi, dhb, tokens, after(gain1, g_a), a_in, w_in)
    sums = totals_by_shift(ids, g_a, after(g_i, input_grad))
    small = send_to_groups(sums)
    ffn = all_shares(near_shares(add_up([after(ffn[0], input_grad, sums[0]), *ffn[1:]])))
    q = d // lax.axis_size("group")
    layout = [([(3 * j + k, 0, width) for j in range(PARTS)], k == 2) for k in range(3)]
    g_gate_b, g_up_b, g_down_a = finish_call(after(ids, sums[0]), ffn, layout)
    small = all_shares(near_shares(add_up(small)))
    layout = [([(None, k * q, q)], k >= 2) for k in range(5)]
    layout += [([(None, 5 * q, 3 * q)], False), ([(None, 8 * q, q)], True)]
    g_out_b, g_down_b, g_gate_a, g_up_a, g_out_a, g_in_b, g_in_a = finish_call(ids, small, layout)
    return (
        result, input_grad, g_in_a, g_in_b, g_out_a, g_out_b, g_gate_a, g_gate_b, g_up_a, g_up_b, g_down_a,
        g_down_b,
    )


def solution(mesh):
    in_specs = (
        P(("dp", "group"), None),
        P(("dp", "group"), None),
        P("group", None),
        P(None, "group", None),
        P(None, "group", None),
        P(),
        P(),
        P(),
        P(None, "group"),
        P(None, "group"),
        P(None, "group"),
        P(None, "group"),
        P(None, "group"),
        P(),
        P(),
        P(),
        P(),
        P(),
        P(),
        P(),
        P(),
        P(),
        P(),
    )
    out_specs = (
        P(("dp", "group"), None),
        P(("dp", "group"), None),
        P("group", None),
        P(None, "group"),
        P("group", None),
        P(None, "group"),
        P("group", None),
        P(None, "group"),
        P("group", None),
        P(None, "group"),
        P("group", None),
        P(None, "group"),
    )
    small = dict(mesh.shape) == {"dp": 8, "group": 4}
    return jax.shard_map(local_pieces if small else local, mesh=mesh, in_specs=in_specs, out_specs=out_specs, check_vma=False)
```

```python
import jax
import jax.numpy as jnp
from jax import lax
from jax.experimental import pallas as pl
from jax.experimental.pallas import tpu as pltpu
from jax.sharding import PartitionSpec as P

ADAPTER_RANK = 16


eps_norm = 1e-05
adapter_scale = 2.0


def matrix_product(left, right):
    return jnp.dot(left, right, preferred_element_type=jnp.float32)


def transposed_left_matmul(left, right):
    return lax.dot_general(
        left, right, (((0,), (0,)), ((), ())), preferred_element_type=jnp.float32
    )


def transposed_right_matmul(left, right):
    return lax.dot_general(
        left, right, (((1,), (1,)), ((), ())), preferred_element_type=jnp.float32
    )


def per_token_tables(
    sequence_length_row, adapter_index_row, count_of_rows, adapter_column_span, adapter_rank_size
):
    count = sequence_length_row.shape[0]
    earlier = jnp.arange(count)[:, None] <= jnp.arange(count)[None, :]
    finish = jnp.sum(jnp.where(earlier, sequence_length_row[:, None], 0), axis=0)
    starts = finish - sequence_length_row
    counter = jnp.arange(count_of_rows, dtype=jnp.int32)
    member = ((counter[:, None] >= starts[None, :]) & (counter[:, None] < finish[None, :])).astype(
        jnp.int32
    )
    beginning = jnp.sum(member * starts[None, :], axis=1)
    position = counter - beginning
    chosen = jnp.sum(member * adapter_index_row[None, :], axis=1)
    column_span = jnp.arange(adapter_column_span, dtype=jnp.int32) // adapter_rank_size
    select_adapter = (column_span[None, :] == chosen[:, None]).astype(jnp.bfloat16)
    after_one = (position >= 1).astype(jnp.float32)[:, None]
    after_two = (position >= 2).astype(jnp.float32)[:, None]
    return (select_adapter, after_one, after_two)


def delayed(values, amount):
    return jnp.concatenate(
        [jnp.zeros((amount, values.shape[1]), values.dtype), values[:-amount]], axis=0
    )


def advanced(values, amount):
    return jnp.concatenate(
        [values[amount:], jnp.zeros((amount, values.shape[1]), values.dtype)], axis=0
    )


def regroup(values, picks, pieces):
    size = values.shape[0] // pieces
    return jnp.concatenate(
        [lax.dynamic_slice_in_dim(values, picks[i] * size, size, 0) for i in range(pieces)], axis=0
    )


def gather_weight(shard):
    size = shard.shape[0] // lax.axis_size("dp")
    piece = lax.dynamic_slice_in_dim(shard, lax.axis_index("dp") * size, size, 0)
    stacked = lax.all_gather(piece, ("group", "dp"))
    return stacked.reshape(lax.axis_size("group"), shard.shape[0], shard.shape[1])


def wide_product(rows, stacked):
    out = jnp.einsum("rk,gkn->rgn", rows, stacked, preferred_element_type=jnp.float32)
    return out.reshape(rows.shape[0], -1)


def wide_product_back(grads, stacked):
    shaped = grads.reshape(grads.shape[0], stacked.shape[0], stacked.shape[2])
    return jnp.einsum("rgn,gkn->rk", shaped, stacked, preferred_element_type=jnp.float32)


def reduce_grads(terms):
    groups = lax.axis_size("group")
    parts = [t.astype(jnp.bfloat16).reshape(groups, -1, t.shape[1]) for t in terms]
    joined = jnp.concatenate(parts, axis=1)
    flat = joined.reshape(-1, joined.shape[2])
    mine = lax.psum_scatter(flat, ("group", "dp"), scatter_dimension=0, tiled=True)
    share = lax.all_gather(mine, "dp", tiled=True)
    out, at = [], 0
    for p in parts:
        out.append(share[at : at + p.shape[1]].astype(jnp.float32))
        at += p.shape[1]
    return out


def inverse_root(values):
    return lax.rsqrt(jnp.mean(values * values, axis=-1, keepdims=True) + eps_norm)


def norm_back(values, inverse, gain, incoming_gradient):
    scaled = gain * incoming_gradient
    return inverse * scaled - values * (inverse * inverse * inverse) * jnp.mean(
        values * scaled, axis=-1, keepdims=True
    )


def adapter_project(
    input_rows, frozen_weight, adapter_down_factor, adapter_up_factor, select_adapter
):
    reduced_sum = (
        matrix_product(input_rows, adapter_down_factor).astype(jnp.bfloat16) * select_adapter
    )
    return (
        wide_product(input_rows, frozen_weight)
        + adapter_scale * matrix_product(reduced_sum, adapter_up_factor),
        reduced_sum,
    )


def adapter_project_backward(
    incoming_gradient,
    input_rows,
    frozen_weight,
    adapter_down_factor,
    adapter_up_factor,
    reduced_sum,
    select_adapter,
):
    gradient_rank_space = incoming_gradient.astype(jnp.bfloat16)
    gradient_up_factor = adapter_scale * transposed_left_matmul(gradient_rank_space, reduced_sum)
    gradient_reduced_sum = (
        adapter_scale
        * transposed_right_matmul(gradient_rank_space, adapter_up_factor)
        * select_adapter
    ).astype(jnp.bfloat16)
    grad_down = transposed_left_matmul(input_rows, gradient_reduced_sum)
    input_gradients = wide_product_back(
        gradient_rank_space, frozen_weight
    ) + transposed_right_matmul(gradient_reduced_sum, adapter_down_factor)
    return (input_gradients, grad_down, gradient_up_factor)


def local(
    tokens,
    cotangent,
    order,
    lengths,
    adapter_ids,
    norm_gain,
    ffn_gain,
    conv_weight,
    in_weight,
    out_weight,
    gate_weight,
    up_weight,
    down_weight,
    input_first_factor,
    input_second_factor,
    output_first_factor,
    output_second_factor,
    gate_first_factor,
    gate_second_factor,
    up_first_factor,
    up_second_factor,
    down_first_factor,
    down_second_factor,
):
    dp_count = lax.axis_size("dp")
    dp_index = lax.axis_index("dp")
    count_of_rows = tokens.shape[0]
    model_width = tokens.shape[1]
    order_row = order[0]
    counting = jnp.arange(dp_count, dtype=jnp.int32)
    inverse_row = jnp.sum(
        jnp.where(order_row[None, :] == counting[:, None], counting[None, :], 0), axis=1
    )
    arrived = lax.all_to_all(cotangent, "dp", split_axis=0, concat_axis=0, tiled=True)
    cotangent = lax.all_to_all(
        regroup(arrived, inverse_row, dp_count), "dp", split_axis=0, concat_axis=0, tiled=True
    )
    pack_source = dp_index
    hidden_in = tokens
    sequence_length_row = lengths[:, 0, :][pack_source]
    adapter_index_row = adapter_ids[:, 0, :][pack_source]
    select_adapter, after_one, after_two = per_token_tables(
        sequence_length_row,
        adapter_index_row,
        count_of_rows,
        input_first_factor.shape[1],
        ADAPTER_RANK,
    )
    shards = (in_weight, out_weight, gate_weight, up_weight, down_weight)
    full_in, full_out, full_gate, full_up, full_down = [gather_weight(w) for w in shards]
    hidden32 = hidden_in.astype(jnp.float32)
    inverse_one = inverse_root(hidden32)
    normed = (hidden32 * inverse_one * norm_gain).astype(jnp.bfloat16)
    mixed_in, reduced_in = adapter_project(
        normed, full_in, input_first_factor, input_second_factor, select_adapter
    )
    input_gate = mixed_in[:, :model_width]
    output_gate = mixed_in[:, model_width : 2 * model_width]
    conv_input = mixed_in[:, 2 * model_width :]
    gated = input_gate * conv_input
    convolved = (
        conv_weight[2] * gated
        + conv_weight[1] * delayed(gated, 1) * after_one
        + conv_weight[0] * delayed(gated, 2) * after_two
    )
    mixer = (output_gate * convolved).astype(jnp.bfloat16)
    branch, reduced_out = adapter_project(
        mixer, full_out, output_first_factor, output_second_factor, select_adapter
    )
    middle = hidden32 + branch
    inverse_two = inverse_root(middle)
    normed_two = (middle * inverse_two * ffn_gain).astype(jnp.bfloat16)
    gate_pre, reduced_gate = adapter_project(
        normed_two, full_gate, gate_first_factor, gate_second_factor, select_adapter
    )
    up_pre, reduced_up = adapter_project(
        normed_two, full_up, up_first_factor, up_second_factor, select_adapter
    )
    sigmoid_gate = jax.nn.sigmoid(gate_pre)
    activated = (gate_pre * sigmoid_gate * up_pre).astype(jnp.bfloat16)
    ffn_out, reduced_down = adapter_project(
        activated, full_down, down_first_factor, down_second_factor, select_adapter
    )
    result = (middle + ffn_out).astype(jnp.bfloat16)
    back_in, back_out, back_gate, back_up, back_down = full_in, full_out, full_gate, full_up, full_down
    upstream32 = cotangent.astype(jnp.float32)
    grad_act, down_a_grad, down_b_grad = adapter_project_backward(
        upstream32,
        activated,
        back_down,
        down_first_factor,
        down_second_factor,
        reduced_down,
        select_adapter,
    )
    grad_gate_pre = grad_act * up_pre * (sigmoid_gate * (1.0 + gate_pre * (1.0 - sigmoid_gate)))
    grad_up_pre = grad_act * gate_pre * sigmoid_gate
    grad_from_gate, gate_a_grad, gate_b_grad = adapter_project_backward(
        grad_gate_pre,
        normed_two,
        back_gate,
        gate_first_factor,
        gate_second_factor,
        reduced_gate,
        select_adapter,
    )
    grad_from_up, up_a_grad, up_b_grad = adapter_project_backward(
        grad_up_pre,
        normed_two,
        back_up,
        up_first_factor,
        up_second_factor,
        reduced_up,
        select_adapter,
    )
    grad_middle = upstream32 + norm_back(
        middle, inverse_two, ffn_gain, grad_from_gate + grad_from_up
    )
    grad_mixer, out_a_grad, out_b_grad = adapter_project_backward(
        grad_middle,
        mixer,
        back_out,
        output_first_factor,
        output_second_factor,
        reduced_out,
        select_adapter,
    )
    grad_output_gate = grad_mixer * convolved
    grad_conv = grad_mixer * output_gate
    grad_gated = (
        conv_weight[2] * grad_conv
        + conv_weight[1] * advanced(grad_conv * after_one, 1)
        + conv_weight[0] * advanced(grad_conv * after_two, 2)
    )
    grad_mixed = jnp.concatenate(
        [grad_gated * conv_input, grad_output_gate, grad_gated * input_gate], axis=1
    )
    grad_normed, in_a_grad, in_b_grad = adapter_project_backward(
        grad_mixed,
        normed,
        back_in,
        input_first_factor,
        input_second_factor,
        reduced_in,
        select_adapter,
    )
    grad_input = (grad_middle + norm_back(hidden32, inverse_one, norm_gain, grad_normed)).astype(
        jnp.bfloat16
    )
    early = reduce_grads(
        [down_a_grad, down_b_grad, gate_a_grad, gate_b_grad, up_a_grad, up_b_grad, out_a_grad, out_b_grad]
    )
    late = reduce_grads([in_a_grad, in_b_grad])
    totals = (
        late[0], late[1].T, early[6], early[7].T, early[2], early[3].T, early[4], early[5].T,
        early[0], early[1].T,
    )
    return (
        result,
        grad_input,
        totals[0],
        totals[1],
        totals[2],
        totals[3],
        totals[4],
        totals[5],
        totals[6],
        totals[7],
        totals[8],
        totals[9],
    )


f32 = jnp.float32
bf16 = jnp.bfloat16
VMEM_BYTES = 60 * 2**20
PARTS = 3
X_BIT, Y_BIT, CORE_BIT = 2, 4, 1


def nn(a, b):
    return lax.dot_general(a, b, (((1,), (0,)), ((), ())), preferred_element_type=f32)


def nt(a, b):
    return lax.dot_general(a, b, (((1,), (1,)), ((), ())), preferred_element_type=f32)


def swap_dp(values, bit):
    return lax.ppermute(values, "dp", [(i, i ^ bit) for i in range(lax.axis_size("dp"))])


def stacked(parts, start, width):
    size = parts[0].shape[0]

    def kernel(*refs):
        out_ref, sems = refs[-2], refs[-1]
        copies = [
            pltpu.make_async_copy(
                refs[k].at[:, start : start + width], out_ref.at[k * size : (k + 1) * size], sems.at[k]
            )
            for k in range(len(parts))
        ]
        for copy in copies:
            copy.start()
        for copy in copies:
            copy.wait()

    return pl.pallas_call(
        kernel,
        name="stacked",
        out_shape=jax.ShapeDtypeStruct((len(parts) * size, width), parts[0].dtype),
        in_specs=[any_spec()] * len(parts),
        out_specs=vmem_spec(),
        scratch_shapes=[pltpu.SemaphoreType.DMA((len(parts),))],
        compiler_params=pltpu.CompilerParams(vmem_limit_bytes=4 * 2**20),
    )(*parts)


def others(ids, values):
    groups, size, width = values.shape

    def kernel(ids_ref, in_ref, out_ref, sem):
        for t in range(1, groups):
            q = lax.rem(ids_ref[1] + groups - t, groups)
            pltpu.make_async_copy(in_ref.at[q], out_ref.at[(t - 1) * size : t * size], sem).start()
        pltpu.make_async_copy(out_ref, out_ref, sem).wait()

    return pl.pallas_call(
        kernel,
        name="others",
        out_shape=sds(((groups - 1) * size, width), bf16),
        in_specs=[smem_spec(), any_spec()],
        out_specs=vmem_spec(),
        scratch_shapes=[pltpu.SemaphoreType.DMA],
        compiler_params=pltpu.CompilerParams(vmem_limit_bytes=4 * 2**20),
    )(ids, values)


def picked(values, picks, pieces):
    size = values.shape[0] // pieces

    def kernel(picks_ref, in_ref, out_ref, sem):
        for k in range(pieces):
            at = pl.multiple_of(picks_ref[k] * size, size)
            pltpu.make_async_copy(in_ref.at[pl.ds(at, size)], out_ref.at[k * size : (k + 1) * size], sem).start()
        pltpu.make_async_copy(out_ref, out_ref, sem).wait()

    return pl.pallas_call(
        kernel,
        name="picked",
        out_shape=jax.ShapeDtypeStruct(values.shape, values.dtype),
        in_specs=[smem_spec(), any_spec()],
        out_specs=vmem_spec(),
        scratch_shapes=[pltpu.SemaphoreType.DMA],
        compiler_params=pltpu.CompilerParams(vmem_limit_bytes=6 * 2**20),
    )(picks, values)


def totals_by_shift(ids, one, two):
    terms, groups = one.shape[0], one.shape[1]
    shape = list(one.shape[2:])
    along = 0 if len(shape) == 3 else len(shape) - 1
    cut = shape[along]
    shape[along] += two.shape[2 + along]

    def kernel(ids_ref, one_ref, two_ref, *out_refs):
        z = ids_ref[1]
        for t in range(groups):
            q = lax.rem(z + t, groups)
            for in_ref, at in ((one_ref, slice(0, cut)), (two_ref, slice(cut, shape[along]))):
                whole = in_ref[0, q].astype(f32)
                for k in range(1, terms):
                    whole = whole + in_ref[k, q].astype(f32)
                where = (at,) if along == 0 else (slice(None), at)
                out_refs[(t - 1) % groups][where] = whole.astype(bf16)

    return pl.pallas_call(
        kernel,
        name="totals",
        out_shape=[jax.ShapeDtypeStruct(tuple(shape), bf16)] * groups,
        in_specs=[smem_spec(), vmem_spec(), vmem_spec()],
        out_specs=[vmem_spec()] * groups,
        compiler_params=pltpu.CompilerParams(vmem_limit_bytes=16 * 2**20),
    )(ids, one, two)


def from_planes(joined, widths):
    groups = lax.axis_size("group")
    got = [
        lax.ppermute(joined, "group", [(i, (i + t) % groups) for i in range(groups)])
        for t in range(1, groups)
    ]
    out, at = [], 0
    for width in widths:
        out.append(stacked(got, at, width))
        at += width
    return out


def after(values, *others):
    return lax.optimization_barrier((values, *others))[0]


def piece_table(relay=None):
    both = X_BIT | Y_BIT
    table = [(m, (1, 2, 3)) for m in (0, X_BIT, Y_BIT)]
    if relay is None:
        table.append((both, (1, 2, 3)))
    else:
        table += [(both, tuple(range(1, relay + 1))), (both, tuple(range(relay + 1, 4)))]
    return table + [(m | CORE_BIT, steps) for m, steps in table]


def any_spec():
    return pl.BlockSpec(memory_space=pl.ANY)


def hbm_spec():
    return pl.BlockSpec(memory_space=pltpu.HBM)


def vmem_spec():
    return pl.BlockSpec(memory_space=pltpu.VMEM)


def smem_spec():
    return pl.BlockSpec(memory_space=pltpu.SMEM)


def params(size=VMEM_BYTES):
    return pltpu.CompilerParams(vmem_limit_bytes=size)


def cost(flops):
    return pl.CostEstimate(flops=int(flops) // 4096, transcendentals=0, bytes_accessed=0)


def sds(shape, dtype):
    return jax.ShapeDtypeStruct(shape, dtype)


BN = 256


def col(i):
    return pl.ds(pl.multiple_of(i * BN, BN), BN)


ROWS = 128


def row(i):
    return pl.ds(pl.multiple_of(i * ROWS, ROWS), ROWS)


def loop(n, body):
    def step(i, carry):
        body(i)
        return carry

    lax.fori_loop(0, n, step, 0)


def fetched(pairs, sems):
    copies = [pltpu.make_async_copy(a, b, sems.at[k]) for k, (a, b) in enumerate(pairs)]
    for copy in copies:
        copy.start()
    return [copy.wait for copy in copies]


def put_at(buf, sem, src, r0, c0):
    dst = buf.at[pl.ds(pl.multiple_of(r0, 64), src.shape[0]), pl.ds(pl.multiple_of(c0, 128), src.shape[1])]
    pltpu.make_async_copy(src, dst, sem).start()


def own_pieces(ids, in_shard, out_shard, gate_shard, up_shard, down_shard, dps, parts):
    d = in_shard.shape[0]
    pr = d // dps
    quarter = gate_shard.shape[1]
    width = quarter // PARTS
    dr = 4 * width // dps
    per = width // dr
    h_i, h_o, h_d = in_shard.shape[1], out_shard.shape[1], down_shard.shape[1]
    copies = [lax.axis_size("group") if j else 1 for j in range(PARTS)]
    shapes = [(copies[j] * pr, 3 * width if j else h_i + h_o + 3 * width) for j in parts]

    def kernel(ids_ref, in_ref, out_ref, gate_ref, up_ref, down_ref, *rest):
        outs, sems = rest[:-1], rest[-1]
        s = ids_ref[0]
        mine = pl.ds(pl.multiple_of(s * pr, pr), pr)
        for j, dst in zip(parts, outs):
            at = 0

            def put(src, r0=0, n=pr, width_=None):
                for k in range(copies[j]):
                    to = dst.at[k * pr + r0 : k * pr + r0 + n, at : at + width_]
                    pltpu.make_async_copy(src, to, sems.at[j]).start()

            if j == 0:
                put(in_ref.at[mine], width_=h_i)
                at = h_i
                put(out_ref.at[mine], width_=h_o)
                at = h_i + h_o
            cols = pl.ds(j * width, width)
            put(gate_ref.at[mine, cols], width_=width)
            at += width
            put(up_ref.at[mine, cols], width_=width)
            at += width
            top = pl.multiple_of((s // per) * quarter + j * width + (s % per) * dr, 64)
            put(down_ref.at[pl.ds(top, pr)], width_=h_d)
            at += h_d
            half = dr - pr
            put(down_ref.at[pl.ds(top + pr, half), : width - h_d], n=half, width_=width - h_d)
            put(down_ref.at[pl.ds(top + pr, half), width - h_d :], r0=half, n=half, width_=width - h_d)
        for j, dst in zip(parts, outs):
            pltpu.make_async_copy(dst, dst, sems.at[j]).wait()

    return pl.pallas_call(
        kernel,
        name="own",
        out_shape=[sds(v, bf16) for v in shapes],
        in_specs=[smem_spec()] + [hbm_spec()] * 5,
        out_specs=[vmem_spec()] * len(parts),
        scratch_shapes=[pltpu.SemaphoreType.DMA((PARTS,))],
        compiler_params=params(),
    )(ids, in_shard, out_shard, gate_shard, up_shard, down_shard)


def gather_copies(ids_ref, p_refs, table, pr, buf, sem, shard_ref, lo):
    s, z = ids_ref[0], ids_ref[1]
    n = shard_ref.shape[1]
    put_at(buf, sem, shard_ref, 0, z * n)
    for p_ref, (mask, steps) in zip(p_refs, table):
        for k, t in enumerate(steps):
            put_at(buf, sem, p_ref.at[k * pr : (k + 1) * pr, lo : lo + n], (s ^ mask) * pr, ((z - t) & 3) * n)


def front_call(ids, pieces, relay, in_shard, x, gain1, taps, sel2, m1, m2, a_in, b_in):
    rows, d = x.shape
    table = piece_table(relay)
    n_pieces = len(pieces)
    pr = d // lax.axis_size("dp")
    c = a_in.shape[1]
    blocks = d // BN

    def kernel(*refs):
        ids_ref = refs[0]
        p_refs = refs[1 : 1 + n_pieces]
        (in_ref, x_ref, g1_ref, taps_ref, sel_ref, m1_ref, m2_ref, a_in_ref, b_in_ref) = refs[1 + n_pieces : 10 + n_pieces]
        (n1_out, zin_ref, mix_out, cv_out, y_out, w_out, n1_ref, mix_ref, cv_ref, y_ref, w_in,
         sem_in, sems) = refs[10 + n_pieces :]
        gather_copies(ids_ref, p_refs, table, pr, w_in, sem_in, in_ref, 0)
        g1 = g1_ref[...]

        def norm1(i):
            v = x_ref[row(i), :].astype(f32)
            r = lax.rsqrt(jnp.mean(v * v, axis=-1, keepdims=True) + eps_norm)
            n1_ref[row(i), :] = (v * r * g1).astype(bf16)

        loop(rows // ROWS, norm1)
        zin_ref[...] = nn(n1_ref[...], a_in_ref[...]).astype(bf16) * sel_ref[...]
        pltpu.make_async_copy(w_in, w_in, sem_in).wait()
        stores = fetched([(n1_ref, n1_out), (w_in, w_out)], sems)
        m1 = m1_ref[...]
        m2 = m2_ref[...]

        def mix(j):
            def part(k):
                cc = col(k * blocks + j)
                v = nn(n1_ref[...], w_in[:, cc]) + nn(zin_ref[...], b_in_ref[:, cc])
                mix_ref[:, cc] = v.astype(bf16)
                pltpu.make_async_copy(mix_ref.at[:, cc], mix_out.at[:, cc], sems.at[2]).start()
                return v

            bg = part(0)
            bx = bg * part(2)
            cv = (
                taps_ref[2:3, col(j)] * bx
                + taps_ref[1:2, col(j)] * pltpu.roll(bx, 1, 0) * m1
                + taps_ref[0:1, col(j)] * pltpu.roll(bx, 2, 0) * m2
            )
            cv_ref[:, col(j)] = cv.astype(bf16)
            pltpu.make_async_copy(cv_ref.at[:, col(j)], cv_out.at[:, col(j)], sems.at[3]).start()
            y_ref[:, col(j)] = (part(1) * cv).astype(bf16)
            pltpu.make_async_copy(y_ref.at[:, col(j)], y_out.at[:, col(j)], sems.at[4]).start()

        loop(blocks, mix)
        for wait in stores:
            wait()
        pltpu.make_async_copy(mix_ref, mix_out, sems.at[2]).wait()
        pltpu.make_async_copy(cv_ref, cv_out, sems.at[3]).wait()
        pltpu.make_async_copy(y_ref, y_out, sems.at[4]).wait()

    wide = [(rows, d), (rows, 3 * d), (rows, d), (rows, d), (d, 3 * d)]
    return pl.pallas_call(
        kernel,
        name="front",
        out_shape=[sds(wide[0], bf16), sds((rows, c), bf16)] + [sds(v, bf16) for v in wide[1:]],
        in_specs=[smem_spec()] + [any_spec()] * (n_pieces + 1) + [vmem_spec()] * 8,
        out_specs=[any_spec(), vmem_spec()] + [any_spec()] * 4,
        scratch_shapes=[pltpu.VMEM(v, bf16) for v in wide]
        + [pltpu.SemaphoreType.DMA, pltpu.SemaphoreType.DMA((5,))],
        compiler_params=params(),
        cost_estimate=cost(2.6 * rows * d * 3 * d),
    )(ids, *pieces, in_shard, x, gain1, taps, sel2, m1, m2, a_in, b_in)


def join_call(ids, pieces, relay, out_shard, y, x, dy, gain2, sel2, a_out, b_out, a_gate, a_up, b_down):
    rows, d = x.shape
    table = piece_table(relay)
    n_pieces = len(pieces)
    pr = d // lax.axis_size("dp")
    c = a_out.shape[1]
    lo = pieces[0].shape[1] - out_shard.shape[1]

    def kernel(*refs):
        ids_ref = refs[0]
        p_refs = refs[1 : 1 + n_pieces]
        (out_ref, x_hbm, dy_hbm, y_ref, g2_ref, sel_ref, a_out_ref, b_out_ref, a_gate_ref, a_up_ref, b_down_ref) = refs[
            1 + n_pieces : 12 + n_pieces
        ]
        (zout_ref, hb_ref, n2_ref, zgu_ref, dzd_ref, w_out_hbm, x_ref, dy_ref, h_ref, w_out, sem_out, sems) = refs[
            12 + n_pieces :
        ]
        gather_copies(ids_ref, p_refs, table, pr, w_out, sem_out, out_ref, lo)
        wait_x, wait_dy = fetched([(x_hbm, x_ref), (dy_hbm, dy_ref)], sems)
        sel = sel_ref[...]
        zout_ref[...] = nn(y_ref[...], a_out_ref[...]).astype(bf16) * sel
        wait_x()
        pltpu.make_async_copy(w_out, w_out, sem_out).wait()
        store = pltpu.make_async_copy(w_out, w_out_hbm, sems.at[2])
        store.start()
        wait_dy()
        dzd_ref[...] = (nt(dy_ref[...], b_down_ref[...]) * sel.astype(f32)).astype(bf16)

        def mid(j):
            o = nn(y_ref[...], w_out[:, col(j)]) + nn(zout_ref[...], b_out_ref[:, col(j)])
            h_ref[:, col(j)] = x_ref[:, col(j)].astype(f32) + o

        loop(d // BN, mid)
        g2 = g2_ref[...]

        def norm2(i):
            v = h_ref[row(i), :]
            hb_ref[row(i), :] = v.astype(bf16)
            r = lax.rsqrt(jnp.mean(v * v, axis=-1, keepdims=True) + eps_norm)
            n2_ref[row(i), :] = (v * r * g2).astype(bf16)

        loop(rows // ROWS, norm2)
        zgu_ref[:, :c] = nn(n2_ref[...], a_gate_ref[...]).astype(bf16) * sel
        zgu_ref[:, c:] = nn(n2_ref[...], a_up_ref[...]).astype(bf16) * sel
        store.wait()

    return pl.pallas_call(
        kernel,
        name="join",
        out_shape=[
            sds((rows, c), bf16), sds((rows, d), bf16), sds((rows, d), bf16), sds((rows, 2 * c), bf16),
            sds((rows, c), bf16), sds((d, d), bf16),
        ],
        in_specs=[smem_spec()] + [any_spec()] * (n_pieces + 3) + [vmem_spec()] * 8,
        out_specs=[vmem_spec()] * 5 + [any_spec()],
        scratch_shapes=[
            pltpu.VMEM((rows, d), bf16), pltpu.VMEM((rows, d), bf16), pltpu.VMEM((rows, d), f32), pltpu.VMEM((d, d), bf16),
            pltpu.SemaphoreType.DMA, pltpu.SemaphoreType.DMA((3,)),
        ],
        compiler_params=params(),
        cost_estimate=cost(2.6 * rows * d * d),
    )(ids, *pieces, out_shard, x, dy, y, gain2, sel2, a_out, b_out, a_gate, a_up, b_down)


def ffn_call(part, ids, pieces, relay, gate_shard, up_shard, down_shard, n2, dy, zgu, dzd,
             b_gate, b_up, a_down, earlier, *state):
    rows, d = n2.shape
    table = piece_table(relay)
    n_pieces = len(pieces)
    quarter = gate_shard.shape[1]
    width = quarter // PARTS
    fp = 4 * width
    pr = d // lax.axis_size("dp")
    dr = fp // lax.axis_size("dp")
    c = zgu.shape[1] // 2
    h_d = down_shard.shape[1]
    n_state = len(state)
    first = n_state == 1
    joins = earlier is not None
    n_join = int(joins)
    dps = lax.axis_size("dp")
    half_rows = rows // 2

    def kernel(*refs):
        ids_ref = refs[0]
        p_refs = refs[1 : 1 + n_pieces]
        rest = refs[1 + n_pieces :]
        (gs_ref, us_ref, ds_ref, bg_hbm, bu_hbm, ad_hbm, n2_hbm, dy_hbm, zgu_hbm, dzd_hbm) = rest[:10]
        earlier_ref = rest[10] if joins else None
        rest = rest[10 + n_join :]
        state_in = rest[:n_state]
        state_out = rest[n_state : n_state + 4]
        (grads_out, acc_ref, dn_ref, dz_ref, zd_ref, grads_ref, wgu, wd, nzg, nzu, dyz, act, dgu,
         da_all, g_all, sems) = rest[n_state + 4 :]
        state = (acc_ref, dn_ref, dz_ref, zd_ref)
        s = ids_ref[0]
        z = ids_ref[1]
        sem_d, sem_g, sem_y, sem_n, sem_b, sem_o = [sems.at[i] for i in range(6)]
        sem_s = sems.at[6:14]

        def put(buf, sem, src, r0, c0, ra=64):
            dst = buf.at[pl.ds(pl.multiple_of(r0, ra), src.shape[0]), pl.ds(pl.multiple_of(c0, 128), src.shape[1])]
            pltpu.make_async_copy(src, dst, sem).start()

        def pieces_to(fn):
            for p_ref, (mask, steps) in zip(p_refs, table):
                for k, t in enumerate(steps):
                    fn(p_ref, k * pr, s ^ mask, (z - t) & 3)

        put(dyz, sem_y, dy_hbm, 0, 0)
        put(dyz, sem_y, dzd_hbm, 0, d)
        for q in range(4):
            at = pl.ds(q * quarter + part * width, width)
            put(wd, sem_d, ds_ref.at[at, :], q * width, z * h_d)
            put(wd, sem_d, ad_hbm.at[at, :], q * width, d)
        half = dr - pr

        def put_down(p, r, s_, z_):
            at = 2 * width
            put(wd, sem_d, p.at[r : r + pr, at : at + h_d], s_ * dr, z_ * h_d)
            put(wd, sem_d, p.at[r : r + half, at + h_d :], s_ * dr + pr, z_ * h_d)
            put(wd, sem_d, p.at[r + half : r + pr, at + h_d :], s_ * dr + pr, z_ * h_d + width - h_d)

        pieces_to(put_down)
        put(nzg, sem_n, n2_hbm, 0, 0)
        put(nzg, sem_n, zgu_hbm.at[:, :c], 0, d)
        put(nzu, sem_n, n2_hbm, 0, 0)
        put(nzu, sem_n, zgu_hbm.at[:, c:], 0, d)
        mine = pl.ds(part * width, width)
        put(wgu, sem_g, gs_ref.at[:, mine], 0, z * width)
        put(wgu, sem_g, us_ref.at[:, mine], 0, fp + z * width)
        for q in range(4):
            at = pl.ds(q * quarter + part * width, width)
            put(wgu, sem_g, bg_hbm.at[:, at], d, q * width)
            put(wgu, sem_g, bu_hbm.at[:, at], d, fp + q * width)

        def put_up(p, r, s_, z_):
            put(wgu, sem_g, p.at[r : r + pr, :width], s_ * pr, z_ * width)
            put(wgu, sem_g, p.at[r : r + pr, width : 2 * width], s_ * pr, fp + z_ * width)

        pieces_to(put_up)
        if joins:
            load_earlier = pltpu.make_async_copy(earlier_ref, grads_ref.at[:, :, :3], sem_b)
            load_earlier.start()
        loads = [pltpu.make_async_copy(a, b, sem_s.at[k]) for k, (a, b) in enumerate(zip(state_in, state))]
        stores = [pltpu.make_async_copy(a, b, sem_s.at[4 + k]) for k, (a, b) in enumerate(zip(state, state_out))]
        for load in loads:
            load.start()

        pltpu.make_async_copy(dyz, dyz, sem_y).wait()
        dzd_t = dyz[:, d:].T
        pltpu.make_async_copy(wd, wd, sem_d).wait()

        def down(j):
            da_all[:, col(j)] = nt(dyz[...], wd[col(j), :])

        loop(fp // BN, down)
        pltpu.make_async_copy(nzg, nzg, sem_n).wait()
        pltpu.make_async_copy(nzu, nzu, sem_n).wait()
        pltpu.make_async_copy(wgu, wgu, sem_g).wait()
        zg_t = nzg[:, d:].T
        zu_t = nzu[:, d:].T
        blocks = fp // BN

        def up_col(j):
            return pl.ds(pl.multiple_of(fp + j * BN, BN), BN)

        def point(j):
            for i in range(2):
                rr = slice(i * half_rows, (i + 1) * half_rows)
                g = nn(nzg[rr, :], wgu[:, col(j)])
                u = nn(nzu[rr, :], wgu[:, up_col(j)])
                da = da_all[rr, col(j)]
                sg = jax.nn.sigmoid(g)
                gs = g * sg
                act[rr, col(j)] = (gs * u).astype(bf16)
                dgu[rr, up_col(j)] = (da * gs).astype(bf16)
                dgu[rr, col(j)] = (da * u * (sg + gs * (1.0 - sg))).astype(bf16)

        def weight_grads(j):
            g_all[0, :, col(j)] = nn(zg_t, dgu[:, col(j)])
            g_all[1, :, col(j)] = nn(zu_t, dgu[:, up_col(j)])
            g_all[2, :, col(j)] = nn(dzd_t, act[:, col(j)])

        point(0)

        def both(j):
            point(j + 1)
            weight_grads(j)

        loop(blocks - 1, both)
        weight_grads(blocks - 1)
        for k in range(3):
            for q in range(4):
                v = g_all[k, :, q * width : (q + 1) * width]
                grads_ref[:, q, 3 * n_join + k] = v.reshape(dps, c // dps, width).astype(bf16)
        if joins:
            load_earlier.wait()
        store_grads = pltpu.make_async_copy(grads_ref, grads_out, sem_o)
        store_grads.start()
        for load in loads:
            load.wait()
        zd = nn(act[...], wd[:, d:])
        dzg = nt(dgu[:, :fp], wgu[d:, :fp])
        dzu = nt(dgu[:, fp:], wgu[d:, fp:])
        if first:
            dz_ref[:, :c] = dzg
            dz_ref[:, c:] = dzu
            zd_ref[...] = zd
        else:
            dz_ref[:, :c] += dzg
            dz_ref[:, c:] += dzu
            zd_ref[...] += zd
        stores[2].start()
        stores[3].start()

        def out_block(j):
            acc_ref[:, col(j)] = (acc_ref[:, col(j)].astype(f32) + nn(act[...], wd[:, col(j)])).astype(bf16)

        loop(d // BN, out_block)
        stores[0].start()

        def dn_block(j):
            v = nt(dgu[...], wgu[col(j), :])
            dn_ref[:, col(j)] = (v if first else dn_ref[:, col(j)].astype(f32) + v).astype(bf16)

        loop(d // BN, dn_block)
        stores[1].start()
        store_grads.wait()
        for store in stores:
            store.wait()

    state_shapes = [((rows, d), bf16), ((rows, d), bf16), ((rows, 2 * c), f32), ((rows, c), f32)]
    grads_shape = (dps, 4, 3 * (1 + n_join), c // dps, width)
    n_any = n_pieces + 10 + n_join + n_state
    return pl.pallas_call(
        kernel,
        name=f"ffn{part}",
        out_shape=[sds(*v) for v in state_shapes] + [sds(grads_shape, bf16)],
        in_specs=[smem_spec()] + [any_spec()] * n_any,
        out_specs=[any_spec()] * 5,
        scratch_shapes=[pltpu.VMEM(*v) for v in state_shapes] + [
            pltpu.VMEM(grads_shape, bf16),
            pltpu.VMEM((d + c, 2 * fp), bf16), pltpu.VMEM((fp, d + c), bf16),
            pltpu.VMEM((rows, d + c), bf16), pltpu.VMEM((rows, d + c), bf16), pltpu.VMEM((rows, d + c), bf16),
            pltpu.VMEM((rows, fp), bf16), pltpu.VMEM((rows, 2 * fp), bf16), pltpu.VMEM((rows, fp), f32),
            pltpu.VMEM((3, c, fp), f32),
            pltpu.SemaphoreType.DMA((14,)),
        ],
        compiler_params=params(),
        cost_estimate=cost(2.6 * rows * d * 6 * fp),
    )(ids, *pieces, gate_shard, up_shard, down_shard, b_gate, b_up, a_down, n2, dy, zgu, dzd,
      *([earlier] if joins else []), *state)


def norm_back_rows(v, gain, dn):
    r = lax.rsqrt(jnp.mean(v * v, axis=-1, keepdims=True) + eps_norm)
    scaled = gain * dn
    return r * scaled - v * (r * r * r * jnp.mean(v * scaled, axis=-1, keepdims=True))


def spread(ref, at, v):
    dps, c = ref.shape[0], v.shape[0]
    n = v.shape[1] // 4
    for q in range(4):
        ref[:, q, :, at : at + n] = v[:, q * n : (q + 1) * n].reshape(dps, c // dps, n).astype(bf16)


def middle_call(acc, dn, dz_acc, zd_acc, h, n2, dy, y, zout, sel2, gain2, b_down, a_gate, a_up, b_out):
    rows, d = h.shape
    c = zout.shape[1]
    blocks = d // BN
    dps = lax.axis_size("dp")

    def kernel(dn_hbm, n2_hbm, dy_hbm, h_hbm, y_hbm, acc_hbm, dz_in, zd_in, zout_ref, sel_ref, g2_ref,
               b_down_ref, a_gate_ref, a_up_ref, b_out_ref, res_out, dhb_out, dzo, ga_ref,
               dn_ref, n2_ref, dy_ref, h_ref, y_ref, acc_ref, dh_ref, dhb, dzgu, zd, sems):
        wait_dn, wait_n2, wait_dy, wait_h, wait_y, wait_acc = fetched(
            [(dn_hbm, dn_ref), (n2_hbm, n2_ref), (dy_hbm, dy_ref), (h_hbm, h_ref), (y_hbm, y_ref), (acc_hbm, acc_ref)],
            sems,
        )
        sel = sel_ref[...]
        sel_f = sel.astype(f32)
        zd[...] = zd_in[...].astype(bf16) * sel
        dzgu[:, :c] = (dz_in[:, :c] * sel_f).astype(bf16)
        dzgu[:, c:] = (dz_in[:, c:] * sel_f).astype(bf16)
        wait_dn()

        def dns(j):
            v = nt(dzgu[:, :c], a_gate_ref[col(j), :]) + nt(dzgu[:, c:], a_up_ref[col(j), :])
            dh_ref[:, col(j)] = dn_ref[:, col(j)].astype(f32) + v

        loop(blocks, dns)
        wait_n2()
        g = nn(dzgu[...].T, n2_ref[...])
        spread(ga_ref, 2 * (d // 4), g[:c])
        spread(ga_ref, 3 * (d // 4), g[c:])
        wait_dy()
        wait_h()
        g2 = g2_ref[...]

        def norm2(i):
            v = dy_ref[row(i), :].astype(f32) + norm_back_rows(h_ref[row(i), :].astype(f32), g2, dh_ref[row(i), :])
            dhb[row(i), :] = v.astype(bf16)

        loop(rows // ROWS, norm2)
        store_dhb = pltpu.make_async_copy(dhb, dhb_out, sems.at[6])
        store_dhb.start()
        wait_acc()

        def results(j):
            v = acc_ref[:, col(j)].astype(f32) + nn(zd[...], b_down_ref[:, col(j)])
            acc_ref[:, col(j)] = v.astype(bf16)

        loop(blocks, results)
        store_res = pltpu.make_async_copy(acc_ref, res_out, sems.at[7])
        store_res.start()
        spread(ga_ref, d // 4, nn(zd[...].T, dy_ref[...]))
        dzo[...] = (nt(dhb[...], b_out_ref[...]) * sel_f).astype(bf16)
        spread(ga_ref, 0, nn(zout_ref[...].T, dhb[...]))
        wait_y()
        spread(ga_ref, 4 * (d // 4), nn(dzo[...].T, y_ref[...]))
        store_dhb.wait()
        store_res.wait()

    wide = pltpu.VMEM((rows, d), bf16)
    return pl.pallas_call(
        kernel,
        name="middle",
        out_shape=[
            sds((rows, d), bf16), sds((rows, d), bf16), sds((rows, c), bf16),
            sds((dps, 4, c // dps, 5 * (d // 4)), bf16),
        ],
        in_specs=[any_spec()] * 6 + [vmem_spec()] * 9,
        out_specs=[any_spec()] * 2 + [vmem_spec()] * 2,
        scratch_shapes=[
            *[wide] * 6, pltpu.VMEM((rows, d), f32), wide, pltpu.VMEM((rows, 2 * c), bf16),
            pltpu.VMEM((rows, c), bf16), pltpu.SemaphoreType.DMA((8,)),
        ],
        compiler_params=params(),
        cost_estimate=cost(2 * rows * d * 4 * d),
    )(dn, n2, dy, h, y, acc, dz_acc, zd_acc, zout, sel2, gain2, b_down, a_gate, a_up, b_out)


def back_call(dhb, dzo, mix, cv, zin, n1, sel2, m1, m2, taps, a_out, b_in, w_out):
    rows, d = dhb.shape
    c = zin.shape[1]
    blocks = d // BN
    dps = lax.axis_size("dp")

    def kernel(w_out_hbm, dhb_hbm, cv_hbm, mix_hbm, n1_hbm, dzo, zin_ref, sel_ref, m1_ref, m2_ref, taps_ref,
               a_out_ref, b_in_ref, dp_out, dzi_ref, gi_ref, w_out_ref, dhb, cv_ref, mix_ref, n1_ref, dp_ref, sems):
        wanted = [(w_out_hbm, w_out_ref), (dhb_hbm, dhb)]
        for j in range(blocks):
            wanted.append((cv_hbm.at[:, col(j)], cv_ref.at[:, col(j)]))
            for k in (1, 2, 0):
                cc = col(k * blocks + j)
                wanted.append((mix_hbm.at[:, cc], mix_ref.at[:, cc]))
        wait_w, wait_dhb, *wait_block, wait_n1 = fetched([*wanted, (n1_hbm, n1_ref)], sems)
        sel_f = sel_ref[...].astype(f32)
        m1 = m1_ref[...]
        m2 = m2_ref[...]
        wait_w()
        wait_dhb()

        def conv(j):
            dyc = nt(dhb[...], w_out_ref[col(j), :]) + nt(dzo[...], a_out_ref[col(j), :])
            for wait in wait_block[4 * j : 4 * j + 4]:
                wait()
            dp_ref[:, col(blocks + j)] = (dyc * cv_ref[:, col(j)].astype(f32)).astype(bf16)
            dcv = dyc * mix_ref[:, col(blocks + j)].astype(f32)
            dbx = (
                taps_ref[2:3, col(j)] * dcv
                + taps_ref[1:2, col(j)] * pltpu.roll(dcv * m1, rows - 1, 0)
                + taps_ref[0:1, col(j)] * pltpu.roll(dcv * m2, rows - 2, 0)
            )
            dp_ref[:, col(j)] = (dbx * mix_ref[:, col(2 * blocks + j)].astype(f32)).astype(bf16)
            dp_ref[:, col(2 * blocks + j)] = (dbx * mix_ref[:, col(j)].astype(f32)).astype(bf16)

        for j in range(blocks):
            conv(j)
        store = pltpu.make_async_copy(dp_ref, dp_out, sems.at[4 * blocks + 3])
        store.start()
        dzi_ref[...] = (nt(dp_ref[...], b_in_ref[...]) * sel_f).astype(bf16)
        spread(gi_ref, 0, nn(zin_ref[...].T, dp_ref[...]))
        wait_n1()
        spread(gi_ref, 3 * (d // 4), nn(dzi_ref[...].T, n1_ref[...]))
        store.wait()

    wide, long = pltpu.VMEM((rows, d), bf16), pltpu.VMEM((rows, 3 * d), bf16)
    return pl.pallas_call(
        kernel,
        name="back",
        out_shape=[
            sds((rows, 3 * d), bf16), sds((rows, c), bf16), sds((dps, 4, c // dps, d), bf16),
        ],
        in_specs=[any_spec()] * 5 + [vmem_spec()] * 8,
        out_specs=[any_spec()] + [vmem_spec()] * 2,
        scratch_shapes=[pltpu.VMEM((d, d), bf16), wide, wide, long, wide, long, pltpu.SemaphoreType.DMA((4 * blocks + 4,))],
        compiler_params=params(),
        cost_estimate=cost(2 * rows * d * 4 * d),
    )(w_out, dhb, cv, mix, n1, dzo, zin, sel2, m1, m2, taps, a_out, b_in)


def last_call(dp, dzi, dh, x, gain1, a_in, w_in):
    rows, d = x.shape
    parts = 4

    def kernel(dp_hbm, w_in_hbm, dh_hbm, x_hbm, dzi_ref, g1_ref, a_in_ref, out_hbm, dp_ref, w_in_ref, dh_ref, x_ref,
               dn_ref, sems):
        n = d // parts
        wait_dp, *wait_w, wait_dh, wait_x = fetched(
            [(dp_hbm, dp_ref)]
            + [(w_in_hbm.at[k * n : (k + 1) * n], w_in_ref.at[k * n : (k + 1) * n]) for k in range(parts)]
            + [(dh_hbm, dh_ref), (x_hbm, x_ref)],
            sems,
        )
        wait_dp()
        for wait in wait_w:
            wait()

        def dns(j):
            dn_ref[:, col(j)] = nt(dp_ref[...], w_in_ref[col(j), :]) + nt(dzi_ref[...], a_in_ref[col(j), :])

        loop(d // BN, dns)
        g1 = g1_ref[...]
        wait_dh()
        wait_x()

        def norm1(i):
            v = dh_ref[row(i), :].astype(f32) + norm_back_rows(x_ref[row(i), :].astype(f32), g1, dn_ref[row(i), :])
            dh_ref[row(i), :] = v.astype(bf16)
            pltpu.make_async_copy(dh_ref.at[row(i)], out_hbm.at[row(i)], sems.at[parts + 3]).start()

        loop(rows // ROWS, norm1)
        pltpu.make_async_copy(dh_ref, out_hbm, sems.at[parts + 3]).wait()

    return pl.pallas_call(
        kernel,
        name="last",
        out_shape=sds((rows, d), bf16),
        in_specs=[any_spec()] * 4 + [vmem_spec()] * 3,
        out_specs=any_spec(),
        scratch_shapes=[
            pltpu.VMEM((rows, 3 * d), bf16), pltpu.VMEM((d, 3 * d), bf16), pltpu.VMEM((rows, d), bf16),
            pltpu.VMEM((rows, d), bf16), pltpu.VMEM((rows, d), f32), pltpu.SemaphoreType.DMA((parts + 4,)),
        ],
        compiler_params=params(),
        cost_estimate=cost(2 * rows * d * 4 * d),
    )(dp, w_in, dh, x, dzi, gain1, a_in)


def core_copies(arrays):
    return [swap_dp(a, CORE_BIT) for a in arrays]


def near(zs):
    return [swap_dp(zs, X_BIT), swap_dp(zs, Y_BIT), swap_dp(zs, X_BIT | Y_BIT)]


def far(xs, ys, relay):
    cut = xs.shape[0] // 3 * relay
    return [swap_dp(xs[:cut], Y_BIT), swap_dp(ys[cut:], X_BIT)]


def near_shares(values):
    return [values, *near(values)]


def all_shares(shares):
    return [*shares, *core_copies(shares)]


def finish_call(ids, shares, layout):
    masks = [m for m, _ in piece_table()]
    n = len(shares)
    r = shares[0].shape[-2]
    c = r * n
    widths = [sum(w for _, _, w in parts) for parts, _ in layout]

    def kernel(*refs):
        ids_ref, ins, outs, bufs = refs[0], refs[1 : 1 + n], refs[1 + n : 1 + n + len(layout)], refs[1 + n + len(layout) :]
        s = ids_ref[0]
        for k, (parts, flip) in enumerate(layout):
            target = bufs[k] if flip else outs[k]
            for share, mask in zip(ins, masks):
                at = pl.ds(pl.multiple_of((s ^ mask) * r, r), r)
                to = 0
                for lead, start, w in parts:
                    v = share[:, start : start + w] if lead is None else share[lead, :, start : start + w]
                    target[at, to : to + w] = v.astype(f32)
                    to += w
            if flip:
                outs[k][...] = bufs[k][...].T

    return pl.pallas_call(
        kernel,
        name="finish",
        out_shape=[sds((w, c) if flip else (c, w), f32) for w, (_, flip) in zip(widths, layout)],
        in_specs=[smem_spec()] + [vmem_spec()] * n,
        out_specs=[vmem_spec()] * len(layout),
        scratch_shapes=[pltpu.VMEM((c, w), f32) for w in widths],
        compiler_params=pltpu.CompilerParams(vmem_limit_bytes=16 * 2**20),
    )(ids, *shares)


def exchange(values, axis):
    flat = values.reshape(values.shape[0], -1, values.shape[-1])
    return lax.all_to_all(flat, axis, split_axis=0, concat_axis=0, tiled=True).reshape(values.shape)


def send_to_groups(sums):
    groups = lax.axis_size("group")
    out = [
        lax.ppermute(sums[t - 1], "group", [(i, (i + t) % groups) for i in range(groups)])
        for t in range(1, groups)
    ]
    return [*out, sums[-1]]


def add_up(parts):
    whole = parts[0].astype(f32)
    for p in parts[1:]:
        whole = whole + p.astype(f32)
    return whole.astype(bf16)


def local_pieces(
    tokens, cotangent, order, lengths, adapter_ids, norm_gain, ffn_gain, conv_weight,
    in_weight, out_weight, gate_weight, up_weight, down_weight,
    a_in, b_in, a_out, b_out, a_gate, b_gate, a_up, b_up, a_down, b_down,
):
    dp_count = lax.axis_size("dp")
    s = lax.axis_index("dp")
    z = lax.axis_index("group")
    ids = jnp.stack([s, z]).astype(jnp.int32)
    rows, d = tokens.shape
    order_row = order[0]
    counting = jnp.arange(dp_count, dtype=jnp.int32)
    inverse_row = jnp.sum(
        jnp.where(order_row[None, :] == counting[:, None], counting[None, :], 0), axis=1
    )
    width = gate_weight.shape[1] // PARTS
    sel, after_one, after_two = per_token_tables(
        lengths[:, 0, :][s], adapter_ids[:, 0, :][s], rows, a_in.shape[1], ADAPTER_RANK
    )
    sel2 = sel * adapter_scale
    shards = (in_weight, out_weight, gate_weight, up_weight, down_weight)
    packed = own_pieces(ids, *shards, dp_count, (0,))
    packed = [*packed, *own_pieces(after(ids, packed[0]), *shards, dp_count, tuple(range(1, PARTS)))]
    arrived = lax.all_to_all(cotangent, "dp", split_axis=0, concat_axis=0, tiled=True)
    io_width = in_weight.shape[1] + out_weight.shape[1]
    zs_io, *zs = from_planes(packed[0], [io_width, 3 * width])
    near_io = [swap_dp(zs_io, X_BIT), swap_dp(zs_io, Y_BIT)]
    near_io += far(*near_io, 1)
    io = [zs_io, *near_io]
    io = io + core_copies(io)
    dy = lax.all_to_all(
        picked(arrived, after(inverse_row, packed[1], sel2, after_one, after_two), dp_count), "dp", split_axis=0, concat_axis=0,
        tiled=True,
    )

    gain1 = norm_gain[None, :]
    gain2 = ffn_gain[None, :]
    groups = lax.axis_size("group")

    def over_planes(pieces):
        return others(ids, exchange(pieces.reshape(groups, -1, 3 * width), "group"))

    zs.append(over_planes(after(packed[1], *near_io)))
    first = after(zs[0], dy, *near_io)
    nears = near(first)
    n1, zin, mix, cv, y, w_in = front_call(
        after(ids, dy, zs[0]), io, 1, in_weight, tokens, gain1, conv_weight, sel2, after_one, after_two, a_in, b_in,
    )
    zs.append(over_planes(after(packed[2], zin, zs[1])))
    zout, h, n2, zgu, dzd, w_out = join_call(
        ids, io, 1, out_weight, y, tokens, dy, gain2, sel2, a_out, b_out, a_gate, a_up, b_down,
    )
    state = (h,)
    previous = n2
    grads = []
    for j in range(PARTS):
        arrays = [zs[j], *[after(v, previous) for v in nears]]
        arrays = arrays + core_copies(arrays)
        if j + 1 < PARTS:
            nears = near(after(zs[j + 1], previous, *nears))
        if j == PARTS - 1:
            early = exchange(after(grads[-1], *nears), "dp")
        *state, g = ffn_call(
            j, after(ids, *zs[j + 1 : j + 2]), arrays, None, gate_weight, up_weight,
            down_weight, n2, dy, zgu, dzd, b_gate, b_up, a_down, grads[0] if j == 1 else None, *state,
        )
        previous = state[2]
        grads.append(g)
    late = exchange(grads[-1], "dp")
    result, dhb, dzo, g_a = middle_call(
        *state, h, n2, dy, y, zout, sel2, after(gain2, early), b_down, a_gate, a_up, b_out
    )
    ffn_sums = totals_by_shift(ids, early, after(late, dzo))
    g_a = exchange(g_a, "dp")
    ffn = send_to_groups(ffn_sums)
    dp, dzi, g_i = back_call(
        dhb, dzo, mix, cv, zin, n1, sel2, after_one, after_two, after(conv_weight, ffn_sums[0]), a_out, b_in, w_out,
    )
    g_i = exchange(g_i, "dp")
    input_grad = last_call(dp, dzi, dhb, tokens, after(gain1, g_a), a_in, w_in)
    sums = totals_by_shift(ids, g_a, after(g_i, input_grad))
    small = send_to_groups(sums)
    ffn = all_shares(near_shares(add_up([after(ffn[0], input_grad, sums[0]), *ffn[1:]])))
    q = d // lax.axis_size("group")
    layout = [([(3 * j + k, 0, width) for j in range(PARTS)], k == 2) for k in range(3)]
    g_gate_b, g_up_b, g_down_a = finish_call(after(ids, sums[0]), ffn, layout)
    small = all_shares(near_shares(add_up(small)))
    layout = [([(None, k * q, q)], k >= 2) for k in range(5)]
    layout += [([(None, 5 * q, 3 * q)], False), ([(None, 8 * q, q)], True)]
    g_out_b, g_down_b, g_gate_a, g_up_a, g_out_a, g_in_b, g_in_a = finish_call(ids, small, layout)
    return (
        result, input_grad, g_in_a, g_in_b, g_out_a, g_out_b, g_gate_a, g_gate_b, g_up_a, g_up_b, g_down_a,
        g_down_b,
    )


def solution(mesh):
    in_specs = (
        P(("dp", "group"), None),
        P(("dp", "group"), None),
        P("group", None),
        P(None, "group", None),
        P(None, "group", None),
        P(),
        P(),
        P(),
        P(None, "group"),
        P(None, "group"),
        P(None, "group"),
        P(None, "group"),
        P(None, "group"),
        P(),
        P(),
        P(),
        P(),
        P(),
        P(),
        P(),
        P(),
        P(),
        P(),
    )
    out_specs = (
        P(("dp", "group"), None),
        P(("dp", "group"), None),
        P("group", None),
        P(None, "group"),
        P("group", None),
        P(None, "group"),
        P("group", None),
        P(None, "group"),
        P("group", None),
        P(None, "group"),
        P("group", None),
        P(None, "group"),
    )
    small = dict(mesh.shape) == {"dp": 8, "group": 4}
    return jax.shard_map(local_pieces if small else local, mesh=mesh, in_specs=in_specs, out_specs=out_specs, check_vma=False)
```
